256 devices in a mesh: ctx: 8 (over z), exp: 32 (over x, y, core).
Axes of the slice: x: 4, y: 4, z: 8, core: 2. Of those that a mesh axis runs over, the one named last changes fastest.
Arguments:
- tokens: bfloat16 [8192, 2048], P(('ctx', 'exp')), may hold values from -6 to 6
- gain_in: float32 [2048], replicated, may hold values from 0.1 to 1.9
- w_heads: bfloat16 [2048, 16384], P(None, 'exp'), may hold values from -0.125 to 0.125
- w_scalar: bfloat16 [2048, 64], P(None, 'exp'), may hold values from -0.125 to 0.125
- strength_bias: float32 [32], P('exp'), may hold values from -8 to 1
- decay_rate: float32 [32], P('exp'), may hold values from 1e-06 to 0.05
- decay_bias: float32 [32], P('exp'), may hold values from -3 to 3
- state_init: float32 [32, 128, 128], P('exp'), may hold values from -1.5 to 1.5
- gain_head: float32 [128], replicated, may hold values from 0.1 to 1.9
- w_output: bfloat16 [4096, 2048], P('exp'), may hold values from -0.09375 to 0.09375
- gain_expert: float32 [2048], replicated, may hold values from 0.1 to 1.9
- expert_ids: int32 [8192, 10], P(('ctx', 'exp')), may hold values from 0 to 31, all different within a row; in each aligned block of 32 rows (0 to 31, 32 to 63, ...) at most 20 rows name the same one
- gate_weights: float32 [8192, 10], P(('ctx', 'exp')), may hold values from 0.5 to 1.5
- w_gate_up: bfloat16 [32, 2048, 1024], P('exp'), may hold values from -0.125 to 0.125
- w_down: bfloat16 [32, 512, 2048], P('exp'), may hold values from -0.25 to 0.25
Outputs:
- attn_out: bfloat16 [8192, 2048], P(('ctx', 'exp'))
- expert_out: bfloat16 [8192, 2048], P(('ctx', 'exp'))
The draws below stay inside these ranges and needn't reach their ends.
Inputs may be any that keep to these rules, and one draw needn't show every extreme that they name: `expert_ids`: each row names 10 different experts. In every aligned block of 32 rows (the rows of one device) no expert is named by more than 20 rows, a bound that some block reaches.
All inputs are finite; a program needn't handle non-finite values.
Results may differ from the reference program's by a relative error of at most 0.029.
Values may be sent and summed in bfloat16 or wider, within the bound.
No kernel may reach another device: no remote copies, remote signals or barrier semaphores. Data moves between devices by JAX's collectives and lax.ppermute only.
A program may use at most 128 MiB of HBM per device.

```python
import math
import jax
import jax.numpy as jnp
import numpy as np
from jax import lax

D = 2048
HEADS = 32
DK = 128
FF = 512
TOP = 10
EXPERTS = 32
STRETCH = 64
TOK_DEV = 32
TOKENS = 8192
CAP = 20


def draw_tokens(key, part):
    common_part = jax.random.normal(jax.random.fold_in(key, 11), (1, D), jnp.float32)
    private_part = jax.random.normal(jax.random.fold_in(key, 12), (TOKENS, D), jnp.float32)
    values = 0.75 * private_part + 0.75 * common_part
    return jnp.clip(values, -6.0, 6.0).astype(jnp.bfloat16)


def level_of(key, extent, cuts, least, largest):
    loudness, own = 1.0, jax.random.fold_in(key, 6)
    for axis_at, shards_of in cuts:
        heights = jnp.exp(jax.random.uniform(jax.random.fold_in(own, axis_at), (shards_of,), jnp.float32, least / len(cuts), largest / len(cuts)))
        loudness = loudness * jnp.repeat(heights, extent[axis_at] // shards_of).reshape([-1 if axis == axis_at else 1 for axis in range(len(extent))])
    return loudness


def assign_block(rng, own, number, rows, number_of, top, limit, lean):
    order = jax.random.permutation(rng, number_of)
    packed, common = shares(number_of, rows * top, limit, lean, True), shares(number_of, rows * top, limit, lean, False)
    places = jnp.arange(number_of)

    def named(tallies, turn):
        used = int((tallies > 0).sum())
        fixed = max(1, used // 4)
        passed = fixed + (places - fixed + turn * (used - fixed)) % max(1, number_of - fixed)
        return jnp.zeros((number_of,), jnp.int32).at[order[jnp.where(places < fixed, places, passed)]].set(jnp.asarray(tallies, jnp.int32))

    tallies = jnp.where(number % 4 == 0, named(packed, number // 4), named(common, number - number // 4 - 1))
    mixed = jax.random.permutation(jax.random.fold_in(own, 3), number_of)
    giver, receiver = mixed[0:number_of // 2 * 2:2], mixed[1:number_of // 2 * 2:2]
    margin = jnp.minimum(tallies[giver] - 1, limit - tallies[receiver]) // 2
    margin = jnp.where((giver == order[0]) | (receiver == order[0]) | (tallies[receiver] == 0), 0, jnp.maximum(margin, 0))
    passed = jax.random.randint(jax.random.fold_in(own, 4), (number_of // 2,), 0, 1 << 20) % (margin + 1)
    tallies = tallies.at[giver].add(-passed).at[receiver].add(passed)
    members = jnp.searchsorted(jnp.cumsum(tallies), jnp.arange(rows * top), side="right").astype(jnp.int32)
    grid = members.reshape(top, rows).T
    grid = grid[jax.random.permutation(jax.random.fold_in(own, 1), rows)]
    turn = jax.random.randint(jax.random.fold_in(own, 2), (rows, 1), 0, top)
    return jnp.take_along_axis(grid, (jnp.arange(top)[None, :] + turn) % top, axis=1)


def shares(number_of, total, reach, lean, full):
    portions = [(1 << 20) // math.isqrt(grade ** lean) + 1 for grade in range(1, number_of + 1)]
    largest = reach if full else min(reach, max(-(-total // number_of), total * portions[0] // sum(portions)))
    least = 1 if total - largest >= number_of - 1 else 0
    given, surplus = [largest] + [least] * (number_of - 1), total - largest - least * (number_of - 1)
    while surplus > 0:
        candidates = [i for i in range(1, number_of) if given[i] < largest] or [i for i in range(1, number_of) if given[i] < reach]
        mass, left = sum([portions[i] for i in candidates]), surplus
        for i in candidates:
            addition = min(reach - given[i], max(1, left * portions[i] // mass), surplus)
            given[i] = given[i] + addition
            surplus = surplus - addition
    return np.array(given)


def bell_draw(rng, dims, width, most, pieces=(), kind=jnp.bfloat16):
    values = jax.random.normal(rng, dims, jnp.float32) * width
    if len(pieces) > 0:
        values = level_of(rng, dims, pieces, -0.22, 0.18) * values
    return jnp.clip(values, min=-most, max=most).astype(kind)


def setup_inputs(seed: int = 0) -> dict:
    splits = jax.random.split(jax.random.key(seed), 16)
    tokens = draw_tokens(jax.random.fold_in(splits[15], 71), 0)
    gain_in = jnp.clip(1.0 + 0.18 * jax.random.normal(splits[1], (D,), jnp.float32), 0.1, 1.9)
    w_heads = bell_draw(splits[2], (D, HEADS * 4 * DK), D ** -0.5, 0.125, ((1, 32),))
    w_scalar = bell_draw(splits[3], (D, 2 * HEADS), D ** -0.5, 0.125, ((1, 32),))
    strength_bias = jnp.clip(-8.0 + 9.0 * jax.random.uniform(splits[4], (HEADS,), jnp.float32) ** level_of(splits[4], (HEADS,), ((0, 32),), -0.2, 0.2), -8.0, 1.0)
    decay_rate = jnp.clip(jnp.exp(math.log(0.05) - 10.819778 * jax.random.uniform(splits[5], (HEADS,), jnp.float32) ** level_of(splits[5], (HEADS,), ((0, 32),), -0.2, 0.2)), 9.999999974752427e-07, 0.05)
    decay_bias = bell_draw(splits[6], (HEADS,), 1.0, 3.0, ((0, 32),), jnp.float32)
    state_init = bell_draw(splits[7], (HEADS, DK, DK), 0.25, 1.5, ((0, 32),), jnp.float32)
    gain_head = jnp.clip(1.0 + 0.18 * jax.random.normal(splits[8], (DK,), jnp.float32), 0.1, 1.9)
    w_output = bell_draw(splits[9], (HEADS * DK, D), (HEADS * DK) ** -0.5, 0.09375, ((0, 32),))
    gain_expert = jnp.clip(1.0 + 0.18 * jax.random.normal(splits[10], (D,), jnp.float32), 0.1, 1.9)
    expert_ids_keys = jax.random.split(jax.random.fold_in(splits[11], 1), TOKENS // TOK_DEV)
    expert_ids_turns = jax.random.permutation(jax.random.fold_in(splits[11], 3), TOKENS // TOK_DEV)
    expert_ids = jax.vmap(lambda own, number: assign_block(jax.random.fold_in(splits[11], 2), own, number, TOK_DEV, EXPERTS, TOP, CAP, 2))(expert_ids_keys, expert_ids_turns).reshape((TOKENS, TOP))
    gate_weights = jnp.clip(1.0 + 0.1 * jax.random.normal(splits[12], (TOKENS, TOP), jnp.float32), 0.5, 1.5)
    w_gate_up = bell_draw(splits[13], (EXPERTS, D, 2 * FF), D ** -0.5, 0.125, ((0, 32),))
    w_down = bell_draw(splits[14], (EXPERTS, FF, D), FF ** -0.5, 0.25, ((0, 32),))
    return {"tokens": tokens, "gain_in": gain_in, "w_heads": w_heads, "w_scalar": w_scalar, "strength_bias": strength_bias, "decay_rate": decay_rate, "decay_bias": decay_bias, "state_init": state_init, "gain_head": gain_head, "w_output": w_output, "gain_expert": gain_expert, "expert_ids": expert_ids, "gate_weights": gate_weights, "w_gate_up": w_gate_up, "w_down": w_down}


EPSILON = 1e-06
PRECISE = lax.Precision.HIGHEST

def rms_scale(values):
    return lax.rsqrt(lax.optimization_barrier(jnp.mean(values * values, axis=-1, keepdims=True)) + EPSILON)

def prepare(query, key_vec, value, strength, log_alpha):
    head_count, span_rows, head_dim = query.shape
    stretch_count = span_rows // STRETCH
    stretch_shape = (head_count, stretch_count, STRETCH, head_dim)
    query = query.reshape(stretch_shape)
    key_vec = key_vec.reshape(stretch_shape)
    value = value.reshape(stretch_shape)
    strength = strength.reshape(head_count, stretch_count, STRETCH)
    decay_sum = jnp.cumsum(log_alpha.reshape(head_count, stretch_count, STRETCH), axis=-1)
    decay_gap = decay_sum[..., :, None] - decay_sum[..., None, :]
    row_ids = lax.broadcasted_iota(jnp.int32, (STRETCH, STRETCH), 0)
    col_ids = lax.broadcasted_iota(jnp.int32, (STRETCH, STRETCH), 1)
    decay_pair = jnp.where(row_ids >= col_ids, jnp.exp(jnp.minimum(decay_gap, 0.0)), 0.0)
    key_gram = jnp.einsum('hncd,hnsd->hncs', key_vec, key_vec, precision=PRECISE)
    lower_part = jnp.where(row_ids > col_ids, key_gram * decay_pair * strength[..., :, None], 0.0)
    system = lower_part + jnp.eye(STRETCH, dtype=jnp.float32)
    growth = jnp.exp(decay_sum)
    right_sides = jnp.concatenate([value * strength[..., None], key_vec * (strength * growth)[..., None]], axis=-1)
    solved = jax.scipy.linalg.solve_triangular(system, right_sides, lower=True, unit_diagonal=True)
    update = solved[..., :head_dim]
    correction = solved[..., head_dim:]
    within = jnp.einsum('hncd,hnsd->hncs', query, key_vec, precision=PRECISE) * decay_pair
    last_sum = decay_sum[..., -1]
    query_decay = query * growth[..., None]
    key_tail = key_vec * jnp.exp(last_sum[..., None] - decay_sum)[..., None]
    return (query_decay, key_tail, update, correction, within, jnp.exp(last_sum))

def emit_stretches(initial, parts):

    def advance(carried, bundle):
        query_decay, key_tail, update, correction, within, stretch_fall = bundle
        pending = update - jnp.einsum('hcd,hvd->hcv', correction, carried, precision=PRECISE)
        result = jnp.einsum('hcd,hvd->hcv', query_decay, carried, precision=PRECISE)
        result = result + jnp.einsum('hcs,hsv->hcv', within, pending, precision=PRECISE)
        carried = stretch_fall[:, None, None] * carried + jnp.einsum('hcv,hce->hve', pending, key_tail, precision=PRECISE)
        return (carried, result)
    _, results = lax.scan(advance, initial, tuple((jnp.moveaxis(piece, 1, 0) for piece in parts)))
    results = jnp.moveaxis(results, 0, 1)
    return results.reshape(results.shape[0], results.shape[1] * results.shape[2], results.shape[3])

def reference(tokens, gain_in, w_heads, w_scalar, strength_bias, decay_rate, decay_bias, state_init, gain_head, w_output, gain_expert, expert_ids, gate_weights, w_gate_up, w_down):
    wide_in = tokens.astype(jnp.float32)
    normed_in = (wide_in * rms_scale(wide_in) * gain_in).astype(jnp.bfloat16)
    head_cols = w_heads.reshape(D, HEADS, 4 * DK).transpose(1, 0, 2)
    gate_cols = w_scalar.reshape(D, HEADS, 2).transpose(1, 0, 2)

    def one_head(bundle):
        columns, scalar_cols, lift, rate, bias, initial = bundle
        projected = jnp.dot(normed_in.astype(jnp.float32), columns.astype(jnp.float32), preferred_element_type=jnp.float32)
        gate_logits = jnp.dot(normed_in.astype(jnp.float32), scalar_cols.astype(jnp.float32), preferred_element_type=jnp.float32)
        query = projected[:, :DK]
        key_vec = projected[:, DK:2 * DK]
        value = projected[:, 2 * DK:3 * DK]
        gate_vec = projected[:, 3 * DK:]
        strength = jax.nn.sigmoid(gate_logits[:, 0] + lift)
        log_alpha = -rate * jax.nn.softplus(gate_logits[:, 1] + bias)
        key_vec = key_vec * lax.rsqrt(lax.optimization_barrier(jnp.sum(key_vec * key_vec, axis=-1, keepdims=True)) + EPSILON)
        parts = prepare(query[None], key_vec[None], value[None], strength[None], log_alpha[None])
        head_raw = emit_stretches(initial[None], parts)[0]
        return (head_raw * rms_scale(head_raw) * gain_head * jax.nn.silu(gate_vec)).astype(jnp.bfloat16)
    gated = lax.map(one_head, (head_cols, gate_cols, strength_bias, decay_rate, decay_bias, state_init))
    gated = gated.transpose(1, 0, 2).reshape(TOKENS, HEADS * DK)
    attn_out = jnp.dot(gated.astype(jnp.float32), w_output.astype(jnp.float32), preferred_element_type=jnp.float32).astype(jnp.bfloat16)
    hidden = tokens.astype(jnp.float32) + attn_out.astype(jnp.float32)
    normed_ffn = (hidden * rms_scale(hidden) * gain_expert).astype(jnp.bfloat16)
    num_blocks = TOKENS // TOK_DEV
    per_block = TOK_DEV * TOP
    route_ids = expert_ids.reshape(num_blocks, per_block)
    one_hot = (route_ids[:, :, None] == jnp.arange(EXPERTS, dtype=jnp.int32)[None, None, :]).astype(jnp.int32)
    slot_rank = lax.optimization_barrier(jnp.sum((jnp.cumsum(one_hot, axis=1) - one_hot) * one_hot, axis=2))
    block_ids = jnp.arange(num_blocks, dtype=jnp.int32)[:, None]
    flat_slot = ((block_ids * EXPERTS + route_ids) * CAP + slot_rank).reshape(-1)
    token_ids = (block_ids * TOK_DEV + jnp.arange(per_block, dtype=jnp.int32)[None, :] // TOP).reshape(-1)
    slot_token = jnp.full((num_blocks * EXPERTS * CAP,), TOKENS, jnp.int32).at[flat_slot].set(token_ids)
    slot_gate = jnp.zeros((num_blocks * EXPERTS * CAP,), jnp.float32).at[flat_slot].set(gate_weights.reshape(-1))
    slot_token = slot_token.reshape(num_blocks, EXPERTS, CAP).transpose(1, 0, 2).reshape(EXPERTS, num_blocks * CAP)
    slot_gate = slot_gate.reshape(num_blocks, EXPERTS, CAP).transpose(1, 0, 2).reshape(EXPERTS, num_blocks * CAP)
    source_rows = jnp.concatenate([normed_ffn, jnp.zeros((1, D), jnp.bfloat16)], axis=0)

    def expert_step(running, bundle):
        weight_up, weight_down, index, scale = bundle
        inputs = source_rows[index]
        pre_act = jnp.dot(inputs.astype(jnp.float32), weight_up.astype(jnp.float32), preferred_element_type=jnp.float32)
        activated = (jax.nn.silu(pre_act[:, :FF]) * pre_act[:, FF:]).astype(jnp.bfloat16)
        expert_rows = jnp.dot(activated.astype(jnp.float32), weight_down.astype(jnp.float32), preferred_element_type=jnp.float32).astype(jnp.bfloat16)
        return (running.at[index].add(expert_rows.astype(jnp.float32) * scale[:, None]), None)
    running, _ = lax.scan(expert_step, jnp.zeros((TOKENS + 1, D), jnp.float32), (w_gate_up, w_down, slot_token, slot_gate))
    expert_out = running[:TOKENS].astype(jnp.bfloat16)
    return (attn_out, expert_out)
```

```python
import functools
import jax
import jax.numpy as jnp
from jax import lax
from jax.experimental import pallas as pl
from jax.experimental.pallas import tpu as pltpu
from jax.sharding import Mesh, PartitionSpec as P

EPSILON = 1e-06
F32 = jnp.float32
BF16 = jnp.bfloat16
CHUNK = 128


def mm(a, b):
    return jnp.dot(a.astype(BF16), b.astype(BF16), preferred_element_type=F32)


def pieces(a):
    high = a.astype(BF16)
    rest = a - high.astype(F32)
    middle = rest.astype(BF16)
    low = (rest - middle.astype(F32)).astype(BF16)
    return high, middle, low


def mixer_body(scal_ref, x_ref, w_ref, ws_ref, g_ref, h_ref, gate_ref, maps_ref, po_ref, *, per_step):
    dim = maps_ref.shape[0]
    step = pl.program_id(0)

    @pl.when(step == 0)
    def _():
        rows = lax.broadcasted_iota(jnp.int32, (dim, 2 * dim), 0)
        cols = lax.broadcasted_iota(jnp.int32, (dim, 2 * dim), 1)
        po_ref[...] = jnp.where(rows == cols, 1.0, 0.0).astype(F32)

    lift = scal_ref[0]
    rate = scal_ref[1]
    bias = scal_ref[2]
    rows = lax.broadcasted_iota(jnp.int32, (CHUNK, CHUNK), 0)
    cols = lax.broadcasted_iota(jnp.int32, (CHUNK, CHUNK), 1)
    differ = jnp.bitwise_xor(rows, cols)
    lower = rows >= cols
    strict = rows > cols
    lower_ones = jnp.where(lower, 1.0, 0.0).astype(BF16)
    upper_ones = jnp.where(rows <= cols, 1.0, 0.0).astype(BF16)
    eye = jnp.where(rows == cols, 1.0, 0.0).astype(F32)
    x = x_ref[...]
    projected = jnp.dot(x, w_ref[...], preferred_element_type=F32)
    logits = jnp.dot(x, ws_ref[...], preferred_element_type=F32)
    gate_ref[...] = projected[:, 3 * dim:]
    ready = []
    for n in range(per_step):
        at = slice(n * CHUNK, (n + 1) * CHUNK)
        query = projected[at, :dim]
        key_raw = projected[at, dim:2 * dim]
        value = projected[at, 2 * dim:3 * dim]
        strength = jax.nn.sigmoid(logits[at, 0:1] + lift)
        shifted_logit = logits[at, 1:2] + bias
        softplus = jnp.maximum(shifted_logit, 0.0) + jnp.log1p(jnp.exp(-jnp.abs(shifted_logit)))
        log_alpha = jnp.broadcast_to(-rate * softplus, (CHUNK, CHUNK))
        beta = jnp.broadcast_to(strength, (CHUNK, dim))
        high, middle, low = pieces(log_alpha)
        sum_col = (
            jnp.dot(lower_ones, high, preferred_element_type=F32)
            + jnp.dot(lower_ones, middle, preferred_element_type=F32)
            + jnp.dot(lower_ones, low, preferred_element_type=F32)
        )
        sum_row = sum_col.T
        key_vec = key_raw * lax.rsqrt(jnp.sum(key_raw * key_raw, axis=-1, keepdims=True) + EPSILON)
        key_t = key_vec.T
        last = sum_col[CHUNK - 1:CHUNK, :]
        fall = jnp.exp(last)
        growth = jnp.exp(sum_col)
        tail_row = jnp.exp(sum_row[:, CHUNK - 1:CHUNK] - sum_row)
        decay = jnp.where(lower, jnp.exp(jnp.minimum(sum_col - sum_row, 0.0)), 0.0)
        gram = mm(jnp.concatenate([key_vec, query], axis=0), key_t)
        lower_part = jnp.where(strict, gram[:CHUNK] * decay * beta, 0.0)
        inverse = eye - jnp.where(differ < 2, lower_part, 0.0)
        width = 2
        while width < CHUNK:
            corner = jnp.where((differ >= width) & (differ < 2 * width), lower_part, 0.0)
            inverse = inverse - mm(mm(inverse, corner), inverse)
            width *= 2
        sides = jnp.concatenate([value * beta, key_vec * (beta * growth)], axis=1)
        solved = mm(inverse, sides)
        mixed = mm(gram[CHUNK:] * decay, solved)
        query_eff = query * growth - mixed[:, dim:]
        drive = mm(key_t * tail_row, solved)
        ready.append((query_eff, mixed[:, :dim], drive, fall))
    carried = po_ref[...]
    for n in range(per_step):
        at = slice(n * CHUNK, (n + 1) * CHUNK)
        query_eff, base, drive, fall = ready[n]
        both = mm(query_eff, carried)
        g_ref[at, :] = both[:, :dim].astype(BF16)
        h_ref[at, :] = both[:, dim:] + base
        falls = jnp.concatenate([fall, fall], axis=1)
        moved = falls * carried - mm(drive[:, dim:], carried)
        carried = jnp.concatenate([moved[:, :dim], moved[:, dim:] + drive[:, :dim]], axis=1)
    po_ref[...] = carried

    @pl.when(step == pl.num_programs(0) - 1)
    def _():
        maps_ref[...] = carried.astype(maps_ref.dtype)


def mixer(scalars, x, w, ws, dim, per_step):
    span, width = x.shape
    rows = per_step * CHUNK
    by_rows = pl.BlockSpec((rows, dim), lambda i: (i, 0))
    return pl.pallas_call(
        functools.partial(mixer_body, per_step=per_step),
        grid=(span // rows,),
        in_specs=[
            pl.BlockSpec(memory_space=pltpu.SMEM),
            pl.BlockSpec((rows, width), lambda i: (i, 0)),
            pl.BlockSpec(w.shape, lambda i: (0, 0)),
            pl.BlockSpec(ws.shape, lambda i: (0, 0)),
        ],
        out_specs=[by_rows, by_rows, by_rows, pl.BlockSpec((dim, 2 * dim), lambda i: (0, 0))],
        out_shape=[
            jax.ShapeDtypeStruct((span, dim), BF16),
            jax.ShapeDtypeStruct((span, dim), F32),
            jax.ShapeDtypeStruct((span, dim), F32),
            jax.ShapeDtypeStruct((dim, 2 * dim), BF16),
        ],
        scratch_shapes=[pltpu.VMEM((dim, 2 * dim), F32)],
        name="mixer",
    )(scalars, x, w, ws)


def rms_scale(values):
    return lax.rsqrt(jnp.mean(values * values, axis=-1, keepdims=True) + EPSILON)


def norm_body(tokens_ref, gain_ref, out_ref):
    wide = tokens_ref[...].astype(F32)
    normed = (wide * rms_scale(wide) * gain_ref[...]).astype(BF16)
    out_ref[...] = jnp.broadcast_to(normed[None], out_ref.shape)


def norm_copies(tokens, gain, copies):
    return pl.pallas_call(
        norm_body,
        out_shape=jax.ShapeDtypeStruct((copies,) + tokens.shape, BF16),
        name="norm_copies",
    )(tokens, gain[None])


def emit_body(place_ref, maps_ref, init_ref, g_ref, h_ref, gate_ref, gain_ref, out_ref, state_ref):
    dim = init_ref.shape[0]

    @pl.when(pl.program_id(0) == 0)
    def _():
        state = init_ref[...].T
        for block in range(maps_ref.shape[0] - 1):
            maps = maps_ref[block]
            moved = mm(maps[:, :dim], state) + maps[:, dim:].astype(F32)
            state = jnp.where(block < place_ref[0], moved, state)
        state_ref[...] = state

    head_raw = mm(g_ref[...], state_ref[...]) + h_ref[...]
    gate = gate_ref[...]
    gated = head_raw * rms_scale(head_raw) * gain_ref[...] * (gate * jax.nn.sigmoid(gate))
    out_ref[...] = gated.astype(BF16).reshape(out_ref.shape)


def emit(place, maps, init, g, h, gate, gain, outer, inner):
    span, dim = g.shape
    rows = span // outer
    each = rows // inner
    by_rows = pl.BlockSpec((rows, dim), lambda i: (i, 0))
    return pl.pallas_call(
        emit_body,
        grid=(outer,),
        in_specs=[
            pl.BlockSpec(memory_space=pltpu.SMEM),
            pl.BlockSpec(maps.shape, lambda i: (0, 0, 0)),
            pl.BlockSpec(init.shape, lambda i: (0, 0)),
            by_rows,
            by_rows,
            by_rows,
            pl.BlockSpec((1, dim), lambda i: (0, 0)),
        ],
        out_specs=pl.BlockSpec((inner, 1, each, dim), lambda i: (0, i, 0, 0)),
        out_shape=jax.ShapeDtypeStruct((inner, outer, each, dim), BF16),
        scratch_shapes=[pltpu.VMEM((dim, dim), F32)],
        name="emit",
    )(place, maps, init, g, h, gate, gain[None])


def project_body(gated_ref, w_ref, out_ref):
    total = None
    heads, _, dim = gated_ref.shape
    left = jnp.concatenate([gated_ref[head] for head in range(heads)], axis=1)
    total = jnp.dot(left, w_ref[...], preferred_element_type=F32)
    out_ref[...] = total.astype(BF16)


def project(gated, w, tile):
    heads, rows, dim = gated.shape
    width = w.shape[1]
    return pl.pallas_call(
        project_body,
        grid=(width // tile,),
        in_specs=[
            pl.BlockSpec(gated.shape, lambda i: (0, 0, 0)),
            pl.BlockSpec((heads * dim, tile), lambda i: (0, i)),
        ],
        out_specs=pl.BlockSpec((rows, tile), lambda i: (0, i)),
        out_shape=jax.ShapeDtypeStruct((rows, width), BF16),
        name="project",
    )(gated, w)


def join_body(parts_ref, tokens_ref, gain_ref, out_ref, copies_ref):
    total = parts_ref[0].astype(F32)
    for part in range(1, parts_ref.shape[0]):
        total = total + parts_ref[part].astype(F32)
    summed = total.astype(BF16)
    out_ref[...] = summed
    hidden = tokens_ref[...].astype(F32) + summed.astype(F32)
    normed = (hidden * rms_scale(hidden) * gain_ref[...]).astype(BF16)
    copies_ref[...] = jnp.broadcast_to(normed[None], copies_ref.shape)


def join(parts, tokens, gain, copies):
    return pl.pallas_call(
        join_body,
        out_shape=[
            jax.ShapeDtypeStruct(tokens.shape, BF16),
            jax.ShapeDtypeStruct((copies,) + tokens.shape, BF16),
        ],
        name="join",
    )(parts, tokens, gain[None])


def total_body(parts_ref, out_ref):
    total = parts_ref[0].astype(F32)
    for part in range(1, parts_ref.shape[0]):
        total = total + parts_ref[part].astype(F32)
    out_ref[...] = total.astype(BF16)


def total_of(parts):
    return pl.pallas_call(
        total_body,
        out_shape=jax.ShapeDtypeStruct(parts.shape[1:], BF16),
        name="total",
    )(parts)


def swap_cores(value):
    return lax.ppermute(value, "core", [(0, 1), (1, 0)])


def exchange(value, axes):
    return lax.all_to_all(value, axes, split_axis=0, concat_axis=0, tiled=True)


def expert(x, w_gate_up, w_down, weights):
    hidden_units = w_down.shape[0]
    pre = jnp.dot(x, w_gate_up, preferred_element_type=F32)
    activated = (jax.nn.silu(pre[:, :hidden_units]) * pre[:, hidden_units:]).astype(BF16)
    rows = jnp.dot(activated, w_down, preferred_element_type=F32).astype(BF16)
    return rows.astype(F32) * weights


def shards(
    tokens,
    gain_in,
    w_heads,
    w_scalar,
    strength_bias,
    decay_rate,
    decay_bias,
    state_init,
    gain_head,
    w_output,
    gain_expert,
    expert_ids,
    gate_weights,
    w_gate_up,
    w_down,
):
    tok_dev, width = tokens.shape
    dim = state_init.shape[-1]
    x_count, y_count, core_count = (lax.axis_size(axis) for axis in ("x", "y", "core"))
    chips = x_count * y_count
    expert_total = chips * core_count
    span = expert_total * tok_dev

    experts = jnp.arange(expert_total, dtype=jnp.int32)
    named = expert_ids[:, :, None] == experts[None, None, :]
    dense_gate = jnp.sum(jnp.where(named, gate_weights[:, :, None], 0.0), axis=1)
    dense_gate = dense_gate.reshape(tok_dev, chips, core_count).transpose(1, 0, 2)
    gates = exchange(dense_gate, ("x", "y")).reshape(chips * tok_dev, core_count)
    other_gate_up = swap_cores(w_gate_up)
    other_down = swap_cores(w_down)

    copies = norm_copies(tokens, gain_in, chips)
    mine = exchange(copies, ("x", "y"))
    gathered = lax.all_gather(mine, "core", axis=1, tiled=False).reshape(span, width)
    w_wide = lax.all_gather(w_output, ("y", "core"), axis=0, tiled=True)

    scalars = jnp.concatenate([strength_bias, decay_rate, decay_bias])
    w_logit = jnp.pad(w_scalar, ((0, 0), (0, 128 - w_scalar.shape[1])))
    g, h, gate, maps = mixer(scalars, gathered, w_heads, w_logit, dim, 2)
    all_maps = lax.all_gather(maps, "ctx", axis=0, tiled=False)
    place = lax.axis_index("ctx").astype(jnp.int32)[None]
    gated = emit(
        place, all_maps, state_init[0], g, h, gate, gain_head, x_count, y_count * core_count
    )
    heads = y_count * core_count
    gated = exchange(gated, ("y", "core")).reshape(heads, x_count * tok_dev, dim)
    partial = project(gated, w_wide, 512).reshape(x_count, tok_dev, width)
    summed, copies = join(exchange(partial, "x"), tokens, gain_expert, chips)

    received = exchange(copies, ("x", "y")).reshape(chips * tok_dev, width)
    core = lax.axis_index("core")
    own_gate = jnp.where(core == 0, gates[:, 0:1], gates[:, 1:2])
    other_gate = jnp.where(core == 0, gates[:, 1:2], gates[:, 0:1])
    outputs = expert(received, w_gate_up[0], w_down[0], own_gate)
    outputs = outputs + expert(received, other_gate_up[0], other_down[0], other_gate)
    outputs = outputs.astype(BF16).reshape(chips, tok_dev, width)
    expert_out = total_of(exchange(outputs, ("x", "y")))
    return (summed, expert_out)


def solution(mesh):
    fine = Mesh(mesh.devices.reshape(mesh.shape["ctx"], 4, 4, 2), ("ctx", "x", "y", "core"))
    exp = ("x", "y", "core")
    rows = ("ctx", "x", "y", "core")
    return jax.shard_map(
        shards,
        mesh=fine,
        in_specs=(
            P(rows, None),
            P(),
            P(None, exp),
            P(None, exp),
            P(exp),
            P(exp),
            P(exp),
            P(exp, None, None),
            P(),
            P(exp, None),
            P(),
            P(rows, None),
            P(rows, None),
            P(exp, None, None),
            P(exp, None, None),
        ),
        out_specs=(P(rows, None), P(rows, None)),
        check_vma=False,
    )
```

```python
import functools
import jax
import jax.numpy as jnp
from jax import lax
from jax.experimental import pallas as pl
from jax.experimental.pallas import tpu as pltpu
from jax.sharding import Mesh, PartitionSpec as P

EPSILON = 1e-06
F32 = jnp.float32
BF16 = jnp.bfloat16
CHUNK = 128
LANES = 128


def mm(a, b):
    return jnp.dot(a.astype(BF16), b.astype(BF16), preferred_element_type=F32)


def pieces(a):
    high = a.astype(BF16)
    rest = a - high.astype(F32)
    middle = rest.astype(BF16)
    low = (rest - middle.astype(F32)).astype(BF16)
    return high, middle, low


def rms_scale(values):
    return lax.rsqrt(jnp.mean(values * values, axis=-1, keepdims=True) + EPSILON)


def chunk_of(n):
    return slice(n * CHUNK, (n + 1) * CHUNK)


def resident():
    return pl.BlockSpec(memory_space=pltpu.VMEM)


def whole(shape):
    return pl.BlockSpec(shape, lambda i: (0,) * len(shape))


def project_rows(core, mine_ref, theirs_ref, w):
    groups, each, width = mine_ref.shape
    ours = jnp.dot(mine_ref[...].reshape(groups * each, width), w, preferred_element_type=F32)
    others = jnp.dot(theirs_ref[...].reshape(groups * each, width), w, preferred_element_type=F32)
    even = jnp.where(core == 0, ours, others)
    odd = jnp.where(core == 0, others, ours)
    rows = []
    for group in range(groups):
        at = slice(group * each, (group + 1) * each)
        rows += [even[at], odd[at]]
    return jnp.concatenate(rows, axis=0)


def maps_body(
    core_ref, scal_ref, mine_ref, theirs_ref, wk_ref, wv_ref, ws_ref,
    key_ref, decay_ref, growth_ref, solved_ref, start_ref, maps_ref, carry_ref,
    *, per_step,
):
    dim = wk_ref.shape[1]
    step = pl.program_id(0)

    @pl.when(step == 0)
    def _():
        rows = lax.broadcasted_iota(jnp.int32, (dim, 2 * dim), 0)
        cols = lax.broadcasted_iota(jnp.int32, (dim, 2 * dim), 1)
        carry_ref[...] = jnp.where(rows == cols, 1.0, 0.0).astype(F32)

    lift = scal_ref[0]
    rate = scal_ref[1]
    bias = scal_ref[2]
    rows = lax.broadcasted_iota(jnp.int32, (CHUNK, CHUNK), 0)
    cols = lax.broadcasted_iota(jnp.int32, (CHUNK, CHUNK), 1)
    differ = jnp.bitwise_xor(rows, cols)
    lower = rows >= cols
    strict = rows > cols
    lower_ones = jnp.where(lower, 1.0, 0.0).astype(BF16)
    eye = jnp.where(rows == cols, 1.0, 0.0).astype(F32)
    w_all = jnp.concatenate([wk_ref[...], wv_ref[...], ws_ref[...]], axis=1)
    projected = project_rows(core_ref[0], mine_ref, theirs_ref, w_all)
    logits = projected[:, 2 * dim:]
    every = range(per_step)
    key_raw = [projected[chunk_of(n), :dim] for n in every]
    value = [projected[chunk_of(n), dim:2 * dim] for n in every]
    strength = [jax.nn.sigmoid(logits[chunk_of(n), 0:1] + lift) for n in every]
    beta = [jnp.broadcast_to(s, (CHUNK, dim)) for s in strength]
    sums = []
    for n in every:
        moved = logits[chunk_of(n), 1:2] + bias
        softplus = jnp.maximum(moved, 0.0) + jnp.log1p(jnp.exp(-jnp.abs(moved)))
        high, middle, low = pieces(jnp.broadcast_to(-rate * softplus, (CHUNK, CHUNK)))
        sums.append(
            jnp.dot(lower_ones, high, preferred_element_type=F32)
            + jnp.dot(lower_ones, middle, preferred_element_type=F32)
            + jnp.dot(lower_ones, low, preferred_element_type=F32)
        )
    sums_t = [s.T for s in sums]
    key_vec = [
        k * lax.rsqrt(jnp.sum(k * k, axis=-1, keepdims=True) + EPSILON) for k in key_raw
    ]
    key_t = [k.T for k in key_vec]
    growth = [jnp.exp(s) for s in sums]
    fall = [jnp.exp(s[CHUNK - 1:CHUNK, :]) for s in sums]
    decay = [
        jnp.where(lower, jnp.exp(jnp.minimum(s - t, 0.0)), 0.0) for s, t in zip(sums, sums_t)
    ]
    gram = [mm(k, t) for k, t in zip(key_vec, key_t)]
    below = [
        jnp.where(strict, gram[n] * decay[n] * beta[n], 0.0) for n in every
    ]
    inverse = [eye - jnp.where(differ < 2, b, 0.0) for b in below]
    width = 2
    while width < CHUNK:
        ring = (differ >= width) & (differ < 2 * width)
        corner = [jnp.where(ring, b, 0.0) for b in below]
        half = [mm(inverse[n], corner[n]) for n in every]
        inverse = [inverse[n] - mm(half[n], inverse[n]) for n in every]
        width *= 2
    solved = [
        mm(
            inverse[n],
            jnp.concatenate([value[n] * beta[n], key_vec[n] * (beta[n] * growth[n])], axis=1),
        ).astype(BF16)
        for n in every
    ]
    tails = [jnp.exp(t[:, CHUNK - 1:CHUNK] - t) for t in sums_t]
    drive = [mm(key_t[n] * tails[n], solved[n]) for n in every]
    for n in every:
        key_ref[n] = key_t[n].astype(BF16)
        decay_ref[n] = decay[n]
        growth_ref[n] = growth[n]
        solved_ref[n] = solved[n]
    carried = carry_ref[...]
    for n in every:
        start_ref[n] = carried.astype(BF16)
        falls = jnp.concatenate([fall[n], fall[n]], axis=1)
        moved = falls * carried - mm(drive[n][:, dim:], carried)
        carried = jnp.concatenate([moved[:, :dim], moved[:, dim:] + drive[n][:, :dim]], axis=1)
    carry_ref[...] = carried
    maps_ref[...] = carried.astype(BF16)


def block_maps(core, scalars, mine, theirs, w, ws, dim, per_step):
    groups, each, width = mine.shape
    span = 2 * groups * each
    rows = per_step * CHUNK
    x_spec = pl.BlockSpec((rows // (2 * each), each, width), lambda i: (i, 0, 0))
    count = span // CHUNK

    def stacked(size):
        return pl.BlockSpec((per_step, CHUNK, size), lambda i: (i, 0, 0))

    return pl.pallas_call(
        functools.partial(maps_body, per_step=per_step),
        grid=(span // rows,),
        in_specs=[
            pl.BlockSpec(memory_space=pltpu.SMEM),
            pl.BlockSpec(memory_space=pltpu.SMEM),
            x_spec,
            x_spec,
            pl.BlockSpec((width, dim), lambda i: (0, 1)),
            pl.BlockSpec((width, dim), lambda i: (0, 2)),
            whole(ws.shape),
        ],
        out_specs=[
            stacked(CHUNK), stacked(CHUNK), stacked(dim), stacked(2 * dim), stacked(2 * dim),
            whole((dim, 2 * dim)),
        ],
        out_shape=[
            jax.ShapeDtypeStruct((count, dim, CHUNK), BF16),
            jax.ShapeDtypeStruct((count, CHUNK, CHUNK), F32),
            jax.ShapeDtypeStruct((count, CHUNK, dim), F32),
            jax.ShapeDtypeStruct((count, CHUNK, 2 * dim), BF16),
            jax.ShapeDtypeStruct((count, dim, 2 * dim), BF16),
            jax.ShapeDtypeStruct((dim, 2 * dim), BF16),
        ],
        scratch_shapes=[pltpu.VMEM((dim, 2 * dim), F32)],
        name="block_maps",
    )(core, scalars, mine, theirs, w, w, ws)


def reads_body(
    core_ref, mine_ref, theirs_ref, wq_ref, wg_ref, gain_ref, key_ref, decay_ref, growth_ref, solved_ref, start_ref,
    slope_ref, base_ref, gate_ref,
    *, per_step,
):
    dim = wq_ref.shape[1]
    w_pair = jnp.concatenate([wq_ref[...], wg_ref[...]], axis=1)
    projected = project_rows(core_ref[0], mine_ref, theirs_ref, w_pair)
    every = range(per_step)
    query = [projected[chunk_of(n), :dim] for n in every]
    scores = [mm(query[n], key_ref[n]) * decay_ref[n] for n in every]
    mixed = [mm(scores[n], solved_ref[n]) for n in every]
    both = [mm(query[n] * growth_ref[n] - mixed[n][:, dim:], start_ref[n]) for n in every]
    for n in every:
        slope_ref[chunk_of(n), :] = both[n][:, :dim].astype(BF16)
        base_ref[chunk_of(n), :] = both[n][:, dim:] + mixed[n][:, :dim]
    gate = projected[:, dim:]
    gate_ref[...] = gate * jax.nn.sigmoid(gate) * gain_ref[...]


def block_reads(core, mine, theirs, w, gain, parts, dim, per_step):
    key_t, decay, growth, solved, starts = parts
    groups, each, width = mine.shape
    span = 2 * groups * each
    rows = per_step * CHUNK
    x_spec = pl.BlockSpec((rows // (2 * each), each, width), lambda i: (i, 0, 0))

    def stacked(size):
        return pl.BlockSpec((per_step, CHUNK, size), lambda i: (i, 0, 0))

    by_rows = pl.BlockSpec((rows, dim), lambda i: (i, 0))
    return pl.pallas_call(
        functools.partial(reads_body, per_step=per_step),
        grid=(span // rows,),
        in_specs=[
            pl.BlockSpec(memory_space=pltpu.SMEM),
            x_spec,
            x_spec,
            pl.BlockSpec((width, dim), lambda i: (0, 0)),
            pl.BlockSpec((width, dim), lambda i: (0, 3)),
            whole((1, dim)),
            stacked(CHUNK), stacked(CHUNK), stacked(dim), stacked(2 * dim), stacked(2 * dim),
        ],
        out_specs=[by_rows, by_rows, by_rows],
        out_shape=[
            jax.ShapeDtypeStruct((span, dim), BF16),
            jax.ShapeDtypeStruct((span, dim), F32),
            jax.ShapeDtypeStruct((span, dim), F32),
        ],
        name="block_reads",
    )(core, mine, theirs, w, w, gain[None], key_t, decay, growth, solved, starts)


def norm_body(tokens_ref, gain_ref, out_ref):
    wide = tokens_ref[...].astype(F32)
    normed = (wide * rms_scale(wide) * gain_ref[...]).astype(BF16)
    out_ref[...] = jnp.broadcast_to(normed[None], out_ref.shape)


def norm_copies(tokens, gain, copies):
    return pl.pallas_call(
        norm_body,
        out_shape=jax.ShapeDtypeStruct((copies,) + tokens.shape, BF16),
        name="norm_copies",
    )(tokens, gain[None])


def emit_body(place_ref, maps_ref, init_ref, slope_ref, base_ref, gate_ref, out_ref, state_ref):
    dim = init_ref.shape[0]

    @pl.when(pl.program_id(0) == 0)
    def _():
        state = init_ref[...].T
        for block in range(maps_ref.shape[0] - 1):
            maps = maps_ref[block]
            moved = mm(maps[:, :dim], state) + maps[:, dim:].astype(F32)
            state = jnp.where(block < place_ref[0], moved, state)
        state_ref[...] = state

    head_raw = mm(slope_ref[...], state_ref[...]) + base_ref[...]
    gated = head_raw * rms_scale(head_raw) * gate_ref[...]
    out_ref[...] = gated.astype(BF16).reshape(out_ref.shape)


def emit(place, maps, init, slope, base, gate, outer, inner):
    span, dim = slope.shape
    rows = span // outer
    each = rows // inner
    by_rows = pl.BlockSpec((rows, dim), lambda i: (i, 0))
    return pl.pallas_call(
        emit_body,
        grid=(outer,),
        in_specs=[
            pl.BlockSpec(memory_space=pltpu.SMEM),
            resident(),
            whole(init.shape),
            by_rows,
            by_rows,
            by_rows,
        ],
        out_specs=pl.BlockSpec((inner, 1, each, dim), lambda i: (0, i, 0, 0)),
        out_shape=jax.ShapeDtypeStruct((inner, outer, each, dim), BF16),
        scratch_shapes=[pltpu.VMEM((dim, dim), F32)],
        name="emit",
    )(place, near(maps), init, slope, base, gate)


def project_body(place_ref, gated_ref, *refs):
    *w_refs, out_ref = refs
    core = place_ref[0]
    row = place_ref[1]
    count = len(w_refs) // 2
    left = []
    for at in range(2 * count):
        head = 2 * lax.rem(row + count - at % count, count)
        left.append(gated_ref[head + (core if at < count else 1 - core)])
    total = jnp.dot(
        jnp.concatenate(left, axis=1),
        jnp.concatenate([ref[...] for ref in w_refs], axis=0),
        preferred_element_type=F32,
    )
    out_ref[...] = total.astype(BF16)


def project(place, gated, weights, tile):
    heads, rows, dim = gated.shape
    width = weights[0].shape[1]
    w_spec = pl.BlockSpec((dim, tile), lambda i: (0, i))
    return pl.pallas_call(
        project_body,
        grid=(width // tile,),
        in_specs=[pl.BlockSpec(memory_space=pltpu.SMEM), resident()] + [w_spec] * heads,
        out_specs=pl.BlockSpec((rows, tile), lambda i: (0, i)),
        out_shape=jax.ShapeDtypeStruct((rows, width), BF16),
        name="project",
    )(place, near(gated), *weights)


def join_body(parts_ref, tokens_ref, gain_ref, routes_ref, out_ref, copies_ref):
    width = tokens_ref.shape[1]
    total = parts_ref[0].astype(F32)
    for part in range(1, parts_ref.shape[0]):
        total = total + parts_ref[part].astype(F32)
    summed = total.astype(BF16)
    out_ref[...] = summed
    hidden = tokens_ref[...].astype(F32) + summed.astype(F32)
    normed = (hidden * rms_scale(hidden) * gain_ref[...]).astype(BF16)
    copies = copies_ref.shape[0]
    copies_ref[:, :, :width] = jnp.broadcast_to(normed[None], (copies,) + normed.shape)
    copies_ref[:, :, width:] = routes_ref[...]


def join(parts, tokens, gain, routes):
    copies, rows, extra = routes.shape
    return pl.pallas_call(
        join_body,
        out_shape=[
            jax.ShapeDtypeStruct(tokens.shape, BF16),
            jax.ShapeDtypeStruct((copies, rows, tokens.shape[1] + extra), BF16),
        ],
        name="join",
    )(near(parts), tokens, gain[None], routes)


def experts_body(
    x_ref, gate_a_ref, up_a_ref, down_a_ref, gate_b_ref, up_b_ref, down_b_ref, out_ref,
    rows_ref, total_ref,
    *, tiles,
):
    step = pl.program_id(0)
    width = out_ref.shape[1]

    def tile(gate_ref, up_ref, down_ref):
        x = x_ref[:, :width]
        gate = jnp.dot(x, gate_ref[0], preferred_element_type=F32)
        up = jnp.dot(x, up_ref[0], preferred_element_type=F32)
        activated = (gate * jax.nn.sigmoid(gate) * up).astype(BF16)
        return jnp.dot(activated, down_ref[0], preferred_element_type=F32)

    def weight(which):
        extra = x_ref[:, width:].astype(F32)
        first = 3 * which
        return (
            extra[:, first:first + 1]
            + extra[:, first + 1:first + 2]
            + extra[:, first + 2:first + 3]
        )

    for which, refs in enumerate(
        ((gate_a_ref, up_a_ref, down_a_ref), (gate_b_ref, up_b_ref, down_b_ref))
    ):
        for part in range(tiles):

            @pl.when(step == which * tiles + part)
            def _(refs=refs, which=which, part=part):
                rows = tile(*refs)
                if part > 0:
                    rows = rows_ref[...] + rows
                if part < tiles - 1:
                    rows_ref[...] = rows
                else:
                    scaled = rows.astype(BF16).astype(F32) * weight(which)
                    if which == 0:
                        total_ref[...] = scaled
                    else:
                        out_ref[...] = (total_ref[...] + scaled).astype(BF16)


def experts_of(x, first, second, tiles):
    rows, wide = x.shape
    hidden_units, width = first[1].shape[1:]
    tile = hidden_units // tiles

    def specs(start):
        def at(i):
            return jnp.clip(i - start, 0, tiles - 1)

        return [
            pl.BlockSpec((1, width, tile), lambda i: (0, 0, at(i))),
            pl.BlockSpec((1, width, tile), lambda i: (0, 0, tiles + at(i))),
            pl.BlockSpec((1, tile, width), lambda i: (0, at(i), 0)),
        ]

    return pl.pallas_call(
        functools.partial(experts_body, tiles=tiles),
        grid=(2 * tiles,),
        in_specs=[resident()] + specs(0) + specs(tiles),
        out_specs=whole((rows, width)),
        out_shape=jax.ShapeDtypeStruct((rows, width), BF16),
        scratch_shapes=[pltpu.VMEM((rows, width), F32), pltpu.VMEM((rows, width), F32)],
        name="experts",
    )(near(x), first[0], first[0], first[1], second[0], second[0], second[1])


def total_body(parts_ref, out_ref):
    total = parts_ref[0].astype(F32)
    for part in range(1, parts_ref.shape[0]):
        total = total + parts_ref[part].astype(F32)
    out_ref[...] = total.astype(BF16)


def total_of(parts):
    return pl.pallas_call(
        total_body,
        out_shape=jax.ShapeDtypeStruct(parts.shape[1:], BF16),
        name="total",
    )(near(parts))


def shift_y(value, steps):
    count = lax.axis_size("y")
    return lax.ppermute(value, "y", [(at, (at + steps) % count) for at in range(count)])


def near(value):
    return pltpu.with_memory_space_constraint(value, pltpu.VMEM)


def swap_cores(value):
    return lax.ppermute(value, "core", [(0, 1), (1, 0)])


def exchange(value, axes):
    return lax.all_to_all(value, axes, split_axis=0, concat_axis=0, tiled=True)


def shards(
    tokens,
    gain_in,
    w_heads,
    w_scalar,
    strength_bias,
    decay_rate,
    decay_bias,
    state_init,
    gain_head,
    w_output,
    gain_expert,
    expert_ids,
    gate_weights,
    w_gate_up,
    w_down,
):
    tok_dev, width = tokens.shape
    dim = state_init.shape[-1]
    x_count, y_count, core_count = (lax.axis_size(axis) for axis in ("x", "y", "core"))
    ctx_count = lax.axis_size("ctx")
    chips = x_count * y_count
    expert_total = chips * core_count
    core = lax.axis_index("core").astype(jnp.int32)
    place = lax.axis_index("ctx").astype(jnp.int32)

    copies = norm_copies(tokens, gain_in, chips)
    mine = exchange(copies, ("x", "y"))
    theirs = swap_cores(mine)
    w_here, _ = lax.optimization_barrier((w_output, mine))
    w_rows = [w_here] + [shift_y(w_here, steps) for steps in range(1, y_count)]

    scalars = jnp.concatenate([strength_bias, decay_rate, decay_bias])
    w_logit = jnp.pad(w_scalar, ((0, 0), (0, LANES - w_scalar.shape[1])))
    *parts, maps = block_maps(core[None], scalars, mine, theirs, w_heads, w_logit, dim, PER_STEP)
    maps = jnp.broadcast_to(maps[None], (ctx_count,) + maps.shape)
    all_maps = exchange(maps, "ctx")
    slope, base, gate = block_reads(core[None], mine, theirs, w_heads, gain_head, parts, dim, PER_STEP)
    *w_rows, slope = lax.optimization_barrier((*w_rows, slope))
    w_rows = w_rows + [swap_cores(rows) for rows in w_rows]
    gated = emit(
        place[None], all_maps, state_init[0], slope, base, gate, x_count, y_count * core_count
    )
    heads = y_count * core_count
    gated = exchange(gated, ("y", "core")).reshape(heads, x_count * tok_dev, dim)
    partial = project(jnp.stack([core, lax.axis_index("y").astype(jnp.int32)]), gated, w_rows, 512).reshape(x_count, tok_dev, width)

    other_gate_up = swap_cores(w_gate_up)
    other_down = swap_cores(w_down)
    numbers = jnp.arange(expert_total, dtype=jnp.int32)
    named = expert_ids[:, :, None] == numbers[None, None, :]
    routes = jnp.sum(jnp.where(named, gate_weights[:, :, None], 0.0), axis=1)
    routes = routes.reshape(tok_dev, chips, core_count).transpose(1, 0, 2)
    routes = jnp.where(core == 0, routes, routes[:, :, ::-1])
    routes = jnp.stack(pieces(routes), axis=-1).reshape(chips, tok_dev, -1)
    routes = jnp.pad(routes, ((0, 0), (0, 0), (0, LANES - routes.shape[-1])))

    summed, copies = join(exchange(partial, "x"), tokens, gain_expert, routes)
    received = exchange(copies, ("x", "y")).reshape(chips * tok_dev, -1)
    outputs = experts_of(received, (w_gate_up, w_down), (other_gate_up, other_down), 2)
    outputs = outputs.reshape(chips, tok_dev, width)
    expert_out = total_of(exchange(outputs, ("x", "y")))
    return (summed, expert_out)


PER_STEP = 4


def solution(mesh):
    fine = Mesh(mesh.devices.reshape(mesh.shape["ctx"], 4, 4, 2), ("ctx", "x", "y", "core"))
    exp = ("x", "y", "core")
    rows = ("ctx", "x", "y", "core")
    return jax.shard_map(
        shards,
        mesh=fine,
        in_specs=(
            P(rows, None),
            P(),
            P(None, exp),
            P(None, exp),
            P(exp),
            P(exp),
            P(exp),
            P(exp, None, None),
            P(),
            P(exp, None),
            P(),
            P(rows, None),
            P(rows, None),
            P(exp, None, None),
            P(exp, None, None),
        ),
        out_specs=(P(rows, None), P(rows, None)),
        check_vma=False,
    )
```

```python
import functools
import jax
import jax.numpy as jnp
from jax import lax
from jax.experimental import pallas as pl
from jax.experimental.pallas import tpu as pltpu
from jax.sharding import Mesh, PartitionSpec as P

EPSILON = 1e-06
F32 = jnp.float32
BF16 = jnp.bfloat16
CHUNK = 128
LANES = 128


def mm(a, b):
    return jnp.dot(a.astype(BF16), b.astype(BF16), preferred_element_type=F32)


def pieces(a):
    high = a.astype(BF16)
    rest = a - high.astype(F32)
    middle = rest.astype(BF16)
    low = (rest - middle.astype(F32)).astype(BF16)
    return high, middle, low


def rms_scale(values):
    return lax.rsqrt(jnp.mean(values * values, axis=-1, keepdims=True) + EPSILON)


def chunk_of(n):
    return slice(n * CHUNK, (n + 1) * CHUNK)


def resident():
    return pl.BlockSpec(memory_space=pltpu.VMEM)


def whole(shape):
    return pl.BlockSpec(shape, lambda i: (0,) * len(shape))


def project_rows(core, mine_ref, theirs_ref, w):
    groups, each, width = mine_ref.shape
    ours = jnp.dot(mine_ref[...].reshape(groups * each, width), w, preferred_element_type=F32)
    others = jnp.dot(theirs_ref[...].reshape(groups * each, width), w, preferred_element_type=F32)
    even = jnp.where(core == 0, ours, others)
    odd = jnp.where(core == 0, others, ours)
    rows = []
    for group in range(groups):
        at = slice(group * each, (group + 1) * each)
        rows += [even[at], odd[at]]
    return jnp.concatenate(rows, axis=0)


def maps_body(
    core_ref, scal_ref, mine_ref, theirs_ref, wk_ref, wv_ref, ws_ref,
    key_ref, decay_ref, growth_ref, solved_ref, start_ref, maps_ref, carry_ref,
    *, per_step,
):
    dim = wk_ref.shape[1]
    step = pl.program_id(0)

    @pl.when(step == 0)
    def _():
        rows = lax.broadcasted_iota(jnp.int32, (dim, 2 * dim), 0)
        cols = lax.broadcasted_iota(jnp.int32, (dim, 2 * dim), 1)
        carry_ref[...] = jnp.where(rows == cols, 1.0, 0.0).astype(F32)

    lift = scal_ref[0]
    rate = scal_ref[1]
    bias = scal_ref[2]
    rows = lax.broadcasted_iota(jnp.int32, (CHUNK, CHUNK), 0)
    cols = lax.broadcasted_iota(jnp.int32, (CHUNK, CHUNK), 1)
    differ = jnp.bitwise_xor(rows, cols)
    lower = rows >= cols
    strict = rows > cols
    lower_ones = jnp.where(lower, 1.0, 0.0).astype(BF16)
    eye = jnp.where(rows == cols, 1.0, 0.0).astype(F32)
    w_all = jnp.concatenate([wk_ref[...], wv_ref[...], ws_ref[...]], axis=1)
    projected = project_rows(core_ref[0], mine_ref, theirs_ref, w_all)
    logits = projected[:, 2 * dim:]
    every = range(per_step)
    key_raw = [projected[chunk_of(n), :dim] for n in every]
    value = [projected[chunk_of(n), dim:2 * dim] for n in every]
    strength = [jax.nn.sigmoid(logits[chunk_of(n), 0:1] + lift) for n in every]
    beta = [jnp.broadcast_to(s, (CHUNK, dim)) for s in strength]
    sums = []
    for n in every:
        moved = logits[chunk_of(n), 1:2] + bias
        softplus = jnp.maximum(moved, 0.0) + jnp.log1p(jnp.exp(-jnp.abs(moved)))
        high, middle, low = pieces(jnp.broadcast_to(-rate * softplus, (CHUNK, CHUNK)))
        sums.append(
            jnp.dot(lower_ones, high, preferred_element_type=F32)
            + jnp.dot(lower_ones, middle, preferred_element_type=F32)
            + jnp.dot(lower_ones, low, preferred_element_type=F32)
        )
    sums_t = [s.T for s in sums]
    key_vec = [
        k * lax.rsqrt(jnp.sum(k * k, axis=-1, keepdims=True) + EPSILON) for k in key_raw
    ]
    key_t = [k.T for k in key_vec]
    growth = [jnp.exp(s) for s in sums]
    fall = [jnp.exp(s[CHUNK - 1:CHUNK, :]) for s in sums]
    decay = [
        jnp.where(lower, jnp.exp(jnp.minimum(s - t, 0.0)), 0.0) for s, t in zip(sums, sums_t)
    ]
    gram = [mm(k, t) for k, t in zip(key_vec, key_t)]
    below = [
        jnp.where(strict, gram[n] * decay[n] * beta[n], 0.0) for n in every
    ]
    inverse = [eye - jnp.where(differ < 2, b, 0.0) for b in below]
    width = 2
    while width < CHUNK:
        ring = (differ >= width) & (differ < 2 * width)
        corner = [jnp.where(ring, b, 0.0) for b in below]
        half = [mm(inverse[n], corner[n]) for n in every]
        inverse = [inverse[n] - mm(half[n], inverse[n]) for n in every]
        width *= 2
    solved = [
        mm(
            inverse[n],
            jnp.concatenate([value[n] * beta[n], key_vec[n] * (beta[n] * growth[n])], axis=1),
        ).astype(BF16)
        for n in every
    ]
    tails = [jnp.exp(t[:, CHUNK - 1:CHUNK] - t) for t in sums_t]
    drive = [mm(key_t[n] * tails[n], solved[n]) for n in every]
    for n in every:
        key_ref[n] = key_t[n].astype(BF16)
        decay_ref[n] = decay[n]
        growth_ref[n] = growth[n]
        solved_ref[n] = solved[n]
    carried = carry_ref[...]
    for n in every:
        start_ref[n] = carried.astype(BF16)
        falls = jnp.concatenate([fall[n], fall[n]], axis=1)
        moved = falls * carried - mm(drive[n][:, dim:], carried)
        carried = jnp.concatenate([moved[:, :dim], moved[:, dim:] + drive[n][:, :dim]], axis=1)
    carry_ref[...] = carried

    @pl.when(step == pl.num_programs(0) - 1)
    def _():
        maps_ref[...] = jnp.broadcast_to(carried.astype(BF16)[None], maps_ref.shape)


def block_maps(core, scalars, mine, theirs, w, ws, dim, copies, per_step):
    groups, each, width = mine.shape
    span = 2 * groups * each
    rows = per_step * CHUNK
    x_spec = pl.BlockSpec((rows // (2 * each), each, width), lambda i: (i, 0, 0))
    count = span // CHUNK

    def stacked(size):
        return pl.BlockSpec((per_step, CHUNK, size), lambda i: (i, 0, 0))

    return pl.pallas_call(
        functools.partial(maps_body, per_step=per_step),
        grid=(span // rows,),
        in_specs=[
            pl.BlockSpec(memory_space=pltpu.SMEM),
            pl.BlockSpec(memory_space=pltpu.SMEM),
            x_spec,
            x_spec,
            pl.BlockSpec((width, dim), lambda i: (0, 1)),
            pl.BlockSpec((width, dim), lambda i: (0, 2)),
            whole(ws.shape),
        ],
        out_specs=[
            stacked(CHUNK), stacked(CHUNK), stacked(dim), stacked(2 * dim), stacked(2 * dim),
            whole((copies, dim, 2 * dim)),
        ],
        out_shape=[
            jax.ShapeDtypeStruct((count, dim, CHUNK), BF16),
            jax.ShapeDtypeStruct((count, CHUNK, CHUNK), F32),
            jax.ShapeDtypeStruct((count, CHUNK, dim), F32),
            jax.ShapeDtypeStruct((count, CHUNK, 2 * dim), BF16),
            jax.ShapeDtypeStruct((count, dim, 2 * dim), BF16),
            jax.ShapeDtypeStruct((copies, dim, 2 * dim), BF16),
        ],
        scratch_shapes=[pltpu.VMEM((dim, 2 * dim), F32)],
        name="block_maps",
    )(core, scalars, mine, theirs, w, w, ws)


def reads_body(
    core_ref, mine_ref, theirs_ref, wq_ref, wg_ref, gain_ref, key_ref, decay_ref, growth_ref, solved_ref, start_ref,
    slope_ref, base_ref, gate_ref,
    *, per_step,
):
    dim = wq_ref.shape[1]
    w_pair = jnp.concatenate([wq_ref[...], wg_ref[...]], axis=1)
    projected = project_rows(core_ref[0], mine_ref, theirs_ref, w_pair)
    every = range(per_step)
    query = [projected[chunk_of(n), :dim] for n in every]
    scores = [mm(query[n], key_ref[n]) * decay_ref[n] for n in every]
    mixed = [mm(scores[n], solved_ref[n]) for n in every]
    both = [mm(query[n] * growth_ref[n] - mixed[n][:, dim:], start_ref[n]) for n in every]
    for n in every:
        slope_ref[chunk_of(n), :] = both[n][:, :dim].astype(BF16)
        base_ref[chunk_of(n), :] = both[n][:, dim:] + mixed[n][:, :dim]
    gate = projected[:, dim:]
    gate_ref[...] = gate * jax.nn.sigmoid(gate) * gain_ref[...]


def block_reads(core, mine, theirs, w, gain, parts, dim, per_step):
    key_t, decay, growth, solved, starts = parts
    groups, each, width = mine.shape
    span = 2 * groups * each
    rows = per_step * CHUNK
    x_spec = pl.BlockSpec((rows // (2 * each), each, width), lambda i: (i, 0, 0))

    def stacked(size):
        return pl.BlockSpec((per_step, CHUNK, size), lambda i: (i, 0, 0))

    by_rows = pl.BlockSpec((rows, dim), lambda i: (i, 0))
    return pl.pallas_call(
        functools.partial(reads_body, per_step=per_step),
        grid=(span // rows,),
        in_specs=[
            pl.BlockSpec(memory_space=pltpu.SMEM),
            x_spec,
            x_spec,
            pl.BlockSpec((width, dim), lambda i: (0, 0)),
            pl.BlockSpec((width, dim), lambda i: (0, 3)),
            whole((1, dim)),
            stacked(CHUNK), stacked(CHUNK), stacked(dim), stacked(2 * dim), stacked(2 * dim),
        ],
        out_specs=[by_rows, by_rows, by_rows],
        out_shape=[
            jax.ShapeDtypeStruct((span, dim), BF16),
            jax.ShapeDtypeStruct((span, dim), F32),
            jax.ShapeDtypeStruct((span, dim), F32),
        ],
        name="block_reads",
    )(core, mine, theirs, w, w, gain[None], key_t, decay, growth, solved, starts)


def norm_body(tokens_ref, gain_ref, out_ref):
    wide = tokens_ref[...].astype(F32)
    normed = (wide * rms_scale(wide) * gain_ref[...]).astype(BF16)
    out_ref[...] = jnp.broadcast_to(normed[None], out_ref.shape)


def norm_copies(tokens, gain, copies):
    return pl.pallas_call(
        norm_body,
        out_shape=jax.ShapeDtypeStruct((copies,) + tokens.shape, BF16),
        name="norm_copies",
    )(tokens, gain[None])


def emit_body(place_ref, maps_ref, init_ref, slope_ref, base_ref, gate_ref, out_ref, state_ref):
    dim = init_ref.shape[0]

    @pl.when(pl.program_id(0) == 0)
    def _():
        rows = lax.broadcasted_iota(jnp.int32, (dim, 2 * dim), 0)
        cols = lax.broadcasted_iota(jnp.int32, (dim, 2 * dim), 1)
        still = jnp.where(rows == cols, 1.0, 0.0).astype(F32)
        steps = [
            jnp.where(block < place_ref[0], maps_ref[block].astype(F32), still)
            for block in range(maps_ref.shape[0] - 1)
        ]

        def after(later, earlier):
            both = mm(later[:, :dim], earlier)
            return jnp.concatenate([both[:, :dim], both[:, dim:] + later[:, dim:]], axis=1)

        state = mm(steps[0][:, :dim], init_ref[...].T) + steps[0][:, dim:]
        steps = steps[1:]
        while steps:
            rest = [after(b, a) for a, b in zip(steps[1::2], steps[2::2])]
            if len(steps) % 2 == 0:
                pairs = [after(b, a) for a, b in zip(steps[0::2], steps[1::2])]
                state = mm(pairs[0][:, :dim], state) + pairs[0][:, dim:]
                steps = pairs[1:]
            else:
                state = mm(steps[0][:, :dim], state) + steps[0][:, dim:]
                steps = rest
        state_ref[...] = state

    head_raw = mm(slope_ref[...], state_ref[...]) + base_ref[...]
    gated = head_raw * rms_scale(head_raw) * gate_ref[...]
    out_ref[...] = gated.astype(BF16).reshape(out_ref.shape)


def emit(place, maps, init, slope, base, gate, outer, inner):
    span, dim = slope.shape
    rows = span // outer
    each = rows // inner
    by_rows = pl.BlockSpec((rows, dim), lambda i: (i, 0))
    return pl.pallas_call(
        emit_body,
        grid=(outer,),
        in_specs=[
            pl.BlockSpec(memory_space=pltpu.SMEM),
            resident(),
            whole(init.shape),
            by_rows,
            by_rows,
            by_rows,
        ],
        out_specs=pl.BlockSpec((inner, 1, each, dim), lambda i: (0, i, 0, 0)),
        out_shape=jax.ShapeDtypeStruct((inner, outer, each, dim), BF16),
        scratch_shapes=[pltpu.VMEM((dim, dim), F32)],
        name="emit",
    )(place, near(maps), init, slope, base, gate)


def project_body(place_ref, gated_ref, *refs):
    *w_refs, out_ref = refs
    core = place_ref[0]
    row = place_ref[1]
    count = gated_ref.shape[0] // 2
    step = 2 * core - 1 + count
    rows = [row, row, row + step, row + step, row + 2, row + count - step + count,
            row + count - step + count, row + 2]
    cores = [core, 1 - core, core, 1 - core, core, 1 - core, core, 1 - core]
    left = [gated_ref[2 * lax.rem(at, count) + side] for at, side in zip(rows, cores)]
    total = jnp.dot(
        jnp.concatenate(left, axis=1),
        jnp.concatenate([ref[...] for ref in w_refs], axis=0),
        preferred_element_type=F32,
    )
    out_ref[...] = total.astype(BF16).reshape(out_ref.shape)


def project(place, gated, weights, parts, tile):
    heads, rows, dim = gated.shape
    width = weights[0].shape[1]
    return pl.pallas_call(
        project_body,
        grid=(width // tile,),
        in_specs=[pl.BlockSpec(memory_space=pltpu.SMEM), resident()] + [
            pl.BlockSpec((rows.shape[0], tile), lambda i: (0, i)) for rows in weights
        ],
        out_specs=pl.BlockSpec((parts, rows // parts, tile), lambda i: (0, 0, i)),
        out_shape=jax.ShapeDtypeStruct((parts, rows // parts, width), BF16),
        name="project",
    )(place, near(gated), *weights)


def join_body(parts_ref, tokens_ref, gain_ref, routes_ref, out_ref, copies_ref):
    width = tokens_ref.shape[1]
    total = parts_ref[0].astype(F32)
    for part in range(1, parts_ref.shape[0]):
        total = total + parts_ref[part].astype(F32)
    summed = total.astype(BF16)
    out_ref[...] = summed
    hidden = tokens_ref[...].astype(F32) + summed.astype(F32)
    normed = (hidden * rms_scale(hidden) * gain_ref[...]).astype(BF16)
    copies = copies_ref.shape[0]
    copies_ref[:, :, :width] = jnp.broadcast_to(normed[None], (copies,) + normed.shape)
    copies_ref[:, :, width:] = routes_ref[...]


def join(parts, tokens, gain, routes):
    copies, rows, extra = routes.shape
    return pl.pallas_call(
        join_body,
        out_shape=[
            jax.ShapeDtypeStruct(tokens.shape, BF16),
            jax.ShapeDtypeStruct((copies, rows, tokens.shape[1] + extra), BF16),
        ],
        name="join",
    )(near(parts), tokens, gain[None], routes)


def experts_body(
    x_ref, gate_a_ref, up_a_ref, down_a_ref, gate_b_ref, up_b_ref, down_b_ref, out_ref,
    rows_ref, total_ref,
    *, tiles,
):
    step = pl.program_id(0)
    groups, each, width = out_ref.shape
    count = groups * each

    def tile(gate_ref, up_ref, down_ref):
        x = x_ref[:, :, :width].reshape(count, width)
        gate = jnp.dot(x, gate_ref[0], preferred_element_type=F32)
        up = jnp.dot(x, up_ref[0], preferred_element_type=F32)
        activated = (gate * jax.nn.sigmoid(gate) * up).astype(BF16)
        return jnp.dot(activated, down_ref[0], preferred_element_type=F32)

    def weight(which):
        extra = x_ref[:, :, width:].astype(F32).reshape(count, -1)
        first = 3 * which
        return (
            extra[:, first:first + 1]
            + extra[:, first + 1:first + 2]
            + extra[:, first + 2:first + 3]
        )

    for which, refs in enumerate(
        ((gate_a_ref, up_a_ref, down_a_ref), (gate_b_ref, up_b_ref, down_b_ref))
    ):
        for part in range(tiles):

            @pl.when(step == which * tiles + part)
            def _(refs=refs, which=which, part=part):
                rows = tile(*refs)
                if part > 0:
                    rows = rows_ref[...] + rows
                if part < tiles - 1:
                    rows_ref[...] = rows
                else:
                    scaled = rows.astype(BF16).astype(F32) * weight(which)
                    if which == 0:
                        total_ref[...] = scaled
                    else:
                        out_ref[...] = (total_ref[...] + scaled).astype(BF16).reshape(out_ref.shape)


def experts_of(x, first, second, tiles):
    groups, each, wide = x.shape
    rows = groups * each
    hidden_units, width = first[1].shape[1:]
    tile = hidden_units // tiles

    def specs(start):
        def at(i):
            return jnp.clip(i - start, 0, tiles - 1)

        return [
            pl.BlockSpec((1, width, tile), lambda i: (0, 0, at(i))),
            pl.BlockSpec((1, width, tile), lambda i: (0, 0, tiles + at(i))),
            pl.BlockSpec((1, tile, width), lambda i: (0, at(i), 0)),
        ]

    return pl.pallas_call(
        functools.partial(experts_body, tiles=tiles),
        grid=(2 * tiles,),
        in_specs=[resident()] + specs(0) + specs(tiles),
        out_specs=resident(),
        out_shape=jax.ShapeDtypeStruct((groups, each, width), BF16),
        scratch_shapes=[pltpu.VMEM((rows, width), F32), pltpu.VMEM((rows, width), F32)],
        name="experts",
    )(near(x), first[0], first[0], first[1], second[0], second[0], second[1])


def total_body(parts_ref, out_ref):
    total = parts_ref[0].astype(F32)
    for part in range(1, parts_ref.shape[0]):
        total = total + parts_ref[part].astype(F32)
    out_ref[...] = total.astype(BF16)


def total_of(parts):
    return pl.pallas_call(
        total_body,
        out_shape=jax.ShapeDtypeStruct(parts.shape[1:], BF16),
        name="total",
    )(near(parts))


def send_y(value):
    count = lax.axis_size("y")
    up = [(2 * at, 2 * ((at + 1) % count)) for at in range(count)]
    down = [(2 * at + 1, 2 * ((at + count - 1) % count) + 1) for at in range(count)]
    return lax.ppermute(value, ("y", "core"), up + down)


def near(value):
    return pltpu.with_memory_space_constraint(value, pltpu.VMEM)


def swap_cores(value):
    return lax.ppermute(value, "core", [(0, 1), (1, 0)])


def exchange(value, axes):
    return lax.all_to_all(value, axes, split_axis=0, concat_axis=0, tiled=True)


def shards(
    tokens,
    gain_in,
    w_heads,
    w_scalar,
    strength_bias,
    decay_rate,
    decay_bias,
    state_init,
    gain_head,
    w_output,
    gain_expert,
    expert_ids,
    gate_weights,
    w_gate_up,
    w_down,
):
    tok_dev, width = tokens.shape
    dim = state_init.shape[-1]
    x_count, y_count, core_count = (lax.axis_size(axis) for axis in ("x", "y", "core"))
    ctx_count = lax.axis_size("ctx")
    chips = x_count * y_count
    expert_total = chips * core_count
    core = lax.axis_index("core").astype(jnp.int32)
    place = lax.axis_index("ctx").astype(jnp.int32)

    copies = norm_copies(tokens, gain_in, chips)
    mine = exchange(copies, ("x", "y"))
    theirs = swap_cores(mine)
    pair = jnp.concatenate([w_output, swap_cores(w_output)], axis=0)
    pair, _ = lax.optimization_barrier((pair, mine))
    beside = send_y(pair)

    scalars = jnp.concatenate([strength_bias, decay_rate, decay_bias])
    w_logit = jnp.pad(w_scalar, ((0, 0), (0, LANES - w_scalar.shape[1])))
    *parts, maps = block_maps(core[None], scalars, mine, theirs, w_heads, w_logit, dim, ctx_count, PER_STEP)
    beside, maps, far_gate_up, far_down = lax.optimization_barrier(
        (beside, maps, w_gate_up, w_down)
    )
    across = send_y(beside[:dim])
    all_maps = exchange(maps, "ctx")
    slope, base, gate = block_reads(core[None], mine, theirs, w_heads, gain_head, parts, dim, PER_STEP)
    across, slope = lax.optimization_barrier((across, slope))
    w_rows = [pair, beside, across, swap_cores(beside), swap_cores(across)]
    gated = emit(
        place[None], all_maps, state_init[0], slope, base, gate, x_count, y_count * core_count
    )
    heads = y_count * core_count
    gated = exchange(gated, ("y", "core")).reshape(heads, x_count * tok_dev, dim)
    partial = project(jnp.stack([core, lax.axis_index("y").astype(jnp.int32)]), gated, w_rows, x_count, 512)

    other_gate_up = swap_cores(far_gate_up)
    other_down = swap_cores(far_down)
    numbers = jnp.arange(expert_total, dtype=jnp.int32)
    named = expert_ids[:, :, None] == numbers[None, None, :]
    routes = jnp.sum(jnp.where(named, gate_weights[:, :, None], 0.0), axis=1)
    routes = routes.reshape(tok_dev, chips, core_count).transpose(1, 0, 2)
    routes = jnp.where(core == 0, routes, routes[:, :, ::-1])
    routes = jnp.stack(pieces(routes), axis=-1).reshape(chips, tok_dev, -1)
    routes = jnp.pad(routes, ((0, 0), (0, 0), (0, LANES - routes.shape[-1])))

    summed, copies = join(exchange(partial, "x"), tokens, gain_expert, routes)
    received = exchange(copies, ("x", "y"))
    outputs = experts_of(received, (w_gate_up, w_down), (other_gate_up, other_down), 2)
    expert_out = total_of(exchange(outputs, ("x", "y")))
    return (summed, expert_out)


PER_STEP = 4


def solution(mesh):
    fine = Mesh(mesh.devices.reshape(mesh.shape["ctx"], 4, 4, 2), ("ctx", "x", "y", "core"))
    exp = ("x", "y", "core")
    rows = ("ctx", "x", "y", "core")
    return jax.shard_map(
        shards,
        mesh=fine,
        in_specs=(
            P(rows, None),
            P(),
            P(None, exp),
            P(None, exp),
            P(exp),
            P(exp),
            P(exp),
            P(exp, None, None),
            P(),
            P(exp, None),
            P(),
            P(rows, None),
            P(rows, None),
            P(exp, None, None),
            P(exp, None, None),
        ),
        out_specs=(P(rows, None), P(rows, None)),
        check_vma=False,
    )
```

```python
import functools
import jax
import jax.numpy as jnp
from jax import lax
from jax.experimental import pallas as pl
from jax.experimental.pallas import tpu as pltpu
from jax.sharding import Mesh, PartitionSpec as P

EPSILON = 1e-06
F32 = jnp.float32
BF16 = jnp.bfloat16
CHUNK = 128
LANES = 128


def mm(a, b):
    return jnp.dot(a.astype(BF16), b.astype(BF16), preferred_element_type=F32)


def pieces(a):
    high = a.astype(BF16)
    rest = a - high.astype(F32)
    middle = rest.astype(BF16)
    low = (rest - middle.astype(F32)).astype(BF16)
    return high, middle, low


def rms_scale(values):
    return lax.rsqrt(jnp.mean(values * values, axis=-1, keepdims=True) + EPSILON)


def chunk_of(n):
    return slice(n * CHUNK, (n + 1) * CHUNK)


def resident():
    return pl.BlockSpec(memory_space=pltpu.VMEM)


def whole(shape):
    return pl.BlockSpec(shape, lambda i: (0,) * len(shape))


def project_rows(core, mine_ref, theirs_ref, w):
    groups, each, width = mine_ref.shape
    ours = jnp.dot(mine_ref[...].reshape(groups * each, width), w, preferred_element_type=F32)
    others = jnp.dot(theirs_ref[...].reshape(groups * each, width), w, preferred_element_type=F32)
    even = jnp.where(core == 0, ours, others)
    odd = jnp.where(core == 0, others, ours)
    rows = []
    for group in range(groups):
        at = slice(group * each, (group + 1) * each)
        rows += [even[at], odd[at]]
    return jnp.concatenate(rows, axis=0)


def maps_body(
    core_ref, scal_ref, mine_ref, theirs_ref, wk_ref, wv_ref, ws_ref,
    key_ref, decay_ref, growth_ref, solved_ref, start_ref, maps_ref, carry_ref,
    *, per_step,
):
    dim = wk_ref.shape[1]
    step = pl.program_id(0)

    @pl.when(step == 0)
    def _():
        rows = lax.broadcasted_iota(jnp.int32, (dim, 2 * dim), 0)
        cols = lax.broadcasted_iota(jnp.int32, (dim, 2 * dim), 1)
        carry_ref[...] = jnp.where(rows == cols, 1.0, 0.0).astype(F32)

    lift = scal_ref[0]
    rate = scal_ref[1]
    bias = scal_ref[2]
    rows = lax.broadcasted_iota(jnp.int32, (CHUNK, CHUNK), 0)
    cols = lax.broadcasted_iota(jnp.int32, (CHUNK, CHUNK), 1)
    differ = jnp.bitwise_xor(rows, cols)
    lower = rows >= cols
    strict = rows > cols
    lower_ones = jnp.where(lower, 1.0, 0.0).astype(BF16)
    eye = jnp.where(rows == cols, 1.0, 0.0).astype(F32)
    w_all = jnp.concatenate([wk_ref[...], wv_ref[...], ws_ref[...]], axis=1)
    projected = project_rows(core_ref[0], mine_ref, theirs_ref, w_all)
    logits = projected[:, 2 * dim:]
    every = range(per_step)
    key_raw = [projected[chunk_of(n), :dim] for n in every]
    value = [projected[chunk_of(n), dim:2 * dim] for n in every]
    strength = [jax.nn.sigmoid(logits[chunk_of(n), 0:1] + lift) for n in every]
    beta = [jnp.broadcast_to(s, (CHUNK, dim)) for s in strength]
    sums = []
    for n in every:
        moved = logits[chunk_of(n), 1:2] + bias
        softplus = jnp.maximum(moved, 0.0) + jnp.log1p(jnp.exp(-jnp.abs(moved)))
        high, middle, low = pieces(jnp.broadcast_to(-rate * softplus, (CHUNK, CHUNK)))
        sums.append(
            jnp.dot(lower_ones, high, preferred_element_type=F32)
            + jnp.dot(lower_ones, middle, preferred_element_type=F32)
            + jnp.dot(lower_ones, low, preferred_element_type=F32)
        )
    sums_t = [s.T for s in sums]
    key_vec = [
        k * lax.rsqrt(jnp.sum(k * k, axis=-1, keepdims=True) + EPSILON) for k in key_raw
    ]
    key_t = [k.T for k in key_vec]
    growth = [jnp.exp(s) for s in sums]
    fall = [jnp.exp(s[CHUNK - 1:CHUNK, :]) for s in sums]
    decay = [
        jnp.where(lower, jnp.exp(jnp.minimum(s - t, 0.0)), 0.0) for s, t in zip(sums, sums_t)
    ]
    gram = [mm(k, t) for k, t in zip(key_vec, key_t)]
    below = [
        jnp.where(strict, gram[n] * decay[n] * beta[n], 0.0) for n in every
    ]
    inverse = [eye - jnp.where(differ < 2, b, 0.0) for b in below]
    width = 2
    while width < CHUNK:
        ring = (differ >= width) & (differ < 2 * width)
        corner = [jnp.where(ring, b, 0.0) for b in below]
        half = [mm(inverse[n], corner[n]) for n in every]
        inverse = [inverse[n] - mm(half[n], inverse[n]) for n in every]
        width *= 2
    solved = [
        mm(
            inverse[n],
            jnp.concatenate([value[n] * beta[n], key_vec[n] * (beta[n] * growth[n])], axis=1),
        ).astype(BF16)
        for n in every
    ]
    tails = [jnp.exp(t[:, CHUNK - 1:CHUNK] - t) for t in sums_t]
    drive = [mm(key_t[n] * tails[n], solved[n]) for n in every]
    for n in every:
        key_ref[n] = key_t[n].astype(BF16)
        decay_ref[n] = decay[n]
        growth_ref[n] = growth[n]
        solved_ref[n] = solved[n]
    carried = carry_ref[...]
    for n in every:
        start_ref[n] = carried.astype(BF16)
        falls = jnp.concatenate([fall[n], fall[n]], axis=1)
        moved = falls * carried - mm(drive[n][:, dim:], carried)
        carried = jnp.concatenate([moved[:, :dim], moved[:, dim:] + drive[n][:, :dim]], axis=1)
    carry_ref[...] = carried

    @pl.when(step == pl.num_programs(0) - 1)
    def _():
        maps_ref[...] = jnp.broadcast_to(carried.astype(BF16)[None], maps_ref.shape)


def block_maps(core, scalars, mine, theirs, w, ws, dim, copies, per_step):
    groups, each, width = mine.shape
    span = 2 * groups * each
    rows = per_step * CHUNK
    x_spec = pl.BlockSpec((rows // (2 * each), each, width), lambda i: (i, 0, 0))
    count = span // CHUNK

    def stacked(size):
        return pl.BlockSpec((per_step, CHUNK, size), lambda i: (i, 0, 0))

    return pl.pallas_call(
        functools.partial(maps_body, per_step=per_step),
        grid=(span // rows,),
        in_specs=[
            pl.BlockSpec(memory_space=pltpu.SMEM),
            pl.BlockSpec(memory_space=pltpu.SMEM),
            x_spec,
            x_spec,
            pl.BlockSpec((width, dim), lambda i: (0, 1)),
            pl.BlockSpec((width, dim), lambda i: (0, 2)),
            whole(ws.shape),
        ],
        out_specs=[
            stacked(CHUNK), stacked(CHUNK), stacked(dim), stacked(2 * dim), stacked(2 * dim),
            whole((copies, dim, 2 * dim)),
        ],
        out_shape=[
            jax.ShapeDtypeStruct((count, dim, CHUNK), BF16),
            jax.ShapeDtypeStruct((count, CHUNK, CHUNK), F32),
            jax.ShapeDtypeStruct((count, CHUNK, dim), F32),
            jax.ShapeDtypeStruct((count, CHUNK, 2 * dim), BF16),
            jax.ShapeDtypeStruct((count, dim, 2 * dim), BF16),
            jax.ShapeDtypeStruct((copies, dim, 2 * dim), BF16),
        ],
        scratch_shapes=[pltpu.VMEM((dim, 2 * dim), F32)],
        name="block_maps",
    )(core, scalars, mine, theirs, w, w, ws)


def reads_body(
    core_ref, mine_ref, theirs_ref, wq_ref, wg_ref, gain_ref, key_ref, decay_ref, growth_ref, solved_ref, start_ref,
    slope_ref, base_ref, gate_ref,
    *, per_step,
):
    dim = wq_ref.shape[1]
    w_pair = jnp.concatenate([wq_ref[...], wg_ref[...]], axis=1)
    projected = project_rows(core_ref[0], mine_ref, theirs_ref, w_pair)
    every = range(per_step)
    query = [projected[chunk_of(n), :dim] for n in every]
    scores = [mm(query[n], key_ref[n]) * decay_ref[n] for n in every]
    mixed = [mm(scores[n], solved_ref[n]) for n in every]
    both = [mm(query[n] * growth_ref[n] - mixed[n][:, dim:], start_ref[n]) for n in every]
    for n in every:
        slope_ref[chunk_of(n), :] = both[n][:, :dim].astype(BF16)
        base_ref[chunk_of(n), :] = both[n][:, dim:] + mixed[n][:, :dim]
    gate = projected[:, dim:]
    gate_ref[...] = gate * jax.nn.sigmoid(gate) * gain_ref[...]


def block_reads(core, mine, theirs, w, gain, parts, dim, per_step):
    key_t, decay, growth, solved, starts = parts
    groups, each, width = mine.shape
    span = 2 * groups * each
    rows = per_step * CHUNK
    x_spec = pl.BlockSpec((rows // (2 * each), each, width), lambda i: (i, 0, 0))

    def stacked(size):
        return pl.BlockSpec((per_step, CHUNK, size), lambda i: (i, 0, 0))

    by_rows = pl.BlockSpec((rows, dim), lambda i: (i, 0))
    return pl.pallas_call(
        functools.partial(reads_body, per_step=per_step),
        grid=(span // rows,),
        in_specs=[
            pl.BlockSpec(memory_space=pltpu.SMEM),
            x_spec,
            x_spec,
            pl.BlockSpec((width, dim), lambda i: (0, 0)),
            pl.BlockSpec((width, dim), lambda i: (0, 3)),
            whole((1, dim)),
            stacked(CHUNK), stacked(CHUNK), stacked(dim), stacked(2 * dim), stacked(2 * dim),
        ],
        out_specs=[by_rows, by_rows, by_rows],
        out_shape=[
            jax.ShapeDtypeStruct((span, dim), BF16),
            jax.ShapeDtypeStruct((span, dim), F32),
            jax.ShapeDtypeStruct((span, dim), F32),
        ],
        name="block_reads",
    )(core, mine, theirs, w, w, gain[None], key_t, decay, growth, solved, starts)


def send_copies(copies):
    for copy in copies:
        copy.start()
    for copy in copies:
        copy.wait()


def norm_body(tokens_ref, gain_ref, out_ref, normed_ref, sems):
    wide = tokens_ref[...].astype(F32)
    normed_ref[...] = (wide * rms_scale(wide) * gain_ref[...]).astype(BF16)
    send_copies(
        [
            pltpu.make_async_copy(normed_ref, out_ref.at[at], sems.at[at])
            for at in range(out_ref.shape[0])
        ]
    )


def norm_copies(tokens, gain, copies):
    return pl.pallas_call(
        norm_body,
        out_specs=pl.BlockSpec(memory_space=pl.ANY),
        out_shape=jax.ShapeDtypeStruct((copies,) + tokens.shape, BF16),
        scratch_shapes=[pltpu.VMEM(tokens.shape, BF16), pltpu.SemaphoreType.DMA((copies,))],
        name="norm_copies",
    )(tokens, gain[None])


def emit_body(place_ref, maps_ref, init_ref, slope_ref, base_ref, gate_ref, out_ref):
    dim = init_ref.shape[0]
    place = place_ref[2]
    rows = lax.broadcasted_iota(jnp.int32, (dim, 2 * dim), 0)
    cols = lax.broadcasted_iota(jnp.int32, (dim, 2 * dim), 1)
    still = jnp.where(rows == cols, 1.0, 0.0).astype(F32)
    steps = [
        jnp.where(block < place, maps_ref[block].astype(F32), still)
        for block in range(maps_ref.shape[0] - 1)
    ]

    def after(later, earlier):
        both = mm(later[:, :dim], earlier)
        return jnp.concatenate([both[:, :dim], both[:, dim:] + later[:, dim:]], axis=1)

    state = mm(steps[0][:, :dim], init_ref[...].T) + steps[0][:, dim:]
    steps = steps[1:]
    while steps:
        odd = len(steps) % 2
        if odd:
            state = mm(steps[0][:, :dim], state) + steps[0][:, dim:]
            steps = steps[1:]
        steps = [after(later, earlier) for earlier, later in zip(steps[0::2], steps[1::2])]
        if steps and not odd:
            state = mm(steps[0][:, :dim], state) + steps[0][:, dim:]
            steps = steps[1:]
    inner, outer, each, _ = out_ref.shape
    for part in range(outer):
        at = slice(part * inner * each, (part + 1) * inner * each)
        head_raw = mm(slope_ref[at, :], state) + base_ref[at, :]
        gated = head_raw * rms_scale(head_raw) * gate_ref[at, :]
        out_ref[:, part] = gated.astype(BF16).reshape(inner, each, dim)


def emit(place, maps, init, slope, base, gate, outer, inner):
    span, dim = slope.shape
    each = span // (outer * inner)
    return pl.pallas_call(
        emit_body,
        in_specs=[pl.BlockSpec(memory_space=pltpu.SMEM)] + [resident()] * 5,
        out_specs=resident(),
        out_shape=jax.ShapeDtypeStruct((inner, outer, each, dim), BF16),
        name="emit",
    )(place, near(maps), init, slope, base, gate)


def project_body(place_ref, gated_ref, *refs):
    *w_refs, out_ref = refs
    core = place_ref[0]
    row = place_ref[1]
    count = gated_ref.shape[0] // 2
    step = 2 * core - 1 + count
    rows = [row, row, row + step, row + step, row + 2, row + count - step + count,
            row + count - step + count, row + 2]
    cores = [core, 1 - core, core, 1 - core, core, 1 - core, core, 1 - core]
    left = [gated_ref[2 * lax.rem(at, count) + side] for at, side in zip(rows, cores)]
    total = jnp.dot(
        jnp.concatenate(left, axis=1),
        jnp.concatenate([ref[...] for ref in w_refs], axis=0),
        preferred_element_type=F32,
    )
    out_ref[...] = total.astype(BF16).reshape(out_ref.shape)


def project(place, gated, weights, parts, tile):
    heads, rows, dim = gated.shape
    width = weights[0].shape[1]
    return pl.pallas_call(
        project_body,
        grid=(width // tile,),
        in_specs=[pl.BlockSpec(memory_space=pltpu.SMEM), resident()] + [
            pl.BlockSpec((rows.shape[0], tile), lambda i: (0, i)) for rows in weights
        ],
        out_specs=pl.BlockSpec((parts, rows // parts, tile), lambda i: (0, 0, i)),
        out_shape=jax.ShapeDtypeStruct((parts, rows // parts, width), BF16),
        name="project",
    )(place, near(gated), *weights)


def join_body(parts_ref, tokens_ref, gain_ref, routes_ref, out_ref, *refs, halves):
    copies_refs, (normed_ref, sems) = refs[:halves], refs[halves:]
    rows, width = tokens_ref.shape
    copies = routes_ref.shape[0]
    each = rows // halves
    extra = [
        pltpu.make_async_copy(
            routes_ref.at[:, pl.ds(half * each, each), :],
            copies_refs[half].at[:, :, pl.ds(width, routes_ref.shape[2])],
            sems.at[half * (copies + 1) + copies],
        )
        for half in range(halves)
    ]
    for copy in extra:
        copy.start()
    total = parts_ref[0].astype(F32)
    for part in range(1, parts_ref.shape[0]):
        total = total + parts_ref[part].astype(F32)
    summed = total.astype(BF16)
    out_ref[...] = summed
    hidden = tokens_ref[...].astype(F32) + summed.astype(F32)
    normed_ref[...] = (hidden * rms_scale(hidden) * gain_ref[...]).astype(BF16)
    send_copies(
        [
            pltpu.make_async_copy(
                normed_ref.at[pl.ds(half * each, each), :],
                copies_refs[half].at[at, :, pl.ds(0, width)],
                sems.at[half * (copies + 1) + at],
            )
            for half in range(halves)
            for at in range(copies)
        ]
    )
    for copy in extra:
        copy.wait()


def join(parts, tokens, gain, routes, halves):
    copies, rows, extra = routes.shape
    width = tokens.shape[1]
    anywhere = pl.BlockSpec(memory_space=pl.ANY)
    shape = jax.ShapeDtypeStruct((copies, rows // halves, width + extra), BF16)
    return pl.pallas_call(
        functools.partial(join_body, halves=halves),
        in_specs=[resident(), resident(), resident(), anywhere],
        out_specs=[resident()] + [anywhere] * halves,
        out_shape=[jax.ShapeDtypeStruct(tokens.shape, BF16)] + [shape] * halves,
        scratch_shapes=[
            pltpu.VMEM(tokens.shape, BF16),
            pltpu.SemaphoreType.DMA((halves * (copies + 1),)),
        ],
        name="join",
    )(near(parts), tokens, gain[None], routes)


def experts_body(
    x_ref, gate_a_ref, up_a_ref, down_a_ref, gate_b_ref, up_b_ref, down_b_ref, out_ref,
    rows_ref, total_ref,
    *, tiles,
):
    step = pl.program_id(0)
    groups, each, width = out_ref.shape
    count = groups * each

    def tile(gate_ref, up_ref, down_ref):
        x = x_ref[:, :, :width].reshape(count, width)
        gate = jnp.dot(x, gate_ref[0], preferred_element_type=F32)
        up = jnp.dot(x, up_ref[0], preferred_element_type=F32)
        activated = (gate * jax.nn.sigmoid(gate) * up).astype(BF16)
        return jnp.dot(activated, down_ref[0], preferred_element_type=F32)

    def weight(which):
        extra = x_ref[:, :, width:].astype(F32).reshape(count, -1)
        first = 3 * which
        return (
            extra[:, first:first + 1]
            + extra[:, first + 1:first + 2]
            + extra[:, first + 2:first + 3]
        )

    for which, refs in enumerate(
        ((gate_a_ref, up_a_ref, down_a_ref), (gate_b_ref, up_b_ref, down_b_ref))
    ):
        for part in range(tiles):

            @pl.when(step == which * tiles + part)
            def _(refs=refs, which=which, part=part):
                rows = tile(*refs)
                if part > 0:
                    rows = rows_ref[...] + rows
                if part < tiles - 1:
                    rows_ref[...] = rows
                else:
                    scaled = rows.astype(BF16).astype(F32) * weight(which)
                    if which == 0:
                        total_ref[...] = scaled
                    else:
                        out_ref[...] = (total_ref[...] + scaled).astype(BF16).reshape(out_ref.shape)


def experts_of(x, first, second, tiles):
    groups, each, wide = x.shape
    rows = groups * each
    hidden_units, width = first[1].shape[1:]
    tile = hidden_units // tiles

    def specs(start):
        def at(i):
            return jnp.clip(i - start, 0, tiles - 1)

        return [
            pl.BlockSpec((1, width, tile), lambda i: (0, 0, at(i))),
            pl.BlockSpec((1, width, tile), lambda i: (0, 0, tiles + at(i))),
            pl.BlockSpec((1, tile, width), lambda i: (0, at(i), 0)),
        ]

    return pl.pallas_call(
        functools.partial(experts_body, tiles=tiles),
        grid=(2 * tiles,),
        in_specs=[resident()] + specs(0) + specs(tiles),
        out_specs=resident(),
        out_shape=jax.ShapeDtypeStruct((groups, each, width), BF16),
        scratch_shapes=[pltpu.VMEM((rows, width), F32), pltpu.VMEM((rows, width), F32)],
        name="experts",
    )(near(x), first[0], first[0], first[1], second[0], second[0], second[1])


def total_body(*refs):
    *parts_refs, out_ref = refs
    each = parts_refs[0].shape[1]
    for half, parts_ref in enumerate(parts_refs):
        total = parts_ref[0].astype(F32)
        for part in range(1, parts_ref.shape[0]):
            total = total + parts_ref[part].astype(F32)
        out_ref[half * each:(half + 1) * each, :] = total.astype(BF16)


def total_of(halves):
    copies, each, width = halves[0].shape
    return pl.pallas_call(
        total_body,
        in_specs=[resident()] * len(halves),
        out_shape=jax.ShapeDtypeStruct((len(halves) * each, width), BF16),
        name="total",
    )(*[near(parts) for parts in halves])


def send_y(value):
    count = lax.axis_size("y")
    up = [(2 * at, 2 * ((at + 1) % count)) for at in range(count)]
    down = [(2 * at + 1, 2 * ((at + count - 1) % count) + 1) for at in range(count)]
    return lax.ppermute(value, ("y", "core"), up + down)


def near(value):
    return pltpu.with_memory_space_constraint(value, pltpu.VMEM)


def swap_cores(value):
    return lax.ppermute(value, "core", [(0, 1), (1, 0)])


def exchange(value, axes):
    return lax.all_to_all(value, axes, split_axis=0, concat_axis=0, tiled=True)


def shards(
    tokens,
    gain_in,
    w_heads,
    w_scalar,
    strength_bias,
    decay_rate,
    decay_bias,
    state_init,
    gain_head,
    w_output,
    gain_expert,
    expert_ids,
    gate_weights,
    w_gate_up,
    w_down,
):
    tok_dev, width = tokens.shape
    dim = state_init.shape[-1]
    x_count, y_count, core_count = (lax.axis_size(axis) for axis in ("x", "y", "core"))
    ctx_count = lax.axis_size("ctx")
    chips = x_count * y_count
    expert_total = chips * core_count
    core = lax.axis_index("core").astype(jnp.int32)
    place = lax.axis_index("ctx").astype(jnp.int32)

    copies = norm_copies(tokens, gain_in, chips)
    mine = exchange(copies, ("x", "y"))
    pair = jnp.concatenate([w_output, swap_cores(w_output)], axis=0)
    scalars = jnp.concatenate([strength_bias, decay_rate, decay_bias])
    w_logit = jnp.pad(w_scalar, ((0, 0), (0, LANES - w_scalar.shape[1])))
    spots = jnp.stack([core, lax.axis_index("y").astype(jnp.int32), place])
    mine, pair, scalars, w_logit, spots = lax.optimization_barrier(
        (mine, pair, scalars, w_logit, spots)
    )
    theirs = swap_cores(mine)
    beside = send_y(pair)

    *parts, maps = block_maps(spots, scalars, mine, theirs, w_heads, w_logit, dim, ctx_count, PER_STEP)
    beside, maps, far_gate_up, far_down = lax.optimization_barrier(
        (beside, maps, w_gate_up, w_down)
    )
    across = send_y(beside[:dim])
    all_maps = exchange(maps, "ctx")
    slope, base, gate = block_reads(spots, mine, theirs, w_heads, gain_head, parts, dim, PER_STEP)
    across, slope = lax.optimization_barrier((across, slope))
    w_rows = [pair, beside, across, swap_cores(beside), swap_cores(across)]
    gated = emit(
        spots, all_maps, state_init[0], slope, base, gate, x_count, y_count * core_count
    )
    heads = y_count * core_count
    gated = exchange(gated, ("y", "core")).reshape(heads, x_count * tok_dev, dim)
    partial = project(spots, gated, w_rows, x_count, 512)

    other_gate_up = swap_cores(far_gate_up)
    other_down = swap_cores(far_down)
    numbers = jnp.arange(expert_total, dtype=jnp.int32)
    named = expert_ids[:, :, None] == numbers[None, None, :]
    routes = jnp.sum(jnp.where(named, gate_weights[:, :, None], 0.0), axis=1)
    routes = routes.reshape(tok_dev, chips, core_count).transpose(1, 0, 2)
    routes = jnp.where(core == 0, routes, routes[:, :, ::-1])
    routes = jnp.stack(pieces(routes), axis=-1).reshape(chips, tok_dev, -1)
    routes = jnp.pad(routes, ((0, 0), (0, 0), (0, LANES - routes.shape[-1])))

    summed, *copies = join(exchange(partial, "x"), tokens, gain_expert, routes, HALVES)
    returned = []
    for part in copies:
        received = exchange(part, ("x", "y"))
        outputs = experts_of(received, (w_gate_up, w_down), (other_gate_up, other_down), 2)
        returned.append(exchange(outputs, ("x", "y")))
    expert_out = total_of(returned)
    return (summed, expert_out)


PER_STEP = 4
HALVES = 2


def solution(mesh):
    fine = Mesh(mesh.devices.reshape(mesh.shape["ctx"], 4, 4, 2), ("ctx", "x", "y", "core"))
    exp = ("x", "y", "core")
    rows = ("ctx", "x", "y", "core")
    return jax.shard_map(
        shards,
        mesh=fine,
        in_specs=(
            P(rows, None),
            P(),
            P(None, exp),
            P(None, exp),
            P(exp),
            P(exp),
            P(exp),
            P(exp, None, None),
            P(),
            P(exp, None),
            P(),
            P(rows, None),
            P(rows, None),
            P(exp, None, None),
            P(exp, None, None),
        ),
        out_specs=(P(rows, None), P(rows, None)),
        check_vma=False,
    )
```

```python
import functools
import jax
import jax.numpy as jnp
from jax import lax
from jax.experimental import pallas as pl
from jax.experimental.pallas import tpu as pltpu
from jax.sharding import Mesh, PartitionSpec as P

EPSILON = 1e-06
F32 = jnp.float32
BF16 = jnp.bfloat16
CHUNK = 128
LANES = 128


def mm(a, b):
    return jnp.dot(a.astype(BF16), b.astype(BF16), preferred_element_type=F32)


def pieces(a):
    high = a.astype(BF16)
    rest = a - high.astype(F32)
    middle = rest.astype(BF16)
    low = (rest - middle.astype(F32)).astype(BF16)
    return high, middle, low


def rms_scale(values):
    return lax.rsqrt(jnp.mean(values * values, axis=-1, keepdims=True) + EPSILON)


def chunk_of(n):
    return slice(n * CHUNK, (n + 1) * CHUNK)


def room(mebibytes):
    return pltpu.CompilerParams(vmem_limit_bytes=mebibytes * 1024 * 1024)


def resident():
    return pl.BlockSpec(memory_space=pltpu.VMEM)


def whole(shape):
    return pl.BlockSpec(shape, lambda i: (0,) * len(shape))


def project_rows(core, mine, theirs, w):
    groups, each, width = mine.shape
    ours = jnp.dot(mine.reshape(groups * each, width), w, preferred_element_type=F32)
    others = jnp.dot(theirs.reshape(groups * each, width), w, preferred_element_type=F32)
    even = jnp.where(core == 0, ours, others)
    odd = jnp.where(core == 0, others, ours)
    rows = []
    for group in range(groups):
        at = slice(group * each, (group + 1) * each)
        rows += [even[at], odd[at]]
    return rows


def maps_body(
    core_ref, scal_ref, mine_ref, theirs_ref, w_ref, ws_ref,
    key_ref, decay_ref, growth_ref, solved_ref, start_ref, maps_ref,
    mine_buf, theirs_buf, w_buf, ws_buf, sems,
    *, parts,
):
    dim = maps_ref.shape[1]
    groups = mine_ref.shape[0] // parts
    w_copies = [
        pltpu.make_async_copy(w_ref.at[:, pl.ds(dim, 2 * dim)], w_buf, sems.at[0]),
        pltpu.make_async_copy(ws_ref, ws_buf, sems.at[1]),
    ]
    x_copies = []
    for part in range(parts):
        at = pl.ds(part * groups, groups)
        x_copies.append(
            [
                pltpu.make_async_copy(mine_ref.at[at], mine_buf.at[at], sems.at[2 + 2 * part]),
                pltpu.make_async_copy(theirs_ref.at[at], theirs_buf.at[at], sems.at[3 + 2 * part]),
            ]
        )
    for copy in w_copies + [copy for both in x_copies for copy in both]:
        copy.start()
    lift = scal_ref[0]
    rate = scal_ref[1]
    bias = scal_ref[2]
    rows = lax.broadcasted_iota(jnp.int32, (CHUNK, CHUNK), 0)
    cols = lax.broadcasted_iota(jnp.int32, (CHUNK, CHUNK), 1)
    differ = jnp.bitwise_xor(rows, cols)
    lower = rows >= cols
    strict = rows > cols
    lower_ones = jnp.where(lower, 1.0, 0.0).astype(BF16)
    eye = jnp.where(rows == cols, 1.0, 0.0).astype(F32)
    for copy in w_copies:
        copy.wait()
    w_all = jnp.concatenate([w_buf[...], ws_buf[...]], axis=1)
    rows_of = []
    for part in range(parts):
        for copy in x_copies[part]:
            copy.wait()
        at = slice(part * groups, (part + 1) * groups)
        rows_of += project_rows(core_ref[0], mine_buf[at], theirs_buf[at], w_all)
    projected = jnp.concatenate(rows_of, axis=0)
    logits = projected[:, 2 * dim:]
    every = range(projected.shape[0] // CHUNK)
    key_raw = [projected[chunk_of(n), :dim] for n in every]
    value = [projected[chunk_of(n), dim:2 * dim] for n in every]
    strength = [jax.nn.sigmoid(logits[chunk_of(n), 0:1] + lift) for n in every]
    beta = [jnp.broadcast_to(s, (CHUNK, dim)) for s in strength]
    sums = []
    for n in every:
        moved = logits[chunk_of(n), 1:2] + bias
        softplus = jnp.maximum(moved, 0.0) + jnp.log1p(jnp.exp(-jnp.abs(moved)))
        high, middle, low = pieces(jnp.broadcast_to(-rate * softplus, (CHUNK, CHUNK)))
        sums.append(
            jnp.dot(lower_ones, high, preferred_element_type=F32)
            + jnp.dot(lower_ones, middle, preferred_element_type=F32)
            + jnp.dot(lower_ones, low, preferred_element_type=F32)
        )
    sums_t = [s.T for s in sums]
    key_vec = [
        k * lax.rsqrt(jnp.sum(k * k, axis=-1, keepdims=True) + EPSILON) for k in key_raw
    ]
    key_t = [k.T for k in key_vec]
    growth = [jnp.exp(s) for s in sums]
    fall = [jnp.exp(s[CHUNK - 1:CHUNK, :]) for s in sums]
    decay = [
        jnp.where(lower, jnp.exp(jnp.minimum(s - t, 0.0)), 0.0) for s, t in zip(sums, sums_t)
    ]
    gram = [mm(k, t) for k, t in zip(key_vec, key_t)]
    below = [
        jnp.where(strict, gram[n] * decay[n] * beta[n], 0.0) for n in every
    ]
    inverse = [eye - jnp.where(differ < 2, b, 0.0) for b in below]
    width = 2
    while width < CHUNK:
        ring = (differ >= width) & (differ < 2 * width)
        corner = [jnp.where(ring, b, 0.0) for b in below]
        half = [mm(inverse[n], corner[n]) for n in every]
        inverse = [inverse[n] - mm(half[n], inverse[n]) for n in every]
        width *= 2
    solved = [
        mm(
            inverse[n],
            jnp.concatenate([value[n] * beta[n], key_vec[n] * (beta[n] * growth[n])], axis=1),
        ).astype(BF16)
        for n in every
    ]
    tails = [jnp.exp(t[:, CHUNK - 1:CHUNK] - t) for t in sums_t]
    drive = [mm(key_t[n] * tails[n], solved[n]) for n in every]
    for n in every:
        key_ref[n] = key_t[n].astype(BF16)
        decay_ref[n] = decay[n]
        growth_ref[n] = growth[n]
        solved_ref[n] = solved[n]
    wide_rows = lax.broadcasted_iota(jnp.int32, (dim, 2 * dim), 0)
    wide_cols = lax.broadcasted_iota(jnp.int32, (dim, 2 * dim), 1)
    carried = jnp.where(wide_rows == wide_cols, 1.0, 0.0).astype(F32)
    for n in every:
        start_ref[n] = carried.astype(BF16)
        falls = jnp.concatenate([fall[n], fall[n]], axis=1)
        moved = falls * carried - mm(drive[n][:, dim:], carried)
        carried = jnp.concatenate([moved[:, :dim], moved[:, dim:] + drive[n][:, :dim]], axis=1)
    maps_ref[...] = jnp.broadcast_to(carried.astype(BF16)[None], maps_ref.shape)


def block_maps(core, scalars, mine, theirs, w, ws, dim, copies, parts):
    groups, each, width = mine.shape
    count = 2 * groups * each // CHUNK
    scalar = pl.BlockSpec(memory_space=pltpu.SMEM)
    anywhere = pl.BlockSpec(memory_space=pl.ANY)
    return pl.pallas_call(
        functools.partial(maps_body, parts=parts),
        in_specs=[scalar, scalar] + [anywhere] * 4,
        out_shape=[
            jax.ShapeDtypeStruct((count, dim, CHUNK), BF16),
            jax.ShapeDtypeStruct((count, CHUNK, CHUNK), F32),
            jax.ShapeDtypeStruct((count, CHUNK, dim), F32),
            jax.ShapeDtypeStruct((count, CHUNK, 2 * dim), BF16),
            jax.ShapeDtypeStruct((count, dim, 2 * dim), BF16),
            jax.ShapeDtypeStruct((copies, dim, 2 * dim), BF16),
        ],
        scratch_shapes=[
            pltpu.VMEM(mine.shape, BF16),
            pltpu.VMEM(theirs.shape, BF16),
            pltpu.VMEM((width, 2 * dim), BF16),
            pltpu.VMEM(ws.shape, BF16),
            pltpu.SemaphoreType.DMA((2 + 2 * parts,)),
        ],
        name="block_maps",
    )(core, scalars, mine, theirs, w, ws)


def reads_body(
    core_ref, mine_ref, theirs_ref, wq_ref, wg_ref, gain_ref, key_ref, decay_ref, growth_ref, solved_ref, start_ref,
    slope_ref, base_ref, gate_ref,
    *, per_step,
):
    dim = wq_ref.shape[1]
    w_pair = jnp.concatenate([wq_ref[...], wg_ref[...]], axis=1)
    projected = jnp.concatenate(
        project_rows(core_ref[0], mine_ref[...], theirs_ref[...], w_pair), axis=0
    )
    every = range(per_step)
    query = [projected[chunk_of(n), :dim] for n in every]
    scores = [mm(query[n], key_ref[n]) * decay_ref[n] for n in every]
    mixed = [mm(scores[n], solved_ref[n]) for n in every]
    both = [mm(query[n] * growth_ref[n] - mixed[n][:, dim:], start_ref[n]) for n in every]
    for n in every:
        slope_ref[chunk_of(n), :] = both[n][:, :dim].astype(BF16)
        base_ref[chunk_of(n), :] = both[n][:, dim:] + mixed[n][:, :dim]
    gate = projected[:, dim:]
    gate_ref[...] = gate * jax.nn.sigmoid(gate) * gain_ref[...]


def block_reads(core, mine, theirs, w, gain, parts, dim, per_step):
    key_t, decay, growth, solved, starts = parts
    groups, each, width = mine.shape
    span = 2 * groups * each
    rows = per_step * CHUNK
    x_spec = pl.BlockSpec((rows // (2 * each), each, width), lambda i: (i, 0, 0))

    def stacked(size):
        return pl.BlockSpec((per_step, CHUNK, size), lambda i: (i, 0, 0))

    by_rows = pl.BlockSpec((rows, dim), lambda i: (i, 0))
    return pl.pallas_call(
        functools.partial(reads_body, per_step=per_step),
        grid=(span // rows,),
        in_specs=[
            pl.BlockSpec(memory_space=pltpu.SMEM),
            x_spec,
            x_spec,
            pl.BlockSpec((width, dim), lambda i: (0, 0)),
            pl.BlockSpec((width, dim), lambda i: (0, 3)),
            whole((1, dim)),
            stacked(CHUNK), stacked(CHUNK), stacked(dim), stacked(2 * dim), stacked(2 * dim),
        ],
        out_specs=[by_rows, by_rows, by_rows],
        out_shape=[
            jax.ShapeDtypeStruct((span, dim), BF16),
            jax.ShapeDtypeStruct((span, dim), F32),
            jax.ShapeDtypeStruct((span, dim), F32),
        ],
        name="block_reads",
    )(core, mine, theirs, w, w, gain[None], key_t, decay, growth, solved, starts)


def send_copies(copies):
    for copy in copies:
        copy.start()
    for copy in copies:
        copy.wait()


def norm_body(tokens_ref, gain_ref, out_ref, normed_ref, sems):
    wide = tokens_ref[...].astype(F32)
    normed_ref[...] = (wide * rms_scale(wide) * gain_ref[...]).astype(BF16)
    send_copies(
        [
            pltpu.make_async_copy(normed_ref, out_ref.at[at], sems.at[at])
            for at in range(out_ref.shape[0])
        ]
    )


def norm_copies(tokens, gain, copies):
    return pl.pallas_call(
        norm_body,
        out_specs=pl.BlockSpec(memory_space=pl.ANY),
        out_shape=jax.ShapeDtypeStruct((copies,) + tokens.shape, BF16),
        scratch_shapes=[pltpu.VMEM(tokens.shape, BF16), pltpu.SemaphoreType.DMA((copies,))],
        name="norm_copies",
    )(tokens, gain[None])


def emit_body(place_ref, maps_ref, init_ref, slope_ref, base_ref, gate_ref, out_ref):
    dim = init_ref.shape[0]
    place = place_ref[2]
    rows = lax.broadcasted_iota(jnp.int32, (dim, 2 * dim), 0)
    cols = lax.broadcasted_iota(jnp.int32, (dim, 2 * dim), 1)
    still = jnp.where(rows == cols, 1.0, 0.0).astype(F32)
    steps = [
        jnp.where(block < place, maps_ref[block].astype(F32), still)
        for block in range(maps_ref.shape[0] - 1)
    ]

    def after(later, earlier):
        both = mm(later[:, :dim], earlier)
        return jnp.concatenate([both[:, :dim], both[:, dim:] + later[:, dim:]], axis=1)

    state = mm(steps[0][:, :dim], init_ref[...].T) + steps[0][:, dim:]
    steps = steps[1:]
    while steps:
        odd = len(steps) % 2
        if odd:
            state = mm(steps[0][:, :dim], state) + steps[0][:, dim:]
            steps = steps[1:]
        steps = [after(later, earlier) for earlier, later in zip(steps[0::2], steps[1::2])]
        if steps and not odd:
            state = mm(steps[0][:, :dim], state) + steps[0][:, dim:]
            steps = steps[1:]
    inner, outer, each, _ = out_ref.shape
    for part in range(outer):
        at = slice(part * inner * each, (part + 1) * inner * each)
        head_raw = mm(slope_ref[at, :], state) + base_ref[at, :]
        gated = head_raw * rms_scale(head_raw) * gate_ref[at, :]
        out_ref[:, part] = gated.astype(BF16).reshape(inner, each, dim)


def emit(place, maps, init, slope, base, gate, outer, inner):
    span, dim = slope.shape
    each = span // (outer * inner)
    return pl.pallas_call(
        emit_body,
        in_specs=[pl.BlockSpec(memory_space=pltpu.SMEM)] + [resident()] * 5,
        out_specs=resident(),
        out_shape=jax.ShapeDtypeStruct((inner, outer, each, dim), BF16),
        name="emit",
    )(place, near(maps), init, slope, base, gate)


def project_body(place_ref, gated_ref, *refs):
    *w_refs, out_ref = refs
    core = place_ref[0]
    row = place_ref[1]
    count = gated_ref.shape[0] // 2
    step = 2 * core - 1 + count
    rows = [row, row, row + step, row + step, row + 2, row + count - step + count,
            row + count - step + count, row + 2]
    cores = [core, 1 - core, core, 1 - core, core, 1 - core, core, 1 - core]
    left = [gated_ref[2 * lax.rem(at, count) + side] for at, side in zip(rows, cores)]
    total = jnp.dot(
        jnp.concatenate(left, axis=1),
        jnp.concatenate([ref[...] for ref in w_refs], axis=0),
        preferred_element_type=F32,
    )
    out_ref[...] = total.astype(BF16).reshape(out_ref.shape)


def project(place, gated, weights, parts, tile):
    heads, rows, dim = gated.shape
    width = weights[0].shape[1]
    return pl.pallas_call(
        project_body,
        grid=(width // tile,),
        in_specs=[pl.BlockSpec(memory_space=pltpu.SMEM), resident()] + [
            pl.BlockSpec((rows.shape[0], tile), lambda i: (0, i)) for rows in weights
        ],
        out_specs=pl.BlockSpec((parts, rows // parts, tile), lambda i: (0, 0, i)),
        out_shape=jax.ShapeDtypeStruct((parts, rows // parts, width), BF16),
        name="project",
    )(place, near(gated), *weights)


def join_body(parts_ref, tokens_ref, gain_ref, _, out_ref, copies_ref, normed_ref, sems):
    width = tokens_ref.shape[1]
    total = parts_ref[0].astype(F32)
    for part in range(1, parts_ref.shape[0]):
        total = total + parts_ref[part].astype(F32)
    summed = total.astype(BF16)
    hidden = tokens_ref[...].astype(F32) + summed.astype(F32)
    normed_ref[...] = (hidden * rms_scale(hidden) * gain_ref[...]).astype(BF16)
    copies = [
        pltpu.make_async_copy(normed_ref, copies_ref.at[at, :, pl.ds(0, width)], sems.at[at])
        for at in range(copies_ref.shape[0])
    ]
    for copy in copies:
        copy.start()
    out_ref[...] = summed
    for copy in copies:
        copy.wait()


def join(parts, tokens, gain, payload):
    anywhere = pl.BlockSpec(memory_space=pl.ANY)
    return pl.pallas_call(
        join_body,
        in_specs=[resident(), resident(), resident(), anywhere],
        out_specs=[resident(), anywhere],
        out_shape=[
            jax.ShapeDtypeStruct(tokens.shape, BF16),
            jax.ShapeDtypeStruct(payload.shape, BF16),
        ],
        input_output_aliases={3: 1},
        scratch_shapes=[
            pltpu.VMEM(tokens.shape, BF16),
            pltpu.SemaphoreType.DMA((payload.shape[0],)),
        ],
        name="join",
    )(near(parts), tokens, gain[None], payload)


def experts_body(x_ref, up_a_ref, down_a_ref, up_b_ref, down_b_ref, out_ref, *, tiles):
    groups, each, width = out_ref.shape
    count = groups * each
    hidden_units = down_a_ref.shape[1]
    tile = hidden_units // tiles
    x = x_ref[:, :, :width].reshape(count, width)
    extra = x_ref[:, :, width:].astype(F32).reshape(count, -1)
    total = None
    for which, (up_ref, down_ref) in enumerate(((up_a_ref, down_a_ref), (up_b_ref, down_b_ref))):
        pre = jnp.dot(x, up_ref[0], preferred_element_type=F32)
        gate = pre[:, :hidden_units]
        activated = (gate * jax.nn.sigmoid(gate) * pre[:, hidden_units:]).astype(BF16)
        rows = jnp.dot(activated, down_ref[0], preferred_element_type=F32)
        first = 3 * which
        weight = (
            extra[:, first:first + 1]
            + extra[:, first + 1:first + 2]
            + extra[:, first + 2:first + 3]
        )
        scaled = rows.astype(BF16).astype(F32) * weight
        total = scaled if total is None else total + scaled
    out_ref[...] = total.astype(BF16).reshape(out_ref.shape)


def experts_of(x, first, second, tiles):
    groups, each, _ = x.shape
    width = first[1].shape[2]
    return pl.pallas_call(
        functools.partial(experts_body, tiles=tiles),
        in_specs=[resident()] * 5,
        out_shape=jax.ShapeDtypeStruct((groups, each, width), BF16),
        compiler_params=room(28),
        name="experts",
    )(near(x), *[near(part) for part in first + second])


def total_body(*refs):
    *parts_refs, out_ref = refs
    each = parts_refs[0].shape[1]
    for half, parts_ref in enumerate(parts_refs):
        total = parts_ref[0].astype(F32)
        for part in range(1, parts_ref.shape[0]):
            total = total + parts_ref[part].astype(F32)
        out_ref[half * each:(half + 1) * each, :] = total.astype(BF16)


def total_of(halves):
    copies, each, width = halves[0].shape
    return pl.pallas_call(
        total_body,
        in_specs=[resident()] * len(halves),
        out_shape=jax.ShapeDtypeStruct((len(halves) * each, width), BF16),
        name="total",
    )(*[near(parts) for parts in halves])


def send_y(value):
    count = lax.axis_size("y")
    up = [(2 * at, 2 * ((at + 1) % count)) for at in range(count)]
    down = [(2 * at + 1, 2 * ((at + count - 1) % count) + 1) for at in range(count)]
    return lax.ppermute(value, ("y", "core"), up + down)


def near(value):
    return pltpu.with_memory_space_constraint(value, pltpu.VMEM)


def swap_cores(value):
    return lax.ppermute(value, "core", [(0, 1), (1, 0)])


def exchange(value, axes):
    return lax.all_to_all(value, axes, split_axis=0, concat_axis=0, tiled=True)


def shards(
    tokens,
    gain_in,
    w_heads,
    w_scalar,
    strength_bias,
    decay_rate,
    decay_bias,
    state_init,
    gain_head,
    w_output,
    gain_expert,
    expert_ids,
    gate_weights,
    w_gate_up,
    w_down,
):
    tok_dev, width = tokens.shape
    dim = state_init.shape[-1]
    x_count, y_count, core_count = (lax.axis_size(axis) for axis in ("x", "y", "core"))
    ctx_count = lax.axis_size("ctx")
    chips = x_count * y_count
    expert_total = chips * core_count
    core = lax.axis_index("core").astype(jnp.int32)
    place = lax.axis_index("ctx").astype(jnp.int32)

    copies = norm_copies(tokens, gain_in, chips)
    mine = exchange(copies, ("x", "y"))
    pair = jnp.concatenate([w_output, swap_cores(w_output)], axis=0)
    scalars = jnp.concatenate([strength_bias, decay_rate, decay_bias])
    w_logit = jnp.pad(w_scalar, ((0, 0), (0, LANES - w_scalar.shape[1])))
    spots = jnp.stack([core, lax.axis_index("y").astype(jnp.int32), place])
    mine, pair, scalars, w_logit, spots = lax.optimization_barrier(
        (mine, pair, scalars, w_logit, spots)
    )
    theirs = swap_cores(mine)
    beside = send_y(pair)

    *parts, maps = block_maps(spots, scalars, mine, theirs, w_heads, w_logit, dim, ctx_count, 4)
    beside, maps = lax.optimization_barrier((beside, maps))
    across = send_y(beside[:dim])
    all_maps = exchange(maps, "ctx")
    slope, base, gate = block_reads(spots, mine, theirs, w_heads, gain_head, parts, dim, PER_STEP)
    across, slope = lax.optimization_barrier((across, slope))
    w_rows = [pair, beside, across, swap_cores(beside), swap_cores(across)]
    gated = emit(
        spots, all_maps, state_init[0], slope, base, gate, x_count, y_count * core_count
    )
    heads = y_count * core_count
    gated = exchange(gated, ("y", "core")).reshape(heads, x_count * tok_dev, dim)
    partial = project(spots, gated, w_rows, x_count, 1024)

    numbers = jnp.arange(expert_total, dtype=jnp.int32)
    named = expert_ids[:, :, None] == numbers[None, None, :]
    routes = jnp.sum(jnp.where(named, gate_weights[:, :, None], 0.0), axis=1)
    routes = routes.reshape(tok_dev, chips, core_count).transpose(1, 0, 2)
    routes = jnp.where(core == 0, routes, routes[:, :, ::-1])
    routes = jnp.stack(pieces(routes), axis=-1).reshape(chips, tok_dev, -1)
    payload = jnp.pad(routes, ((0, 0), (0, 0), (width, LANES - routes.shape[-1])))

    summed, copies = join(exchange(partial, "x"), tokens, gain_expert, payload)
    far_gate_up, far_down, summed = lax.optimization_barrier((w_gate_up, w_down, summed))
    swapped = (swap_cores(far_gate_up), swap_cores(far_down))
    received = exchange(copies, ("x", "y"))
    outputs = experts_of(received, (w_gate_up, w_down), swapped, 2)
    expert_out = total_of([exchange(outputs, ("x", "y"))])
    return (summed, expert_out)


PER_STEP = 4


def solution(mesh):
    fine = Mesh(mesh.devices.reshape(mesh.shape["ctx"], 4, 4, 2), ("ctx", "x", "y", "core"))
    exp = ("x", "y", "core")
    rows = ("ctx", "x", "y", "core")
    return jax.shard_map(
        shards,
        mesh=fine,
        in_specs=(
            P(rows, None),
            P(),
            P(None, exp),
            P(None, exp),
            P(exp),
            P(exp),
            P(exp),
            P(exp, None, None),
            P(),
            P(exp, None),
            P(),
            P(rows, None),
            P(rows, None),
            P(exp, None, None),
            P(exp, None, None),
        ),
        out_specs=(P(rows, None), P(rows, None)),
        check_vma=False,
    )
```

```python
import functools
import jax
import jax.numpy as jnp
from jax import lax
from jax.experimental import pallas as pl
from jax.experimental.pallas import tpu as pltpu
from jax.sharding import Mesh, PartitionSpec as P

EPSILON = 1e-06
F32 = jnp.float32
BF16 = jnp.bfloat16
CHUNK = 128
LANES = 128


def mm(a, b):
    return jnp.dot(a.astype(BF16), b.astype(BF16), preferred_element_type=F32)


def pieces(a):
    high = a.astype(BF16)
    rest = a - high.astype(F32)
    middle = rest.astype(BF16)
    low = (rest - middle.astype(F32)).astype(BF16)
    return high, middle, low


def rms_scale(values):
    return lax.rsqrt(jnp.mean(values * values, axis=-1, keepdims=True) + EPSILON)


def chunk_of(n):
    return slice(n * CHUNK, (n + 1) * CHUNK)


def room(mebibytes):
    return pltpu.CompilerParams(vmem_limit_bytes=mebibytes * 1024 * 1024)


def resident():
    return pl.BlockSpec(memory_space=pltpu.VMEM)


def whole(shape):
    return pl.BlockSpec(shape, lambda i: (0,) * len(shape))


def project_rows(core, mine, theirs, w):
    groups, each, width = mine.shape
    ours = jnp.dot(mine.reshape(groups * each, width), w, preferred_element_type=F32)
    others = jnp.dot(theirs.reshape(groups * each, width), w, preferred_element_type=F32)
    even = jnp.where(core == 0, ours, others)
    odd = jnp.where(core == 0, others, ours)
    rows = []
    for group in range(groups):
        at = slice(group * each, (group + 1) * each)
        rows += [even[at], odd[at]]
    return rows


def maps_body(
    core_ref, scal_ref, mine_ref, theirs_ref, w_ref, ws_ref,
    key_ref, decay_ref, growth_ref, solved_ref, start_ref, maps_ref,
    mine_buf, theirs_buf, w_buf, ws_buf, sems,
    *, parts,
):
    dim = maps_ref.shape[1]
    groups = mine_ref.shape[0] // parts
    w_copies = [
        pltpu.make_async_copy(w_ref.at[:, pl.ds(dim, 2 * dim)], w_buf, sems.at[0]),
        pltpu.make_async_copy(ws_ref, ws_buf, sems.at[1]),
    ]
    x_copies = []
    for part in range(parts):
        at = pl.ds(part * groups, groups)
        x_copies.append(
            [
                pltpu.make_async_copy(mine_ref.at[at], mine_buf.at[at], sems.at[2 + 2 * part]),
                pltpu.make_async_copy(theirs_ref.at[at], theirs_buf.at[at], sems.at[3 + 2 * part]),
            ]
        )
    for copy in w_copies + [copy for both in x_copies for copy in both]:
        copy.start()
    lift = scal_ref[0]
    rate = scal_ref[1]
    bias = scal_ref[2]
    rows = lax.broadcasted_iota(jnp.int32, (CHUNK, CHUNK), 0)
    cols = lax.broadcasted_iota(jnp.int32, (CHUNK, CHUNK), 1)
    differ = jnp.bitwise_xor(rows, cols)
    lower = rows >= cols
    strict = rows > cols
    lower_ones = jnp.where(lower, 1.0, 0.0).astype(BF16)
    eye = jnp.where(rows == cols, 1.0, 0.0).astype(F32)
    for copy in w_copies:
        copy.wait()
    w_all = jnp.concatenate([w_buf[...], ws_buf[...]], axis=1)
    rows_of = []
    for part in range(parts):
        for copy in x_copies[part]:
            copy.wait()
        at = slice(part * groups, (part + 1) * groups)
        rows_of += project_rows(core_ref[0], mine_buf[at], theirs_buf[at], w_all)
    projected = jnp.concatenate(rows_of, axis=0)
    logits = projected[:, 2 * dim:]
    every = range(projected.shape[0] // CHUNK)
    key_raw = [projected[chunk_of(n), :dim] for n in every]
    value = [projected[chunk_of(n), dim:2 * dim] for n in every]
    strength = [jax.nn.sigmoid(logits[chunk_of(n), 0:1] + lift) for n in every]
    beta = [jnp.broadcast_to(s, (CHUNK, dim)) for s in strength]
    sums = []
    for n in every:
        moved = logits[chunk_of(n), 1:2] + bias
        softplus = jnp.maximum(moved, 0.0) + jnp.log1p(jnp.exp(-jnp.abs(moved)))
        high, middle, low = pieces(jnp.broadcast_to(-rate * softplus, (CHUNK, CHUNK)))
        sums.append(
            jnp.dot(lower_ones, high, preferred_element_type=F32)
            + jnp.dot(lower_ones, middle, preferred_element_type=F32)
            + jnp.dot(lower_ones, low, preferred_element_type=F32)
        )
    sums_t = [s.T for s in sums]
    key_vec = [
        k * lax.rsqrt(jnp.sum(k * k, axis=-1, keepdims=True) + EPSILON) for k in key_raw
    ]
    key_t = [k.T for k in key_vec]
    growth = [jnp.exp(s) for s in sums]
    fall = [jnp.exp(s[CHUNK - 1:CHUNK, :]) for s in sums]
    decay = [
        jnp.where(lower, jnp.exp(jnp.minimum(s - t, 0.0)), 0.0) for s, t in zip(sums, sums_t)
    ]
    gram = [mm(k, t) for k, t in zip(key_vec, key_t)]
    below = [
        jnp.where(strict, gram[n] * decay[n] * beta[n], 0.0) for n in every
    ]
    inverse = [eye - jnp.where(differ < 2, b, 0.0) for b in below]
    width = 2
    while width < CHUNK:
        ring = (differ >= width) & (differ < 2 * width)
        corner = [jnp.where(ring, b, 0.0) for b in below]
        half = [mm(inverse[n], corner[n]) for n in every]
        inverse = [inverse[n] - mm(half[n], inverse[n]) for n in every]
        width *= 2
    solved = [
        mm(
            inverse[n],
            jnp.concatenate([value[n] * beta[n], key_vec[n] * (beta[n] * growth[n])], axis=1),
        ).astype(BF16)
        for n in every
    ]
    tails = [jnp.exp(t[:, CHUNK - 1:CHUNK] - t) for t in sums_t]
    drive = [mm(key_t[n] * tails[n], solved[n]) for n in every]
    for n in every:
        key_ref[n] = key_t[n].astype(BF16)
        decay_ref[n] = decay[n]
        growth_ref[n] = growth[n]
        solved_ref[n] = solved[n]
    wide_rows = lax.broadcasted_iota(jnp.int32, (dim, 2 * dim), 0)
    wide_cols = lax.broadcasted_iota(jnp.int32, (dim, 2 * dim), 1)
    carried = jnp.where(wide_rows == wide_cols, 1.0, 0.0).astype(F32)
    for n in every:
        start_ref[n] = carried.astype(BF16)
        falls = jnp.concatenate([fall[n], fall[n]], axis=1)
        moved = falls * carried - mm(drive[n][:, dim:], carried)
        carried = jnp.concatenate([moved[:, :dim], moved[:, dim:] + drive[n][:, :dim]], axis=1)
    maps_ref[...] = jnp.broadcast_to(carried.astype(BF16)[None], maps_ref.shape)


def block_maps(core, scalars, mine, theirs, w, ws, dim, copies, parts):
    groups, each, width = mine.shape
    count = 2 * groups * each // CHUNK
    scalar = pl.BlockSpec(memory_space=pltpu.SMEM)
    anywhere = pl.BlockSpec(memory_space=pl.ANY)
    return pl.pallas_call(
        functools.partial(maps_body, parts=parts),
        in_specs=[scalar, scalar] + [anywhere] * 4,
        out_shape=[
            jax.ShapeDtypeStruct((count, dim, CHUNK), BF16),
            jax.ShapeDtypeStruct((count, CHUNK, CHUNK), F32),
            jax.ShapeDtypeStruct((count, CHUNK, dim), F32),
            jax.ShapeDtypeStruct((count, CHUNK, 2 * dim), BF16),
            jax.ShapeDtypeStruct((count, dim, 2 * dim), BF16),
            jax.ShapeDtypeStruct((copies, dim, 2 * dim), BF16),
        ],
        scratch_shapes=[
            pltpu.VMEM(mine.shape, BF16),
            pltpu.VMEM(theirs.shape, BF16),
            pltpu.VMEM((width, 2 * dim), BF16),
            pltpu.VMEM(ws.shape, BF16),
            pltpu.SemaphoreType.DMA((2 + 2 * parts,)),
        ],
        name="block_maps",
    )(core, scalars, mine, theirs, w, ws)


def reads_body(
    core_ref, mine_ref, theirs_ref, wq_ref, wg_ref, gain_ref, key_ref, decay_ref, growth_ref, solved_ref, start_ref,
    slope_ref, base_ref, gate_ref,
    *, per_step,
):
    dim = wq_ref.shape[1]
    w_pair = jnp.concatenate([wq_ref[...], wg_ref[...]], axis=1)
    projected = jnp.concatenate(
        project_rows(core_ref[0], mine_ref[...], theirs_ref[...], w_pair), axis=0
    )
    every = range(per_step)
    query = [projected[chunk_of(n), :dim] for n in every]
    scores = [mm(query[n], key_ref[n]) * decay_ref[n] for n in every]
    mixed = [mm(scores[n], solved_ref[n]) for n in every]
    both = [mm(query[n] * growth_ref[n] - mixed[n][:, dim:], start_ref[n]) for n in every]
    for n in every:
        slope_ref[chunk_of(n), :] = both[n][:, :dim].astype(BF16)
        base_ref[chunk_of(n), :] = both[n][:, dim:] + mixed[n][:, :dim]
    gate = projected[:, dim:]
    gate_ref[...] = gate * jax.nn.sigmoid(gate) * gain_ref[...]


def block_reads(core, mine, theirs, w, gain, parts, dim, per_step):
    key_t, decay, growth, solved, starts = parts
    groups, each, width = mine.shape
    span = 2 * groups * each
    rows = per_step * CHUNK
    x_spec = pl.BlockSpec((rows // (2 * each), each, width), lambda i: (i, 0, 0))

    def stacked(size):
        return pl.BlockSpec((per_step, CHUNK, size), lambda i: (i, 0, 0))

    by_rows = pl.BlockSpec((rows, dim), lambda i: (i, 0))
    return pl.pallas_call(
        functools.partial(reads_body, per_step=per_step),
        grid=(span // rows,),
        in_specs=[
            pl.BlockSpec(memory_space=pltpu.SMEM),
            x_spec,
            x_spec,
            pl.BlockSpec((width, dim), lambda i: (0, 0)),
            pl.BlockSpec((width, dim), lambda i: (0, 3)),
            whole((1, dim)),
            stacked(CHUNK), stacked(CHUNK), stacked(dim), stacked(2 * dim), stacked(2 * dim),
        ],
        out_specs=[by_rows, by_rows, by_rows],
        out_shape=[
            jax.ShapeDtypeStruct((span, dim), BF16),
            jax.ShapeDtypeStruct((span, dim), F32),
            jax.ShapeDtypeStruct((span, dim), F32),
        ],
        name="block_reads",
    )(core, mine, theirs, w, w, gain[None], key_t, decay, growth, solved, starts)


def send_copies(copies):
    for copy in copies:
        copy.start()
    for copy in copies:
        copy.wait()


def norm_body(tokens_ref, gain_ref, out_ref, normed_ref, sems):
    wide = tokens_ref[...].astype(F32)
    normed_ref[...] = (wide * rms_scale(wide) * gain_ref[...]).astype(BF16)
    send_copies(
        [
            pltpu.make_async_copy(normed_ref, out_ref.at[at], sems.at[at])
            for at in range(out_ref.shape[0])
        ]
    )


def norm_copies(tokens, gain, copies):
    return pl.pallas_call(
        norm_body,
        out_specs=pl.BlockSpec(memory_space=pl.ANY),
        out_shape=jax.ShapeDtypeStruct((copies,) + tokens.shape, BF16),
        scratch_shapes=[pltpu.VMEM(tokens.shape, BF16), pltpu.SemaphoreType.DMA((copies,))],
        name="norm_copies",
    )(tokens, gain[None])


def emit_body(
    place_ref, maps_ref, init_ref, slope_ref, base_ref, gate_ref, out_ref,
    slope_buf, base_buf, gate_buf, sems,
):
    moves = [
        pltpu.make_async_copy(source, target, sems.at[at])
        for at, (source, target) in enumerate(
            ((slope_ref, slope_buf), (base_ref, base_buf), (gate_ref, gate_buf))
        )
    ]
    for move in moves:
        move.start()
    dim = init_ref.shape[0]
    place = place_ref[2]
    rows = lax.broadcasted_iota(jnp.int32, (dim, 2 * dim), 0)
    cols = lax.broadcasted_iota(jnp.int32, (dim, 2 * dim), 1)
    still = jnp.where(rows == cols, 1.0, 0.0).astype(F32)
    steps = [
        jnp.where(block < place, maps_ref[block].astype(F32), still)
        for block in range(maps_ref.shape[0] - 1)
    ]

    def after(later, earlier):
        both = mm(later[:, :dim], earlier)
        return jnp.concatenate([both[:, :dim], both[:, dim:] + later[:, dim:]], axis=1)

    state = mm(steps[0][:, :dim], init_ref[...].T) + steps[0][:, dim:]
    steps = steps[1:]
    while steps:
        odd = len(steps) % 2
        if odd:
            state = mm(steps[0][:, :dim], state) + steps[0][:, dim:]
            steps = steps[1:]
        steps = [after(later, earlier) for earlier, later in zip(steps[0::2], steps[1::2])]
        if steps and not odd:
            state = mm(steps[0][:, :dim], state) + steps[0][:, dim:]
            steps = steps[1:]
    for move in moves:
        move.wait()
    inner, outer, each, _ = out_ref.shape
    for part in range(outer):
        at = slice(part * inner * each, (part + 1) * inner * each)
        head_raw = mm(slope_buf[at, :], state) + base_buf[at, :]
        gated = head_raw * rms_scale(head_raw) * gate_buf[at, :]
        out_ref[:, part] = gated.astype(BF16).reshape(inner, each, dim)


def emit(place, maps, init, slope, base, gate, outer, inner):
    span, dim = slope.shape
    each = span // (outer * inner)
    return pl.pallas_call(
        emit_body,
        in_specs=[pl.BlockSpec(memory_space=pltpu.SMEM)]
        + [resident()] * 2
        + [pl.BlockSpec(memory_space=pl.ANY)] * 3,
        out_specs=resident(),
        out_shape=jax.ShapeDtypeStruct((inner, outer, each, dim), BF16),
        scratch_shapes=[
            pltpu.VMEM(slope.shape, slope.dtype),
            pltpu.VMEM(base.shape, base.dtype),
            pltpu.VMEM(gate.shape, gate.dtype),
            pltpu.SemaphoreType.DMA((3,)),
        ],
        name="emit",
    )(place, near(maps), init, slope, base, gate)


def project_body(place_ref, gated_ref, *refs, tiles):
    *w_refs, out_ref, w_buf, sems = refs
    heads, rows, dim = gated_ref.shape
    width = out_ref.shape[-1]
    tile = width // tiles
    moves = []
    for part in range(tiles):
        cols = pl.ds(part * tile, tile)
        moves.append(
            [
                pltpu.make_async_copy(
                    w_ref.at[:, cols],
                    w_buf.at[pl.ds(at * dim, dim), cols],
                    sems.at[part * heads + at],
                )
                for at, w_ref in enumerate(w_refs)
            ]
        )
    for move in [move for group in moves for move in group]:
        move.start()
    core = place_ref[0]
    row = place_ref[1]
    count = heads // 2
    step = 2 * core - 1 + count
    back = row + 2 * count - step
    spots = [row, row, row + step, row + step, row + 2, back, back, row + 2]
    sides = [core, 1 - core, core, 1 - core, core, 1 - core, core, 1 - core]
    left = jnp.concatenate(
        [gated_ref[2 * lax.rem(at, count) + side] for at, side in zip(spots, sides)], axis=1
    )
    for part in range(tiles):
        for move in moves[part]:
            move.wait()
        cols = slice(part * tile, (part + 1) * tile)
        total = jnp.dot(left, w_buf[:, cols], preferred_element_type=F32)
        out_ref[:, :, cols] = total.astype(BF16).reshape(out_ref.shape[:2] + (tile,))


def project(place, gated, weights, parts, tiles):
    heads, rows, dim = gated.shape
    width = weights[0].shape[1]
    return pl.pallas_call(
        functools.partial(project_body, tiles=tiles),
        in_specs=[pl.BlockSpec(memory_space=pltpu.SMEM), resident()]
        + [pl.BlockSpec(memory_space=pl.ANY)] * heads,
        out_specs=resident(),
        out_shape=jax.ShapeDtypeStruct((parts, rows // parts, width), BF16),
        scratch_shapes=[
            pltpu.VMEM((heads * dim, width), BF16),
            pltpu.SemaphoreType.DMA((tiles * heads,)),
        ],
        name="project",
    )(place, near(gated), *weights)


def join_body(parts_ref, tokens_ref, gain_ref, _, out_ref, copies_ref, normed_ref, sems):
    width = tokens_ref.shape[1]
    total = parts_ref[0].astype(F32)
    for part in range(1, parts_ref.shape[0]):
        total = total + parts_ref[part].astype(F32)
    summed = total.astype(BF16)
    hidden = tokens_ref[...].astype(F32) + summed.astype(F32)
    normed_ref[...] = (hidden * rms_scale(hidden) * gain_ref[...]).astype(BF16)
    copies = [
        pltpu.make_async_copy(normed_ref, copies_ref.at[at, :, pl.ds(0, width)], sems.at[at])
        for at in range(copies_ref.shape[0])
    ]
    for copy in copies:
        copy.start()
    out_ref[...] = summed
    for copy in copies:
        copy.wait()


def join(parts, tokens, gain, payload):
    anywhere = pl.BlockSpec(memory_space=pl.ANY)
    return pl.pallas_call(
        join_body,
        in_specs=[resident(), resident(), resident(), anywhere],
        out_specs=[resident(), anywhere],
        out_shape=[
            jax.ShapeDtypeStruct(tokens.shape, BF16),
            jax.ShapeDtypeStruct(payload.shape, BF16),
        ],
        input_output_aliases={3: 1},
        scratch_shapes=[
            pltpu.VMEM(tokens.shape, BF16),
            pltpu.SemaphoreType.DMA((payload.shape[0],)),
        ],
        name="join",
    )(near(parts), near(tokens), gain[None], payload)


def experts_body(x_ref, up_a_ref, down_a_ref, up_b_ref, down_b_ref, out_ref, *, tiles):
    groups, each, width = out_ref.shape
    count = groups * each
    hidden_units = down_a_ref.shape[1]
    tile = hidden_units // tiles
    x = x_ref[:, :, :width].reshape(count, width)
    extra = x_ref[:, :, width:].astype(F32).reshape(count, -1)
    total = None
    for which, (up_ref, down_ref) in enumerate(((up_a_ref, down_a_ref), (up_b_ref, down_b_ref))):
        pre = jnp.dot(x, up_ref[0], preferred_element_type=F32)
        gate = pre[:, :hidden_units]
        activated = (gate * jax.nn.sigmoid(gate) * pre[:, hidden_units:]).astype(BF16)
        rows = jnp.dot(activated, down_ref[0], preferred_element_type=F32)
        first = 3 * which
        weight = (
            extra[:, first:first + 1]
            + extra[:, first + 1:first + 2]
            + extra[:, first + 2:first + 3]
        )
        scaled = rows.astype(BF16).astype(F32) * weight
        total = scaled if total is None else total + scaled
    out_ref[...] = total.astype(BF16).reshape(out_ref.shape)


def experts_of(x, first, second, tiles):
    groups, each, _ = x.shape
    width = first[1].shape[2]
    return pl.pallas_call(
        functools.partial(experts_body, tiles=tiles),
        in_specs=[resident()] * 5,
        out_shape=jax.ShapeDtypeStruct((groups, each, width), BF16),
        compiler_params=room(28),
        name="experts",
    )(near(x), *[near(part) for part in first + second])


def total_body(*refs):
    *parts_refs, out_ref = refs
    each = parts_refs[0].shape[1]
    for half, parts_ref in enumerate(parts_refs):
        total = parts_ref[0].astype(F32)
        for part in range(1, parts_ref.shape[0]):
            total = total + parts_ref[part].astype(F32)
        out_ref[half * each:(half + 1) * each, :] = total.astype(BF16)


def total_of(halves):
    copies, each, width = halves[0].shape
    return pl.pallas_call(
        total_body,
        in_specs=[resident()] * len(halves),
        out_shape=jax.ShapeDtypeStruct((len(halves) * each, width), BF16),
        name="total",
    )(*[near(parts) for parts in halves])


def send_y(value):
    count = lax.axis_size("y")
    up = [(2 * at, 2 * ((at + 1) % count)) for at in range(count)]
    down = [(2 * at + 1, 2 * ((at + count - 1) % count) + 1) for at in range(count)]
    return lax.ppermute(value, ("y", "core"), up + down)


def near(value):
    return pltpu.with_memory_space_constraint(value, pltpu.VMEM)


def swap_cores(value):
    return lax.ppermute(value, "core", [(0, 1), (1, 0)])


def exchange(value, axes):
    return lax.all_to_all(value, axes, split_axis=0, concat_axis=0, tiled=True)


def shards(
    tokens,
    gain_in,
    w_heads,
    w_scalar,
    strength_bias,
    decay_rate,
    decay_bias,
    state_init,
    gain_head,
    w_output,
    gain_expert,
    expert_ids,
    gate_weights,
    w_gate_up,
    w_down,
):
    tok_dev, width = tokens.shape
    dim = state_init.shape[-1]
    x_count, y_count, core_count = (lax.axis_size(axis) for axis in ("x", "y", "core"))
    ctx_count = lax.axis_size("ctx")
    chips = x_count * y_count
    expert_total = chips * core_count
    core = lax.axis_index("core").astype(jnp.int32)
    place = lax.axis_index("ctx").astype(jnp.int32)

    copies = norm_copies(tokens, gain_in, chips)
    mine = exchange(copies, ("x", "y"))
    w_pair = (w_output, swap_cores(w_output))
    scalars = jnp.concatenate([strength_bias, decay_rate, decay_bias])
    w_logit = jnp.pad(w_scalar, ((0, 0), (0, LANES - w_scalar.shape[1])))
    spots = jnp.stack([core, lax.axis_index("y").astype(jnp.int32), place])
    numbers = jnp.arange(expert_total, dtype=jnp.int32)
    named = expert_ids[:, :, None] == numbers[None, None, :]
    routes = jnp.sum(jnp.where(named, gate_weights[:, :, None], 0.0), axis=1)
    routes = routes.reshape(tok_dev, chips, core_count).transpose(1, 0, 2)
    routes = jnp.where(core == 0, routes, routes[:, :, ::-1])
    routes = jnp.stack(pieces(routes), axis=-1).reshape(chips, tok_dev, -1)
    payload = jnp.pad(routes, ((0, 0), (0, 0), (width, LANES - routes.shape[-1])))

    mine, w_pair, scalars, w_logit, spots, payload = lax.optimization_barrier(
        (mine, w_pair, scalars, w_logit, spots, payload)
    )
    theirs = swap_cores(mine)
    beside = tuple(send_y(rows) for rows in w_pair)

    *parts, maps = block_maps(spots, scalars, mine, theirs, w_heads, w_logit, dim, ctx_count, 4)
    beside, maps = lax.optimization_barrier((beside, maps))
    across = send_y(beside[0])
    all_maps = exchange(maps, "ctx")
    slope, base, gate = block_reads(spots, mine, theirs, w_heads, gain_head, parts, dim, PER_STEP)
    across, slope = lax.optimization_barrier((across, slope))
    w_rows = [*w_pair, *beside, across, *[swap_cores(rows) for rows in (*beside, across)]]
    gated = emit(
        spots, all_maps, state_init[0], slope, base, gate, x_count, y_count * core_count
    )
    heads = y_count * core_count
    gated = exchange(gated, ("y", "core")).reshape(heads, x_count * tok_dev, dim)
    partial = project(spots, gated, w_rows, x_count, 4)

    summed, copies = join(exchange(partial, "x"), tokens, gain_expert, payload)
    far_gate_up, far_down, summed = lax.optimization_barrier((w_gate_up, w_down, summed))
    swapped = (swap_cores(far_gate_up), swap_cores(far_down))
    received = exchange(copies, ("x", "y"))
    outputs = experts_of(received, (w_gate_up, w_down), swapped, 2)
    expert_out = total_of([exchange(outputs, ("x", "y"))])
    return (summed, expert_out)


PER_STEP = 4


def solution(mesh):
    fine = Mesh(mesh.devices.reshape(mesh.shape["ctx"], 4, 4, 2), ("ctx", "x", "y", "core"))
    exp = ("x", "y", "core")
    rows = ("ctx", "x", "y", "core")
    return jax.shard_map(
        shards,
        mesh=fine,
        in_specs=(
            P(rows, None),
            P(),
            P(None, exp),
            P(None, exp),
            P(exp),
            P(exp),
            P(exp),
            P(exp, None, None),
            P(),
            P(exp, None),
            P(),
            P(rows, None),
            P(rows, None),
            P(exp, None, None),
            P(exp, None, None),
        ),
        out_specs=(P(rows, None), P(rows, None)),
        check_vma=False,
    )
```

```python
import functools
import jax
import jax.numpy as jnp
from jax import lax
from jax.experimental import pallas as pl
from jax.experimental.pallas import tpu as pltpu
from jax.sharding import Mesh, PartitionSpec as P

EPSILON = 1e-06
F32 = jnp.float32
BF16 = jnp.bfloat16
CHUNK = 128
LANES = 128


def mm(a, b):
    return jnp.dot(a.astype(BF16), b.astype(BF16), preferred_element_type=F32)


def pieces(a):
    high = a.astype(BF16)
    rest = a - high.astype(F32)
    middle = rest.astype(BF16)
    low = (rest - middle.astype(F32)).astype(BF16)
    return high, middle, low


def rms_scale(values):
    return lax.rsqrt(jnp.mean(values * values, axis=-1, keepdims=True) + EPSILON)


def chunk_of(n):
    return slice(n * CHUNK, (n + 1) * CHUNK)


def room(mebibytes):
    return pltpu.CompilerParams(vmem_limit_bytes=mebibytes * 1024 * 1024)


def resident():
    return pl.BlockSpec(memory_space=pltpu.VMEM)


def whole(shape):
    return pl.BlockSpec(shape, lambda i: (0,) * len(shape))


def project_rows(core, mine, theirs, w):
    groups, each, width = mine.shape
    ours = jnp.dot(mine.reshape(groups * each, width), w, preferred_element_type=F32)
    others = jnp.dot(theirs.reshape(groups * each, width), w, preferred_element_type=F32)
    even = jnp.where(core == 0, ours, others)
    odd = jnp.where(core == 0, others, ours)
    rows = []
    for group in range(groups):
        at = slice(group * each, (group + 1) * each)
        rows += [even[at], odd[at]]
    return rows


def maps_body(
    core_ref, scal_ref, mine_ref, theirs_ref, w_ref, ws_ref,
    key_ref, decay_ref, growth_ref, solved_ref, start_ref, maps_ref,
    mine_buf, theirs_buf, w_buf, ws_buf, sems,
    *, parts,
):
    dim = maps_ref.shape[1]
    groups = mine_ref.shape[0] // parts
    w_copies = [
        pltpu.make_async_copy(w_ref.at[:, pl.ds(dim, 2 * dim)], w_buf, sems.at[0]),
        pltpu.make_async_copy(ws_ref, ws_buf, sems.at[1]),
    ]
    x_copies = []
    for part in range(parts):
        at = pl.ds(part * groups, groups)
        x_copies.append(
            [
                pltpu.make_async_copy(mine_ref.at[at], mine_buf.at[at], sems.at[2 + 2 * part]),
                pltpu.make_async_copy(theirs_ref.at[at], theirs_buf.at[at], sems.at[3 + 2 * part]),
            ]
        )
    for copy in w_copies + [copy for both in x_copies for copy in both]:
        copy.start()
    lift = scal_ref[0]
    rate = scal_ref[1]
    bias = scal_ref[2]
    rows = lax.broadcasted_iota(jnp.int32, (CHUNK, CHUNK), 0)
    cols = lax.broadcasted_iota(jnp.int32, (CHUNK, CHUNK), 1)
    differ = jnp.bitwise_xor(rows, cols)
    lower = rows >= cols
    strict = rows > cols
    lower_ones = jnp.where(lower, 1.0, 0.0).astype(BF16)
    eye = jnp.where(rows == cols, 1.0, 0.0).astype(F32)
    for copy in w_copies:
        copy.wait()
    w_all = jnp.concatenate([w_buf[...], ws_buf[...]], axis=1)
    rows_of = []
    for part in range(parts):
        for copy in x_copies[part]:
            copy.wait()
        at = slice(part * groups, (part + 1) * groups)
        rows_of += project_rows(core_ref[0], mine_buf[at], theirs_buf[at], w_all)
    projected = jnp.concatenate(rows_of, axis=0)
    logits = projected[:, 2 * dim:]
    every = range(projected.shape[0] // CHUNK)
    key_raw = [projected[chunk_of(n), :dim] for n in every]
    value = [projected[chunk_of(n), dim:2 * dim] for n in every]
    strength = [jax.nn.sigmoid(logits[chunk_of(n), 0:1] + lift) for n in every]
    beta = [jnp.broadcast_to(s, (CHUNK, dim)) for s in strength]
    sums = []
    for n in every:
        moved = logits[chunk_of(n), 1:2] + bias
        softplus = jnp.maximum(moved, 0.0) + jnp.log1p(jnp.exp(-jnp.abs(moved)))
        high, middle, low = pieces(jnp.broadcast_to(-rate * softplus, (CHUNK, CHUNK)))
        sums.append(
            jnp.dot(lower_ones, high, preferred_element_type=F32)
            + jnp.dot(lower_ones, middle, preferred_element_type=F32)
            + jnp.dot(lower_ones, low, preferred_element_type=F32)
        )
    sums_t = [s.T for s in sums]
    key_vec = [
        k * lax.rsqrt(jnp.sum(k * k, axis=-1, keepdims=True) + EPSILON) for k in key_raw
    ]
    key_t = [k.T for k in key_vec]
    growth = [jnp.exp(s) for s in sums]
    fall = [jnp.exp(s[CHUNK - 1:CHUNK, :]) for s in sums]
    decay = [
        jnp.where(lower, jnp.exp(jnp.minimum(s - t, 0.0)), 0.0) for s, t in zip(sums, sums_t)
    ]
    gram = [mm(k, t) for k, t in zip(key_vec, key_t)]
    below = [
        jnp.where(strict, gram[n] * decay[n] * beta[n], 0.0) for n in every
    ]
    inverse = [eye - jnp.where(differ < 2, b, 0.0) for b in below]
    width = 2
    while width < CHUNK:
        ring = (differ >= width) & (differ < 2 * width)
        corner = [jnp.where(ring, b, 0.0) for b in below]
        half = [mm(inverse[n], corner[n]) for n in every]
        inverse = [inverse[n] - mm(half[n], inverse[n]) for n in every]
        width *= 2
    solved = [
        mm(
            inverse[n],
            jnp.concatenate([value[n] * beta[n], key_vec[n] * (beta[n] * growth[n])], axis=1),
        ).astype(BF16)
        for n in every
    ]
    tails = [jnp.exp(t[:, CHUNK - 1:CHUNK] - t) for t in sums_t]
    drive = [mm(key_t[n] * tails[n], solved[n]) for n in every]
    for n in every:
        key_ref[n] = key_t[n].astype(BF16)
        decay_ref[n] = decay[n]
        growth_ref[n] = growth[n]
        solved_ref[n] = solved[n]
    wide_rows = lax.broadcasted_iota(jnp.int32, (dim, 2 * dim), 0)
    wide_cols = lax.broadcasted_iota(jnp.int32, (dim, 2 * dim), 1)
    carried = jnp.where(wide_rows == wide_cols, 1.0, 0.0).astype(F32)
    for n in every:
        start_ref[n] = carried.astype(BF16)
        falls = jnp.concatenate([fall[n], fall[n]], axis=1)
        moved = falls * carried - mm(drive[n][:, dim:], carried)
        carried = jnp.concatenate([moved[:, :dim], moved[:, dim:] + drive[n][:, :dim]], axis=1)
    maps_ref[...] = jnp.broadcast_to(carried.astype(BF16)[None], maps_ref.shape)


def block_maps(core, scalars, mine, theirs, w, ws, dim, copies, parts):
    groups, each, width = mine.shape
    count = 2 * groups * each // CHUNK
    scalar = pl.BlockSpec(memory_space=pltpu.SMEM)
    anywhere = pl.BlockSpec(memory_space=pl.ANY)
    return pl.pallas_call(
        functools.partial(maps_body, parts=parts),
        in_specs=[scalar, scalar] + [anywhere] * 4,
        out_shape=[
            jax.ShapeDtypeStruct((count, dim, CHUNK), BF16),
            jax.ShapeDtypeStruct((count, CHUNK, CHUNK), F32),
            jax.ShapeDtypeStruct((count, CHUNK, dim), F32),
            jax.ShapeDtypeStruct((count, CHUNK, 2 * dim), BF16),
            jax.ShapeDtypeStruct((count, dim, 2 * dim), BF16),
            jax.ShapeDtypeStruct((copies, dim, 2 * dim), BF16),
        ],
        scratch_shapes=[
            pltpu.VMEM(mine.shape, BF16),
            pltpu.VMEM(theirs.shape, BF16),
            pltpu.VMEM((width, 2 * dim), BF16),
            pltpu.VMEM(ws.shape, BF16),
            pltpu.SemaphoreType.DMA((2 + 2 * parts,)),
        ],
        name="block_maps",
    )(core, scalars, mine, theirs, w, ws)


def reads_body(
    core_ref, mine_ref, theirs_ref, wq_ref, wg_ref, gain_ref, key_ref, decay_ref, growth_ref, solved_ref, start_ref,
    slope_ref, base_ref, gate_ref,
    *, per_step,
):
    dim = wq_ref.shape[1]
    w_pair = jnp.concatenate([wq_ref[...], wg_ref[...]], axis=1)
    projected = jnp.concatenate(
        project_rows(core_ref[0], mine_ref[...], theirs_ref[...], w_pair), axis=0
    )
    every = range(per_step)
    query = [projected[chunk_of(n), :dim] for n in every]
    scores = [mm(query[n], key_ref[n]) * decay_ref[n] for n in every]
    mixed = [mm(scores[n], solved_ref[n]) for n in every]
    both = [mm(query[n] * growth_ref[n] - mixed[n][:, dim:], start_ref[n]) for n in every]
    for n in every:
        slope_ref[chunk_of(n), :] = both[n][:, :dim].astype(BF16)
        base_ref[chunk_of(n), :] = both[n][:, dim:] + mixed[n][:, :dim]
    gate = projected[:, dim:]
    gate_ref[...] = gate * jax.nn.sigmoid(gate) * gain_ref[...]


def block_reads(core, mine, theirs, w, gain, parts, dim, per_step):
    key_t, decay, growth, solved, starts = parts
    groups, each, width = mine.shape
    span = 2 * groups * each
    rows = per_step * CHUNK
    x_spec = pl.BlockSpec((rows // (2 * each), each, width), lambda i: (i, 0, 0))

    def stacked(size):
        return pl.BlockSpec((per_step, CHUNK, size), lambda i: (i, 0, 0))

    by_rows = pl.BlockSpec((rows, dim), lambda i: (i, 0))
    return pl.pallas_call(
        functools.partial(reads_body, per_step=per_step),
        grid=(span // rows,),
        in_specs=[
            pl.BlockSpec(memory_space=pltpu.SMEM),
            x_spec,
            x_spec,
            pl.BlockSpec((width, dim), lambda i: (0, 0)),
            pl.BlockSpec((width, dim), lambda i: (0, 3)),
            whole((1, dim)),
            stacked(CHUNK), stacked(CHUNK), stacked(dim), stacked(2 * dim), stacked(2 * dim),
        ],
        out_specs=[by_rows, by_rows, by_rows],
        out_shape=[
            jax.ShapeDtypeStruct((span, dim), BF16),
            jax.ShapeDtypeStruct((span, dim), F32),
            jax.ShapeDtypeStruct((span, dim), F32),
        ],
        name="block_reads",
    )(core, mine, theirs, w, w, gain[None], key_t, decay, growth, solved, starts)


def send_copies(copies):
    for copy in copies:
        copy.start()
    for copy in copies:
        copy.wait()


def norm_body(tokens_ref, gain_ref, out_ref, normed_ref, sems):
    wide = tokens_ref[...].astype(F32)
    normed_ref[...] = (wide * rms_scale(wide) * gain_ref[...]).astype(BF16)
    send_copies(
        [
            pltpu.make_async_copy(normed_ref, out_ref.at[at], sems.at[at])
            for at in range(out_ref.shape[0])
        ]
    )


def norm_copies(tokens, gain, copies):
    return pl.pallas_call(
        norm_body,
        out_specs=pl.BlockSpec(memory_space=pl.ANY),
        out_shape=jax.ShapeDtypeStruct((copies,) + tokens.shape, BF16),
        scratch_shapes=[pltpu.VMEM(tokens.shape, BF16), pltpu.SemaphoreType.DMA((copies,))],
        name="norm_copies",
    )(tokens, gain[None])


def emit_body(place_ref, maps_ref, init_ref, slope_ref, base_ref, gate_ref, out_ref):
    dim = init_ref.shape[0]
    place = place_ref[2]
    rows = lax.broadcasted_iota(jnp.int32, (dim, 2 * dim), 0)
    cols = lax.broadcasted_iota(jnp.int32, (dim, 2 * dim), 1)
    still = jnp.where(rows == cols, 1.0, 0.0).astype(F32)
    steps = [
        jnp.where(block < place, maps_ref[block].astype(F32), still)
        for block in range(maps_ref.shape[0] - 1)
    ]

    def after(later, earlier):
        both = mm(later[:, :dim], earlier)
        return jnp.concatenate([both[:, :dim], both[:, dim:] + later[:, dim:]], axis=1)

    state = mm(steps[0][:, :dim], init_ref[...].T) + steps[0][:, dim:]
    steps = steps[1:]
    while steps:
        odd = len(steps) % 2
        if odd:
            state = mm(steps[0][:, :dim], state) + steps[0][:, dim:]
            steps = steps[1:]
        steps = [after(later, earlier) for earlier, later in zip(steps[0::2], steps[1::2])]
        if steps and not odd:
            state = mm(steps[0][:, :dim], state) + steps[0][:, dim:]
            steps = steps[1:]
    inner, outer, each, _ = out_ref.shape
    for part in range(outer):
        at = slice(part * inner * each, (part + 1) * inner * each)
        head_raw = mm(slope_ref[at, :], state) + base_ref[at, :]
        gated = head_raw * rms_scale(head_raw) * gate_ref[at, :]
        out_ref[:, part] = gated.astype(BF16).reshape(inner, each, dim)


def emit(place, maps, init, slope, base, gate, outer, inner):
    span, dim = slope.shape
    each = span // (outer * inner)
    return pl.pallas_call(
        emit_body,
        in_specs=[pl.BlockSpec(memory_space=pltpu.SMEM)] + [resident()] * 5,
        out_specs=resident(),
        out_shape=jax.ShapeDtypeStruct((inner, outer, each, dim), BF16),
        name="emit",
    )(place, near(maps), init, slope, base, gate)


def project_body(place_ref, gated_ref, *refs):
    *w_refs, out_ref = refs
    core = place_ref[0]
    row = place_ref[1]
    count = gated_ref.shape[0] // 2
    step = 2 * core - 1 + count
    rows = [row, row, row + step, row + step, row + 2, row + count - step + count,
            row + count - step + count, row + 2]
    cores = [core, 1 - core, core, 1 - core, core, 1 - core, core, 1 - core]
    left = [gated_ref[2 * lax.rem(at, count) + side] for at, side in zip(rows, cores)]
    total = jnp.dot(
        jnp.concatenate(left, axis=1),
        jnp.concatenate([ref[...] for ref in w_refs], axis=0),
        preferred_element_type=F32,
    )
    out_ref[...] = total.astype(BF16).reshape(out_ref.shape)


def project(place, gated, weights, parts, tile):
    heads, rows, dim = gated.shape
    width = weights[0].shape[1]
    return pl.pallas_call(
        project_body,
        grid=(width // tile,),
        in_specs=[pl.BlockSpec(memory_space=pltpu.SMEM), resident()] + [
            pl.BlockSpec((rows.shape[0], tile), lambda i: (0, i)) for rows in weights
        ],
        out_specs=pl.BlockSpec((parts, rows // parts, tile), lambda i: (0, 0, i)),
        out_shape=jax.ShapeDtypeStruct((parts, rows // parts, width), BF16),
        name="project",
    )(place, near(gated), *weights)


def join_body(parts_ref, tokens_ref, gain_ref, out_ref, copies_ref, normed_ref, sems):
    total = parts_ref[0].astype(F32)
    for part in range(1, parts_ref.shape[0]):
        total = total + parts_ref[part].astype(F32)
    summed = total.astype(BF16)
    hidden = tokens_ref[...].astype(F32) + summed.astype(F32)
    normed_ref[...] = (hidden * rms_scale(hidden) * gain_ref[...]).astype(BF16)
    copies = [
        pltpu.make_async_copy(normed_ref, copies_ref.at[at], sems.at[at])
        for at in range(copies_ref.shape[0])
    ]
    for copy in copies:
        copy.start()
    out_ref[...] = summed
    for copy in copies:
        copy.wait()


def join(parts, tokens, gain, copies):
    return pl.pallas_call(
        join_body,
        in_specs=[resident()] * 3,
        out_specs=[resident(), pl.BlockSpec(memory_space=pl.ANY)],
        out_shape=[
            jax.ShapeDtypeStruct(tokens.shape, BF16),
            jax.ShapeDtypeStruct((copies,) + tokens.shape, BF16),
        ],
        scratch_shapes=[pltpu.VMEM(tokens.shape, BF16), pltpu.SemaphoreType.DMA((copies,))],
        name="join",
    )(near(parts), near(tokens), gain[None])


def experts_body(
    place_ref, gates_ref, x_ref, up_a_ref, down_a_ref, up_b_ref, down_b_ref, out_ref,
    *, x_count,
):
    groups, each, width = out_ref.shape
    count = groups * each
    hidden_units = down_a_ref.shape[1]
    y_count = groups // x_count
    blocks = []
    for group in range(groups):
        by_x = lax.rem(place_ref[3] + x_count - group // y_count, x_count)
        by_y = lax.rem(place_ref[1] + y_count - group % y_count, y_count)
        blocks.append(gates_ref[by_y * x_count + by_x])
    gates = jnp.concatenate(blocks, axis=0)
    x = x_ref[...].reshape(count, width)
    total = None
    for which, (up_ref, down_ref) in enumerate(((up_a_ref, down_a_ref), (up_b_ref, down_b_ref))):
        pre = jnp.dot(x, up_ref[0], preferred_element_type=F32)
        gate = pre[:, :hidden_units]
        activated = (gate * jax.nn.sigmoid(gate) * pre[:, hidden_units:]).astype(BF16)
        rows = jnp.dot(activated, down_ref[0], preferred_element_type=F32)
        weight = gates[:, which:which + 1]
        scaled = rows.astype(BF16).astype(F32) * weight
        total = scaled if total is None else total + scaled
    out_ref[...] = total.astype(BF16).reshape(out_ref.shape)


def experts_of(place, gates, x, first, second, x_count):
    return pl.pallas_call(
        functools.partial(experts_body, x_count=x_count),
        in_specs=[pl.BlockSpec(memory_space=pltpu.SMEM)] + [resident()] * 6,
        out_shape=jax.ShapeDtypeStruct(x.shape, BF16),
        compiler_params=room(28),
        name="experts",
    )(place, gates, near(x), *[near(part) for part in first + second])


def total_body(*refs):
    *parts_refs, out_ref = refs
    each = parts_refs[0].shape[1]
    for half, parts_ref in enumerate(parts_refs):
        total = parts_ref[0].astype(F32)
        for part in range(1, parts_ref.shape[0]):
            total = total + parts_ref[part].astype(F32)
        out_ref[half * each:(half + 1) * each, :] = total.astype(BF16)


def total_of(halves):
    copies, each, width = halves[0].shape
    return pl.pallas_call(
        total_body,
        in_specs=[resident()] * len(halves),
        out_shape=jax.ShapeDtypeStruct((len(halves) * each, width), BF16),
        name="total",
    )(*[near(parts) for parts in halves])


def shift(value, axis, steps):
    count = lax.axis_size(axis)
    if steps == 0:
        return value
    return lax.ppermute(value, axis, [(at, (at + steps) % count) for at in range(count)])


def send_y(value):
    count = lax.axis_size("y")
    up = [(2 * at, 2 * ((at + 1) % count)) for at in range(count)]
    down = [(2 * at + 1, 2 * ((at + count - 1) % count) + 1) for at in range(count)]
    return lax.ppermute(value, ("y", "core"), up + down)


def near(value):
    return pltpu.with_memory_space_constraint(value, pltpu.VMEM)


def swap_cores(value):
    return lax.ppermute(value, "core", [(0, 1), (1, 0)])


def exchange(value, axes):
    return lax.all_to_all(value, axes, split_axis=0, concat_axis=0, tiled=True)


def shards(
    tokens,
    gain_in,
    w_heads,
    w_scalar,
    strength_bias,
    decay_rate,
    decay_bias,
    state_init,
    gain_head,
    w_output,
    gain_expert,
    expert_ids,
    gate_weights,
    w_gate_up,
    w_down,
):
    tok_dev, width = tokens.shape
    dim = state_init.shape[-1]
    x_count, y_count, core_count = (lax.axis_size(axis) for axis in ("x", "y", "core"))
    ctx_count = lax.axis_size("ctx")
    chips = x_count * y_count
    expert_total = chips * core_count
    core = lax.axis_index("core").astype(jnp.int32)
    place = lax.axis_index("ctx").astype(jnp.int32)

    copies = norm_copies(tokens, gain_in, chips)
    mine = exchange(copies, ("x", "y"))
    w_pair = (w_output, swap_cores(w_output))
    scalars = jnp.concatenate([strength_bias, decay_rate, decay_bias])
    w_logit = jnp.pad(w_scalar, ((0, 0), (0, LANES - w_scalar.shape[1])))
    row = lax.axis_index("y").astype(jnp.int32)
    spots = jnp.stack([core, row, place, lax.axis_index("x").astype(jnp.int32)])
    numbers = jnp.arange(expert_total, dtype=jnp.int32)
    named = expert_ids[:, :, None] == numbers[None, None, :]
    routes = jnp.sum(jnp.where(named, gate_weights[:, :, None], 0.0), axis=1)
    routes = jnp.concatenate([shift(routes, "x", by) for by in range(x_count)], axis=1)
    routes = jnp.stack([shift(routes, "y", by) for by in range(y_count)])
    routes = routes.reshape(y_count, tok_dev, x_count, expert_total).transpose(0, 2, 1, 3)
    chip = spots[3] * y_count + row
    ours = jnp.stack([numbers == 2 * chip + core, numbers == 2 * chip + 1 - core], axis=1)
    gates = jnp.sum(
        jnp.where(ours[None, None, None], routes[..., None], 0.0), axis=-2
    ).reshape(chips, tok_dev, core_count)
    mine, w_pair, scalars, w_logit, spots, gates = lax.optimization_barrier(
        (mine, w_pair, scalars, w_logit, spots, gates)
    )
    theirs = swap_cores(mine)
    beside = tuple(send_y(rows) for rows in w_pair)

    *parts, maps = block_maps(spots, scalars, mine, theirs, w_heads, w_logit, dim, ctx_count, 4)
    beside, maps = lax.optimization_barrier((beside, maps))
    across = send_y(beside[0])
    all_maps = exchange(maps, "ctx")
    slope, base, gate = block_reads(spots, mine, theirs, w_heads, gain_head, parts, dim, PER_STEP)
    across, slope = lax.optimization_barrier((across, slope))
    w_rows = [*w_pair, *beside, across, *[swap_cores(rows) for rows in (*beside, across)]]
    gated = emit(
        spots, all_maps, state_init[0], slope, base, gate, x_count, y_count * core_count
    )
    heads = y_count * core_count
    gated = exchange(gated, ("y", "core")).reshape(heads, x_count * tok_dev, dim)
    partial = project(spots, gated, w_rows, x_count, 1024)

    summed, copies = join(exchange(partial, "x"), tokens, gain_expert, chips)
    far_gate_up, far_down, summed = lax.optimization_barrier((w_gate_up, w_down, summed))
    swapped = (swap_cores(far_gate_up), swap_cores(far_down))
    received = exchange(copies, ("x", "y"))
    outputs = experts_of(spots, gates, received, (w_gate_up, w_down), swapped, x_count)
    expert_out = total_of([exchange(outputs, ("x", "y"))])
    return (summed, expert_out)


PER_STEP = 4


def solution(mesh):
    fine = Mesh(mesh.devices.reshape(mesh.shape["ctx"], 4, 4, 2), ("ctx", "x", "y", "core"))
    exp = ("x", "y", "core")
    rows = ("ctx", "x", "y", "core")
    return jax.shard_map(
        shards,
        mesh=fine,
        in_specs=(
            P(rows, None),
            P(),
            P(None, exp),
            P(None, exp),
            P(exp),
            P(exp),
            P(exp),
            P(exp, None, None),
            P(),
            P(exp, None),
            P(),
            P(rows, None),
            P(rows, None),
            P(exp, None, None),
            P(exp, None, None),
        ),
        out_specs=(P(rows, None), P(rows, None)),
        check_vma=False,
    )
```

```python
import functools
import jax
import jax.numpy as jnp
from jax import lax
from jax.experimental import pallas as pl
from jax.experimental.pallas import tpu as pltpu
from jax.sharding import Mesh, PartitionSpec as P

EPSILON = 1e-06
F32 = jnp.float32
BF16 = jnp.bfloat16
CHUNK = 128
LANES = 128


def mm(a, b):
    return jnp.dot(a.astype(BF16), b.astype(BF16), preferred_element_type=F32)


def pieces(a):
    high = a.astype(BF16)
    rest = a - high.astype(F32)
    middle = rest.astype(BF16)
    low = (rest - middle.astype(F32)).astype(BF16)
    return high, middle, low


def rms_scale(values):
    return lax.rsqrt(jnp.mean(values * values, axis=-1, keepdims=True) + EPSILON)


def chunk_of(n):
    return slice(n * CHUNK, (n + 1) * CHUNK)


def room(mebibytes):
    return pltpu.CompilerParams(vmem_limit_bytes=mebibytes * 1024 * 1024)


def resident():
    return pl.BlockSpec(memory_space=pltpu.VMEM)


def whole(shape):
    return pl.BlockSpec(shape, lambda i: (0,) * len(shape))


def project_rows(core, mine, theirs, w):
    groups, each, width = mine.shape
    ours = jnp.dot(mine.reshape(groups * each, width), w, preferred_element_type=F32)
    others = jnp.dot(theirs.reshape(groups * each, width), w, preferred_element_type=F32)
    even = jnp.where(core == 0, ours, others)
    odd = jnp.where(core == 0, others, ours)
    rows = []
    for group in range(groups):
        at = slice(group * each, (group + 1) * each)
        rows += [even[at], odd[at]]
    return rows


def ours_body(mine_ref, wk_ref, wv_ref, ws_ref, out_ref):
    groups, each, width = mine_ref.shape
    w_all = jnp.concatenate([wk_ref[...], wv_ref[...], ws_ref[...]], axis=1)
    x = mine_ref[...].reshape(groups * each, width)
    out_ref[...] = jnp.dot(x, w_all, preferred_element_type=F32).reshape(out_ref.shape)


def project_ours(mine, w, ws, dim, steps):
    groups, each, width = mine.shape
    total = 2 * dim + ws.shape[1]
    return pl.pallas_call(
        ours_body,
        grid=(steps,),
        in_specs=[
            pl.BlockSpec((groups // steps, each, width), lambda i: (i, 0, 0)),
            pl.BlockSpec((width, dim), lambda i: (0, 1)),
            pl.BlockSpec((width, dim), lambda i: (0, 2)),
            whole(ws.shape),
        ],
        out_specs=pl.BlockSpec((groups // steps, each, total), lambda i: (i, 0, 0)),
        out_shape=jax.ShapeDtypeStruct((groups, each, total), F32),
        name="project_ours",
    )(mine, w, w, ws)


def interleave(core, ours, others, each):
    even = jnp.where(core == 0, ours, others)
    odd = jnp.where(core == 0, others, ours)
    rows = []
    for at in range(0, ours.shape[0], each):
        rows += [even[at:at + each], odd[at:at + each]]
    return rows


def maps_body(
    core_ref, scal_ref, mine_ref, theirs_ref, w_ref, ws_ref,
    key_ref, decay_ref, growth_ref, solved_ref, start_ref, maps_ref,
    mine_buf, theirs_buf, w_buf, ws_buf, sems,
    *, parts,
):
    dim = maps_ref.shape[1]
    groups = theirs_ref.shape[0] // parts
    each, width = theirs_ref.shape[1:]
    w_copies = [
        pltpu.make_async_copy(w_ref.at[:, pl.ds(dim, 2 * dim)], w_buf, sems.at[0]),
        pltpu.make_async_copy(ws_ref, ws_buf, sems.at[1]),
    ]
    x_copies = []
    for part in range(parts):
        at = pl.ds(part * groups, groups)
        x_copies.append(
            [
                pltpu.make_async_copy(mine_ref.at[at], mine_buf.at[at], sems.at[2 + 2 * part]),
                pltpu.make_async_copy(theirs_ref.at[at], theirs_buf.at[at], sems.at[3 + 2 * part]),
            ]
        )
    for copy in w_copies + [copy for both in x_copies for copy in both]:
        copy.start()
    lift = scal_ref[0]
    rate = scal_ref[1]
    bias = scal_ref[2]
    rows = lax.broadcasted_iota(jnp.int32, (CHUNK, CHUNK), 0)
    cols = lax.broadcasted_iota(jnp.int32, (CHUNK, CHUNK), 1)
    differ = jnp.bitwise_xor(rows, cols)
    lower = rows >= cols
    strict = rows > cols
    lower_ones = jnp.where(lower, 1.0, 0.0).astype(BF16)
    eye = jnp.where(rows == cols, 1.0, 0.0).astype(F32)
    for copy in w_copies:
        copy.wait()
    w_all = jnp.concatenate([w_buf[...], ws_buf[...]], axis=1)
    rows_of = []
    for part in range(parts):
        for copy in x_copies[part]:
            copy.wait()
        at = slice(part * groups, (part + 1) * groups)
        x = theirs_buf[at].reshape(groups * each, width)
        others = jnp.dot(x, w_all, preferred_element_type=F32)
        ours = mine_buf[at].reshape(groups * each, -1)
        rows_of += interleave(core_ref[0], ours, others, each)
    projected = jnp.concatenate(rows_of, axis=0)
    logits = projected[:, 2 * dim:]
    every = range(projected.shape[0] // CHUNK)
    key_raw = [projected[chunk_of(n), :dim] for n in every]
    value = [projected[chunk_of(n), dim:2 * dim] for n in every]
    strength = [jax.nn.sigmoid(logits[chunk_of(n), 0:1] + lift) for n in every]
    beta = [jnp.broadcast_to(s, (CHUNK, dim)) for s in strength]
    sums = []
    for n in every:
        moved = logits[chunk_of(n), 1:2] + bias
        softplus = jnp.maximum(moved, 0.0) + jnp.log1p(jnp.exp(-jnp.abs(moved)))
        high, middle, low = pieces(jnp.broadcast_to(-rate * softplus, (CHUNK, CHUNK)))
        sums.append(
            jnp.dot(lower_ones, high, preferred_element_type=F32)
            + jnp.dot(lower_ones, middle, preferred_element_type=F32)
            + jnp.dot(lower_ones, low, preferred_element_type=F32)
        )
    sums_t = [s.T for s in sums]
    key_vec = [
        k * lax.rsqrt(jnp.sum(k * k, axis=-1, keepdims=True) + EPSILON) for k in key_raw
    ]
    key_t = [k.T for k in key_vec]
    growth = [jnp.exp(s) for s in sums]
    fall = [jnp.exp(s[CHUNK - 1:CHUNK, :]) for s in sums]
    decay = [
        jnp.where(lower, jnp.exp(jnp.minimum(s - t, 0.0)), 0.0) for s, t in zip(sums, sums_t)
    ]
    gram = [mm(k, t) for k, t in zip(key_vec, key_t)]
    below = [
        jnp.where(strict, gram[n] * decay[n] * beta[n], 0.0) for n in every
    ]
    inverse = [eye - jnp.where(differ < 2, b, 0.0) for b in below]
    span = 2
    while span < CHUNK:
        ring = (differ >= span) & (differ < 2 * span)
        corner = [jnp.where(ring, b, 0.0) for b in below]
        half = [mm(inverse[n], corner[n]) for n in every]
        inverse = [inverse[n] - mm(half[n], inverse[n]) for n in every]
        span *= 2
    solved = [
        mm(
            inverse[n],
            jnp.concatenate([value[n] * beta[n], key_vec[n] * (beta[n] * growth[n])], axis=1),
        ).astype(BF16)
        for n in every
    ]
    tails = [jnp.exp(t[:, CHUNK - 1:CHUNK] - t) for t in sums_t]
    drive = [mm(key_t[n] * tails[n], solved[n]) for n in every]
    for n in every:
        key_ref[n] = key_t[n].astype(BF16)
        decay_ref[n] = decay[n]
        growth_ref[n] = growth[n]
        solved_ref[n] = solved[n]
    wide_rows = lax.broadcasted_iota(jnp.int32, (dim, 2 * dim), 0)
    wide_cols = lax.broadcasted_iota(jnp.int32, (dim, 2 * dim), 1)
    carried = jnp.where(wide_rows == wide_cols, 1.0, 0.0).astype(F32)
    for n in every:
        start_ref[n] = carried.astype(BF16)
        falls = jnp.concatenate([fall[n], fall[n]], axis=1)
        moved = falls * carried - mm(drive[n][:, dim:], carried)
        carried = jnp.concatenate([moved[:, :dim], moved[:, dim:] + drive[n][:, :dim]], axis=1)
    maps_ref[...] = jnp.broadcast_to(carried.astype(BF16)[None], maps_ref.shape)


def block_maps(core, scalars, mine, theirs, w, ws, dim, copies, parts):
    groups, each, width = theirs.shape
    count = 2 * groups * each // CHUNK
    scalar = pl.BlockSpec(memory_space=pltpu.SMEM)
    anywhere = pl.BlockSpec(memory_space=pl.ANY)
    return pl.pallas_call(
        functools.partial(maps_body, parts=parts),
        in_specs=[scalar, scalar] + [anywhere] * 4,
        out_shape=[
            jax.ShapeDtypeStruct((count, dim, CHUNK), BF16),
            jax.ShapeDtypeStruct((count, CHUNK, CHUNK), F32),
            jax.ShapeDtypeStruct((count, CHUNK, dim), F32),
            jax.ShapeDtypeStruct((count, CHUNK, 2 * dim), BF16),
            jax.ShapeDtypeStruct((count, dim, 2 * dim), BF16),
            jax.ShapeDtypeStruct((copies, dim, 2 * dim), BF16),
        ],
        scratch_shapes=[
            pltpu.VMEM(mine.shape, F32),
            pltpu.VMEM(theirs.shape, BF16),
            pltpu.VMEM((width, 2 * dim), BF16),
            pltpu.VMEM(ws.shape, BF16),
            pltpu.SemaphoreType.DMA((2 + 2 * parts,)),
        ],
        name="block_maps",
    )(core, scalars, mine, theirs, w, ws)


def reads_body(
    core_ref, mine_ref, theirs_ref, wq_ref, wg_ref, gain_ref, key_ref, decay_ref, growth_ref, solved_ref, start_ref,
    slope_ref, base_ref, gate_ref,
    *, per_step,
):
    dim = wq_ref.shape[1]
    w_pair = jnp.concatenate([wq_ref[...], wg_ref[...]], axis=1)
    projected = jnp.concatenate(
        project_rows(core_ref[0], mine_ref[...], theirs_ref[...], w_pair), axis=0
    )
    every = range(per_step)
    query = [projected[chunk_of(n), :dim] for n in every]
    scores = [mm(query[n], key_ref[n]) * decay_ref[n] for n in every]
    mixed = [mm(scores[n], solved_ref[n]) for n in every]
    both = [mm(query[n] * growth_ref[n] - mixed[n][:, dim:], start_ref[n]) for n in every]
    for n in every:
        slope_ref[chunk_of(n), :] = both[n][:, :dim].astype(BF16)
        base_ref[chunk_of(n), :] = both[n][:, dim:] + mixed[n][:, :dim]
    gate = projected[:, dim:]
    gate_ref[...] = gate * jax.nn.sigmoid(gate) * gain_ref[...]


def block_reads(core, mine, theirs, w, gain, parts, dim, per_step):
    key_t, decay, growth, solved, starts = parts
    groups, each, width = mine.shape
    span = 2 * groups * each
    rows = per_step * CHUNK
    x_spec = pl.BlockSpec((rows // (2 * each), each, width), lambda i: (i, 0, 0))

    def stacked(size):
        return pl.BlockSpec((per_step, CHUNK, size), lambda i: (i, 0, 0))

    by_rows = pl.BlockSpec((rows, dim), lambda i: (i, 0))
    return pl.pallas_call(
        functools.partial(reads_body, per_step=per_step),
        grid=(span // rows,),
        in_specs=[
            pl.BlockSpec(memory_space=pltpu.SMEM),
            x_spec,
            x_spec,
            pl.BlockSpec((width, dim), lambda i: (0, 0)),
            pl.BlockSpec((width, dim), lambda i: (0, 3)),
            whole((1, dim)),
            stacked(CHUNK), stacked(CHUNK), stacked(dim), stacked(2 * dim), stacked(2 * dim),
        ],
        out_specs=[by_rows, by_rows, by_rows],
        out_shape=[
            jax.ShapeDtypeStruct((span, dim), BF16),
            jax.ShapeDtypeStruct((span, dim), F32),
            jax.ShapeDtypeStruct((span, dim), F32),
        ],
        name="block_reads",
    )(core, mine, theirs, w, w, gain[None], key_t, decay, growth, solved, starts)


def send_copies(copies):
    for copy in copies:
        copy.start()
    for copy in copies:
        copy.wait()


def norm_body(tokens_ref, gain_ref, out_ref, normed_ref, sems):
    wide = tokens_ref[...].astype(F32)
    normed_ref[...] = (wide * rms_scale(wide) * gain_ref[...]).astype(BF16)
    send_copies(
        [
            pltpu.make_async_copy(normed_ref, out_ref.at[at], sems.at[at])
            for at in range(out_ref.shape[0])
        ]
    )


def norm_copies(tokens, gain, copies):
    return pl.pallas_call(
        norm_body,
        out_specs=pl.BlockSpec(memory_space=pl.ANY),
        out_shape=jax.ShapeDtypeStruct((copies,) + tokens.shape, BF16),
        scratch_shapes=[pltpu.VMEM(tokens.shape, BF16), pltpu.SemaphoreType.DMA((copies,))],
        name="norm_copies",
    )(tokens, gain[None])


def emit_body(place_ref, maps_ref, init_ref, slope_ref, base_ref, gate_ref, out_ref):
    dim = init_ref.shape[0]
    place = place_ref[2]
    rows = lax.broadcasted_iota(jnp.int32, (dim, 2 * dim), 0)
    cols = lax.broadcasted_iota(jnp.int32, (dim, 2 * dim), 1)
    still = jnp.where(rows == cols, 1.0, 0.0).astype(F32)
    steps = [
        jnp.where(block < place, maps_ref[block].astype(F32), still)
        for block in range(maps_ref.shape[0] - 1)
    ]

    def after(later, earlier):
        both = mm(later[:, :dim], earlier)
        return jnp.concatenate([both[:, :dim], both[:, dim:] + later[:, dim:]], axis=1)

    state = mm(steps[0][:, :dim], init_ref[...].T) + steps[0][:, dim:]
    steps = steps[1:]
    while steps:
        odd = len(steps) % 2
        if odd:
            state = mm(steps[0][:, :dim], state) + steps[0][:, dim:]
            steps = steps[1:]
        steps = [after(later, earlier) for earlier, later in zip(steps[0::2], steps[1::2])]
        if steps and not odd:
            state = mm(steps[0][:, :dim], state) + steps[0][:, dim:]
            steps = steps[1:]
    inner, outer, each, _ = out_ref.shape
    for part in range(outer):
        at = slice(part * inner * each, (part + 1) * inner * each)
        head_raw = mm(slope_ref[at, :], state) + base_ref[at, :]
        gated = head_raw * rms_scale(head_raw) * gate_ref[at, :]
        out_ref[:, part] = gated.astype(BF16).reshape(inner, each, dim)


def emit(place, maps, init, slope, base, gate, outer, inner):
    span, dim = slope.shape
    each = span // (outer * inner)
    return pl.pallas_call(
        emit_body,
        in_specs=[pl.BlockSpec(memory_space=pltpu.SMEM)] + [resident()] * 5,
        out_specs=resident(),
        out_shape=jax.ShapeDtypeStruct((inner, outer, each, dim), BF16),
        name="emit",
    )(place, near(maps), init, slope, base, gate)


def project_body(place_ref, gated_ref, *refs):
    *w_refs, out_ref = refs
    core = place_ref[0]
    row = place_ref[1]
    count = gated_ref.shape[0] // 2
    step = 2 * core - 1 + count
    rows = [row, row, row + step, row + step, row + 2, row + count - step + count,
            row + count - step + count, row + 2]
    cores = [core, 1 - core, core, 1 - core, core, 1 - core, core, 1 - core]
    left = [gated_ref[2 * lax.rem(at, count) + side] for at, side in zip(rows, cores)]
    total = jnp.dot(
        jnp.concatenate(left, axis=1),
        jnp.concatenate([ref[...] for ref in w_refs], axis=0),
        preferred_element_type=F32,
    )
    out_ref[...] = total.astype(BF16).reshape(out_ref.shape)


def project(place, gated, weights, parts, tile):
    heads, rows, dim = gated.shape
    width = weights[0].shape[1]
    return pl.pallas_call(
        project_body,
        grid=(width // tile,),
        in_specs=[pl.BlockSpec(memory_space=pltpu.SMEM), resident()] + [
            pl.BlockSpec((rows.shape[0], tile), lambda i: (0, i)) for rows in weights
        ],
        out_specs=pl.BlockSpec((parts, rows // parts, tile), lambda i: (0, 0, i)),
        out_shape=jax.ShapeDtypeStruct((parts, rows // parts, width), BF16),
        name="project",
    )(place, near(gated), *weights)


def join_body(parts_ref, tokens_ref, gain_ref, _, out_ref, copies_ref, normed_ref, sems):
    width = tokens_ref.shape[1]
    total = parts_ref[0].astype(F32)
    for part in range(1, parts_ref.shape[0]):
        total = total + parts_ref[part].astype(F32)
    summed = total.astype(BF16)
    hidden = tokens_ref[...].astype(F32) + summed.astype(F32)
    normed_ref[...] = (hidden * rms_scale(hidden) * gain_ref[...]).astype(BF16)
    copies = [
        pltpu.make_async_copy(normed_ref, copies_ref.at[at, :, pl.ds(0, width)], sems.at[at])
        for at in range(copies_ref.shape[0])
    ]
    for copy in copies:
        copy.start()
    out_ref[...] = summed
    for copy in copies:
        copy.wait()


def join(parts, tokens, gain, payload):
    anywhere = pl.BlockSpec(memory_space=pl.ANY)
    return pl.pallas_call(
        join_body,
        in_specs=[resident(), resident(), resident(), anywhere],
        out_specs=[resident(), anywhere],
        out_shape=[
            jax.ShapeDtypeStruct(tokens.shape, BF16),
            jax.ShapeDtypeStruct(payload.shape, BF16),
        ],
        input_output_aliases={3: 1},
        scratch_shapes=[
            pltpu.VMEM(tokens.shape, BF16),
            pltpu.SemaphoreType.DMA((payload.shape[0],)),
        ],
        name="join",
    )(near(parts), near(tokens), gain[None], payload)


def experts_body(x_ref, up_a_ref, down_a_ref, up_b_ref, down_b_ref, out_ref, *, tiles):
    groups, each, width = out_ref.shape
    count = groups * each
    hidden_units = down_a_ref.shape[1]
    tile = hidden_units // tiles
    x = x_ref[:, :, :width].reshape(count, width)
    extra = x_ref[:, :, width:].astype(F32).reshape(count, -1)
    total = None
    for which, (up_ref, down_ref) in enumerate(((up_a_ref, down_a_ref), (up_b_ref, down_b_ref))):
        pre = jnp.dot(x, up_ref[0], preferred_element_type=F32)
        gate = pre[:, :hidden_units]
        activated = (gate * jax.nn.sigmoid(gate) * pre[:, hidden_units:]).astype(BF16)
        rows = jnp.dot(activated, down_ref[0], preferred_element_type=F32)
        first = 3 * which
        weight = (
            extra[:, first:first + 1]
            + extra[:, first + 1:first + 2]
            + extra[:, first + 2:first + 3]
        )
        scaled = rows.astype(BF16).astype(F32) * weight
        total = scaled if total is None else total + scaled
    out_ref[...] = total.astype(BF16).reshape(out_ref.shape)


def experts_of(x, first, second, tiles):
    groups, each, _ = x.shape
    width = first[1].shape[2]
    return pl.pallas_call(
        functools.partial(experts_body, tiles=tiles),
        in_specs=[resident()] * 5,
        out_shape=jax.ShapeDtypeStruct((groups, each, width), BF16),
        compiler_params=room(28),
        name="experts",
    )(near(x), *[near(part) for part in first + second])


def total_body(*refs):
    *parts_refs, out_ref = refs
    each = parts_refs[0].shape[1]
    for half, parts_ref in enumerate(parts_refs):
        total = parts_ref[0].astype(F32)
        for part in range(1, parts_ref.shape[0]):
            total = total + parts_ref[part].astype(F32)
        out_ref[half * each:(half + 1) * each, :] = total.astype(BF16)


def total_of(halves):
    copies, each, width = halves[0].shape
    return pl.pallas_call(
        total_body,
        in_specs=[resident()] * len(halves),
        out_shape=jax.ShapeDtypeStruct((len(halves) * each, width), BF16),
        name="total",
    )(*[near(parts) for parts in halves])


def send_y(value):
    count = lax.axis_size("y")
    up = [(2 * at, 2 * ((at + 1) % count)) for at in range(count)]
    down = [(2 * at + 1, 2 * ((at + count - 1) % count) + 1) for at in range(count)]
    return lax.ppermute(value, ("y", "core"), up + down)


def near(value):
    return pltpu.with_memory_space_constraint(value, pltpu.VMEM)


def swap_cores(value):
    return lax.ppermute(value, "core", [(0, 1), (1, 0)])


def exchange(value, axes):
    return lax.all_to_all(value, axes, split_axis=0, concat_axis=0, tiled=True)


def shards(
    tokens,
    gain_in,
    w_heads,
    w_scalar,
    strength_bias,
    decay_rate,
    decay_bias,
    state_init,
    gain_head,
    w_output,
    gain_expert,
    expert_ids,
    gate_weights,
    w_gate_up,
    w_down,
):
    tok_dev, width = tokens.shape
    dim = state_init.shape[-1]
    x_count, y_count, core_count = (lax.axis_size(axis) for axis in ("x", "y", "core"))
    ctx_count = lax.axis_size("ctx")
    chips = x_count * y_count
    expert_total = chips * core_count
    core = lax.axis_index("core").astype(jnp.int32)
    place = lax.axis_index("ctx").astype(jnp.int32)

    copies = norm_copies(tokens, gain_in, chips)
    mine = exchange(copies, ("x", "y"))
    w_pair = (w_output, swap_cores(w_output))
    scalars = jnp.concatenate([strength_bias, decay_rate, decay_bias])
    w_logit = jnp.pad(w_scalar, ((0, 0), (0, LANES - w_scalar.shape[1])))
    spots = jnp.stack([core, lax.axis_index("y").astype(jnp.int32), place])
    numbers = jnp.arange(expert_total, dtype=jnp.int32)
    named = expert_ids[:, :, None] == numbers[None, None, :]
    routes = jnp.sum(jnp.where(named, gate_weights[:, :, None], 0.0), axis=1)
    routes = routes.reshape(tok_dev, chips, core_count).transpose(1, 0, 2)
    routes = jnp.where(core == 0, routes, routes[:, :, ::-1])
    routes = jnp.stack(pieces(routes), axis=-1).reshape(chips, tok_dev, -1)
    payload = jnp.pad(routes, ((0, 0), (0, 0), (width, LANES - routes.shape[-1])))

    mine, w_pair, scalars, w_logit, spots, payload = lax.optimization_barrier(
        (mine, w_pair, scalars, w_logit, spots, payload)
    )
    theirs = swap_cores(mine)
    beside = tuple(send_y(rows) for rows in w_pair)

    ours = project_ours(mine, w_heads, w_logit, dim, 2)
    *parts, maps = block_maps(spots, scalars, ours, theirs, w_heads, w_logit, dim, ctx_count, 4)
    beside, maps = lax.optimization_barrier((beside, maps))
    across = send_y(beside[0])
    all_maps = exchange(maps, "ctx")
    slope, base, gate = block_reads(spots, mine, theirs, w_heads, gain_head, parts, dim, PER_STEP)
    across, slope = lax.optimization_barrier((across, slope))
    w_rows = [*w_pair, *beside, across, *[swap_cores(rows) for rows in (*beside, across)]]
    gated = emit(
        spots, all_maps, state_init[0], slope, base, gate, x_count, y_count * core_count
    )
    heads = y_count * core_count
    gated = exchange(gated, ("y", "core")).reshape(heads, x_count * tok_dev, dim)
    partial = project(spots, gated, w_rows, x_count, 1024)

    summed, copies = join(exchange(partial, "x"), tokens, gain_expert, payload)
    far_gate_up, far_down, summed = lax.optimization_barrier((w_gate_up, w_down, summed))
    swapped = (swap_cores(far_gate_up), swap_cores(far_down))
    received = exchange(copies, ("x", "y"))
    outputs = experts_of(received, (w_gate_up, w_down), swapped, 2)
    expert_out = total_of([exchange(outputs, ("x", "y"))])
    return (summed, expert_out)


PER_STEP = 4


def solution(mesh):
    fine = Mesh(mesh.devices.reshape(mesh.shape["ctx"], 4, 4, 2), ("ctx", "x", "y", "core"))
    exp = ("x", "y", "core")
    rows = ("ctx", "x", "y", "core")
    return jax.shard_map(
        shards,
        mesh=fine,
        in_specs=(
            P(rows, None),
            P(),
            P(None, exp),
            P(None, exp),
            P(exp),
            P(exp),
            P(exp),
            P(exp, None, None),
            P(),
            P(exp, None),
            P(),
            P(rows, None),
            P(rows, None),
            P(exp, None, None),
            P(exp, None, None),
        ),
        out_specs=(P(rows, None), P(rows, None)),
        check_vma=False,
    )
```

```python
import functools
import jax
import jax.numpy as jnp
from jax import lax
from jax.experimental import pallas as pl
from jax.experimental.pallas import tpu as pltpu
from jax.sharding import Mesh, PartitionSpec as P

EPSILON = 1e-06
F32 = jnp.float32
BF16 = jnp.bfloat16
CHUNK = 128
LANES = 128


def mm(a, b):
    return jnp.dot(a.astype(BF16), b.astype(BF16), preferred_element_type=F32)


def pieces(a):
    high = a.astype(BF16)
    rest = a - high.astype(F32)
    middle = rest.astype(BF16)
    low = (rest - middle.astype(F32)).astype(BF16)
    return high, middle, low


def rms_scale(values):
    return lax.rsqrt(jnp.mean(values * values, axis=-1, keepdims=True) + EPSILON)


def chunk_of(n):
    return slice(n * CHUNK, (n + 1) * CHUNK)


def room(mebibytes):
    return pltpu.CompilerParams(vmem_limit_bytes=mebibytes * 1024 * 1024)


def resident():
    return pl.BlockSpec(memory_space=pltpu.VMEM)


def whole(shape):
    return pl.BlockSpec(shape, lambda i: (0,) * len(shape))


def project_rows(core, mine, theirs, w):
    groups, each, width = mine.shape
    ours = jnp.dot(mine.reshape(groups * each, width), w, preferred_element_type=F32)
    others = jnp.dot(theirs.reshape(groups * each, width), w, preferred_element_type=F32)
    even = jnp.where(core == 0, ours, others)
    odd = jnp.where(core == 0, others, ours)
    rows = []
    for group in range(groups):
        at = slice(group * each, (group + 1) * each)
        rows += [even[at], odd[at]]
    return rows


def maps_body(
    core_ref, scal_ref, mine_ref, theirs_ref, w_ref, ws_ref,
    key_ref, decay_ref, growth_ref, solved_ref, start_ref, maps_ref,
    mine_buf, theirs_buf, w_buf, ws_buf, sems,
    *, parts,
):
    dim = maps_ref.shape[1]
    groups = mine_ref.shape[0] // parts
    w_copies = [
        pltpu.make_async_copy(w_ref.at[:, pl.ds(dim, 2 * dim)], w_buf, sems.at[0]),
        pltpu.make_async_copy(ws_ref, ws_buf, sems.at[1]),
    ]
    x_copies = []
    for part in range(parts):
        at = pl.ds(part * groups, groups)
        x_copies.append(
            [
                pltpu.make_async_copy(mine_ref.at[at], mine_buf.at[at], sems.at[2 + 2 * part]),
                pltpu.make_async_copy(theirs_ref.at[at], theirs_buf.at[at], sems.at[3 + 2 * part]),
            ]
        )
    for copy in w_copies + [copy for both in x_copies for copy in both]:
        copy.start()
    lift = scal_ref[0]
    rate = scal_ref[1]
    bias = scal_ref[2]
    rows = lax.broadcasted_iota(jnp.int32, (CHUNK, CHUNK), 0)
    cols = lax.broadcasted_iota(jnp.int32, (CHUNK, CHUNK), 1)
    differ = jnp.bitwise_xor(rows, cols)
    lower = rows >= cols
    strict = rows > cols
    lower_ones = jnp.where(lower, 1.0, 0.0).astype(BF16)
    eye = jnp.where(rows == cols, 1.0, 0.0).astype(F32)
    for copy in w_copies:
        copy.wait()
    w_all = jnp.concatenate([w_buf[...], ws_buf[...]], axis=1)
    rows_of = []
    for part in range(parts):
        for copy in x_copies[part]:
            copy.wait()
        at = slice(part * groups, (part + 1) * groups)
        rows_of += project_rows(core_ref[0], mine_buf[at], theirs_buf[at], w_all)
    projected = jnp.concatenate(rows_of, axis=0)
    logits = projected[:, 2 * dim:]
    every = range(projected.shape[0] // CHUNK)
    key_raw = [projected[chunk_of(n), :dim] for n in every]
    value = [projected[chunk_of(n), dim:2 * dim] for n in every]
    strength = [jax.nn.sigmoid(logits[chunk_of(n), 0:1] + lift) for n in every]
    beta = [jnp.broadcast_to(s, (CHUNK, dim)) for s in strength]
    sums = []
    for n in every:
        moved = logits[chunk_of(n), 1:2] + bias
        softplus = jnp.maximum(moved, 0.0) + jnp.log1p(jnp.exp(-jnp.abs(moved)))
        high, middle, low = pieces(jnp.broadcast_to(-rate * softplus, (CHUNK, CHUNK)))
        sums.append(
            jnp.dot(lower_ones, high, preferred_element_type=F32)
            + jnp.dot(lower_ones, middle, preferred_element_type=F32)
            + jnp.dot(lower_ones, low, preferred_element_type=F32)
        )
    sums_t = [s.T for s in sums]
    key_vec = [
        k * lax.rsqrt(jnp.sum(k * k, axis=-1, keepdims=True) + EPSILON) for k in key_raw
    ]
    key_t = [k.T for k in key_vec]
    growth = [jnp.exp(s) for s in sums]
    fall = [jnp.exp(s[CHUNK - 1:CHUNK, :]) for s in sums]
    decay = [
        jnp.where(lower, jnp.exp(jnp.minimum(s - t, 0.0)), 0.0) for s, t in zip(sums, sums_t)
    ]
    gram = [mm(k, t) for k, t in zip(key_vec, key_t)]
    below = [
        jnp.where(strict, gram[n] * decay[n] * beta[n], 0.0) for n in every
    ]
    inverse = [eye - jnp.where(differ < 2, b, 0.0) for b in below]
    width = 2
    while width < CHUNK:
        ring = (differ >= width) & (differ < 2 * width)
        corner = [jnp.where(ring, b, 0.0) for b in below]
        half = [mm(inverse[n], corner[n]) for n in every]
        inverse = [inverse[n] - mm(half[n], inverse[n]) for n in every]
        width *= 2
    solved = [
        mm(
            inverse[n],
            jnp.concatenate([value[n] * beta[n], key_vec[n] * (beta[n] * growth[n])], axis=1),
        ).astype(BF16)
        for n in every
    ]
    tails = [jnp.exp(t[:, CHUNK - 1:CHUNK] - t) for t in sums_t]
    drive = [mm(key_t[n] * tails[n], solved[n]) for n in every]
    for n in every:
        key_ref[n] = key_t[n].astype(BF16)
        decay_ref[n] = decay[n]
        growth_ref[n] = growth[n]
        solved_ref[n] = solved[n]
    wide_rows = lax.broadcasted_iota(jnp.int32, (dim, 2 * dim), 0)
    wide_cols = lax.broadcasted_iota(jnp.int32, (dim, 2 * dim), 1)
    carried = jnp.where(wide_rows == wide_cols, 1.0, 0.0).astype(F32)
    for n in every:
        start_ref[n] = carried.astype(BF16)
        falls = jnp.concatenate([fall[n], fall[n]], axis=1)
        moved = falls * carried - mm(drive[n][:, dim:], carried)
        carried = jnp.concatenate([moved[:, :dim], moved[:, dim:] + drive[n][:, :dim]], axis=1)
    maps_ref[...] = jnp.broadcast_to(carried.astype(BF16)[None], maps_ref.shape)


def block_maps(core, scalars, mine, theirs, w, ws, dim, copies, parts):
    groups, each, width = mine.shape
    count = 2 * groups * each // CHUNK
    scalar = pl.BlockSpec(memory_space=pltpu.SMEM)
    anywhere = pl.BlockSpec(memory_space=pl.ANY)
    return pl.pallas_call(
        functools.partial(maps_body, parts=parts),
        in_specs=[scalar, scalar] + [anywhere] * 4,
        out_shape=[
            jax.ShapeDtypeStruct((count, dim, CHUNK), BF16),
            jax.ShapeDtypeStruct((count, CHUNK, CHUNK), F32),
            jax.ShapeDtypeStruct((count, CHUNK, dim), F32),
            jax.ShapeDtypeStruct((count, CHUNK, 2 * dim), BF16),
            jax.ShapeDtypeStruct((count, dim, 2 * dim), BF16),
            jax.ShapeDtypeStruct((copies, dim, 2 * dim), BF16),
        ],
        scratch_shapes=[
            pltpu.VMEM(mine.shape, BF16),
            pltpu.VMEM(theirs.shape, BF16),
            pltpu.VMEM((width, 2 * dim), BF16),
            pltpu.VMEM(ws.shape, BF16),
            pltpu.SemaphoreType.DMA((2 + 2 * parts,)),
        ],
        name="block_maps",
    )(core, scalars, mine, theirs, w, ws)


def reads_body(
    core_ref, mine_ref, theirs_ref, wq_ref, wg_ref, gain_ref, key_ref, decay_ref, growth_ref, solved_ref, start_ref,
    slope_ref, base_ref, gate_ref,
    *, per_step,
):
    dim = wq_ref.shape[1]
    w_pair = jnp.concatenate([wq_ref[...], wg_ref[...]], axis=1)
    projected = jnp.concatenate(
        project_rows(core_ref[0], mine_ref[...], theirs_ref[...], w_pair), axis=0
    )
    every = range(per_step)
    query = [projected[chunk_of(n), :dim] for n in every]
    scores = [mm(query[n], key_ref[n]) * decay_ref[n] for n in every]
    mixed = [mm(scores[n], solved_ref[n]) for n in every]
    both = [mm(query[n] * growth_ref[n] - mixed[n][:, dim:], start_ref[n]) for n in every]
    for n in every:
        slope_ref[chunk_of(n), :] = both[n][:, :dim].astype(BF16)
        base_ref[chunk_of(n), :] = both[n][:, dim:] + mixed[n][:, :dim]
    gate = projected[:, dim:]
    gate_ref[...] = gate * jax.nn.sigmoid(gate) * gain_ref[...]


def block_reads(core, mine, theirs, w, gain, parts, dim, per_step):
    key_t, decay, growth, solved, starts = parts
    groups, each, width = mine.shape
    span = 2 * groups * each
    rows = per_step * CHUNK
    x_spec = pl.BlockSpec((rows // (2 * each), each, width), lambda i: (i, 0, 0))

    def stacked(size):
        return pl.BlockSpec((per_step, CHUNK, size), lambda i: (i, 0, 0))

    by_rows = pl.BlockSpec((rows, dim), lambda i: (i, 0))
    return pl.pallas_call(
        functools.partial(reads_body, per_step=per_step),
        grid=(span // rows,),
        in_specs=[
            pl.BlockSpec(memory_space=pltpu.SMEM),
            x_spec,
            x_spec,
            pl.BlockSpec((width, dim), lambda i: (0, 0)),
            pl.BlockSpec((width, dim), lambda i: (0, 3)),
            whole((1, dim)),
            stacked(CHUNK), stacked(CHUNK), stacked(dim), stacked(2 * dim), stacked(2 * dim),
        ],
        out_specs=[by_rows, by_rows, by_rows],
        out_shape=[
            jax.ShapeDtypeStruct((span, dim), BF16),
            jax.ShapeDtypeStruct((span, dim), F32),
            jax.ShapeDtypeStruct((span, dim), F32),
        ],
        name="block_reads",
    )(core, mine, theirs, w, w, gain[None], key_t, decay, growth, solved, starts)


def send_copies(copies):
    for copy in copies:
        copy.start()
    for copy in copies:
        copy.wait()


def norm_body(tokens_ref, gain_ref, out_ref, normed_ref, sems):
    wide = tokens_ref[...].astype(F32)
    normed_ref[...] = (wide * rms_scale(wide) * gain_ref[...]).astype(BF16)
    send_copies(
        [
            pltpu.make_async_copy(normed_ref, out_ref.at[at], sems.at[at])
            for at in range(out_ref.shape[0])
        ]
    )


def norm_copies(tokens, gain, copies):
    return pl.pallas_call(
        norm_body,
        out_specs=pl.BlockSpec(memory_space=pl.ANY),
        out_shape=jax.ShapeDtypeStruct((copies,) + tokens.shape, BF16),
        scratch_shapes=[pltpu.VMEM(tokens.shape, BF16), pltpu.SemaphoreType.DMA((copies,))],
        name="norm_copies",
    )(tokens, gain[None])


def emit_body(place_ref, maps_ref, init_ref, slope_ref, base_ref, gate_ref, out_ref):
    dim = init_ref.shape[0]
    place = place_ref[2]
    rows = lax.broadcasted_iota(jnp.int32, (dim, 2 * dim), 0)
    cols = lax.broadcasted_iota(jnp.int32, (dim, 2 * dim), 1)
    still = jnp.where(rows == cols, 1.0, 0.0).astype(F32)
    steps = [
        jnp.where(block < place, maps_ref[block].astype(F32), still)
        for block in range(maps_ref.shape[0] - 1)
    ]

    def after(later, earlier):
        both = mm(later[:, :dim], earlier)
        return jnp.concatenate([both[:, :dim], both[:, dim:] + later[:, dim:]], axis=1)

    state = mm(steps[0][:, :dim], init_ref[...].T) + steps[0][:, dim:]
    steps = steps[1:]
    while steps:
        odd = len(steps) % 2
        if odd:
            state = mm(steps[0][:, :dim], state) + steps[0][:, dim:]
            steps = steps[1:]
        steps = [after(later, earlier) for earlier, later in zip(steps[0::2], steps[1::2])]
        if steps and not odd:
            state = mm(steps[0][:, :dim], state) + steps[0][:, dim:]
            steps = steps[1:]
    inner, outer, each, _ = out_ref.shape
    for part in range(outer):
        at = slice(part * inner * each, (part + 1) * inner * each)
        head_raw = mm(slope_ref[at, :], state) + base_ref[at, :]
        gated = head_raw * rms_scale(head_raw) * gate_ref[at, :]
        out_ref[:, part] = gated.astype(BF16).reshape(inner, each, dim)


def emit(place, maps, init, slope, base, gate, outer, inner):
    span, dim = slope.shape
    each = span // (outer * inner)
    return pl.pallas_call(
        emit_body,
        in_specs=[pl.BlockSpec(memory_space=pltpu.SMEM)] + [resident()] * 5,
        out_specs=resident(),
        out_shape=jax.ShapeDtypeStruct((inner, outer, each, dim), BF16),
        name="emit",
    )(place, near(maps), init, slope, base, gate)


def project_body(place_ref, gated_ref, *refs):
    *w_refs, out_ref = refs
    core = place_ref[0]
    row = place_ref[1]
    count = gated_ref.shape[0] // 2
    step = 2 * core - 1 + count
    rows = [row, row, row + step, row + step, row + 2, row + count - step + count,
            row + count - step + count, row + 2]
    cores = [core, 1 - core, core, 1 - core, core, 1 - core, core, 1 - core]
    left = [gated_ref[2 * lax.rem(at, count) + side] for at, side in zip(rows, cores)]
    total = jnp.dot(
        jnp.concatenate(left, axis=1),
        jnp.concatenate([ref[...] for ref in w_refs], axis=0),
        preferred_element_type=F32,
    )
    out_ref[...] = total.astype(BF16).reshape(out_ref.shape)


def project(place, gated, weights, parts, tile):
    heads, rows, dim = gated.shape
    width = weights[0].shape[1]
    return pl.pallas_call(
        project_body,
        grid=(width // tile,),
        in_specs=[pl.BlockSpec(memory_space=pltpu.SMEM), resident()] + [
            pl.BlockSpec((rows.shape[0], tile), lambda i: (0, i)) for rows in weights
        ],
        out_specs=pl.BlockSpec((parts, rows // parts, tile), lambda i: (0, 0, i)),
        out_shape=jax.ShapeDtypeStruct((parts, rows // parts, width), BF16),
        name="project",
    )(place, near(gated), *weights)


def join_body(parts_ref, tokens_ref, gain_ref, _, out_ref, copies_ref, normed_ref, sems):
    width = tokens_ref.shape[1]
    total = parts_ref[0].astype(F32)
    for part in range(1, parts_ref.shape[0]):
        total = total + parts_ref[part].astype(F32)
    summed = total.astype(BF16)
    hidden = tokens_ref[...].astype(F32) + summed.astype(F32)
    normed_ref[...] = (hidden * rms_scale(hidden) * gain_ref[...]).astype(BF16)
    copies = [
        pltpu.make_async_copy(normed_ref, copies_ref.at[at, :, pl.ds(0, width)], sems.at[at])
        for at in range(copies_ref.shape[0])
    ]
    for copy in copies:
        copy.start()
    out_ref[...] = summed
    for copy in copies:
        copy.wait()


def join(parts, tokens, gain, payload):
    anywhere = pl.BlockSpec(memory_space=pl.ANY)
    return pl.pallas_call(
        join_body,
        in_specs=[resident(), resident(), resident(), anywhere],
        out_specs=[resident(), anywhere],
        out_shape=[
            jax.ShapeDtypeStruct(tokens.shape, BF16),
            jax.ShapeDtypeStruct(payload.shape, BF16),
        ],
        input_output_aliases={3: 1},
        scratch_shapes=[
            pltpu.VMEM(tokens.shape, BF16),
            pltpu.SemaphoreType.DMA((payload.shape[0],)),
        ],
        name="join",
    )(near(parts), near(tokens), gain[None], payload)


def experts_body(x_ref, up_a_ref, down_a_ref, up_b_ref, down_b_ref, out_ref, *, tiles):
    groups, each, width = out_ref.shape
    count = groups * each
    hidden_units = down_a_ref.shape[1]
    tile = hidden_units // tiles
    x = x_ref[:, :, :width].reshape(count, width)
    extra = x_ref[:, :, width:].astype(F32).reshape(count, -1)
    total = None
    for which, (up_ref, down_ref) in enumerate(((up_a_ref, down_a_ref), (up_b_ref, down_b_ref))):
        pre = jnp.dot(x, up_ref[0], preferred_element_type=F32)
        gate = pre[:, :hidden_units]
        activated = (gate * jax.nn.sigmoid(gate) * pre[:, hidden_units:]).astype(BF16)
        rows = jnp.dot(activated, down_ref[0], preferred_element_type=F32)
        first = 3 * which
        weight = (
            extra[:, first:first + 1]
            + extra[:, first + 1:first + 2]
            + extra[:, first + 2:first + 3]
        )
        scaled = rows.astype(BF16).astype(F32) * weight
        total = scaled if total is None else total + scaled
    out_ref[...] = total.astype(BF16).reshape(out_ref.shape)


def experts_of(x, first, second, tiles):
    groups, each, _ = x.shape
    width = first[1].shape[2]
    return pl.pallas_call(
        functools.partial(experts_body, tiles=tiles),
        in_specs=[resident()] * 5,
        out_shape=jax.ShapeDtypeStruct((groups, each, width), BF16),
        compiler_params=room(28),
        name="experts",
    )(near(x), *[near(part) for part in first + second])


def total_body(*refs):
    *parts_refs, out_ref = refs
    each = parts_refs[0].shape[1]
    for half, parts_ref in enumerate(parts_refs):
        total = parts_ref[0].astype(F32)
        for part in range(1, parts_ref.shape[0]):
            total = total + parts_ref[part].astype(F32)
        out_ref[half * each:(half + 1) * each, :] = total.astype(BF16)


def total_of(halves):
    copies, each, width = halves[0].shape
    return pl.pallas_call(
        total_body,
        in_specs=[resident()] * len(halves),
        out_shape=jax.ShapeDtypeStruct((len(halves) * each, width), BF16),
        name="total",
    )(*[near(parts) for parts in halves])


def send_y(value):
    count = lax.axis_size("y")
    up = [(2 * at, 2 * ((at + 1) % count)) for at in range(count)]
    down = [(2 * at + 1, 2 * ((at + count - 1) % count) + 1) for at in range(count)]
    return lax.ppermute(value, ("y", "core"), up + down)


def near(value):
    return pltpu.with_memory_space_constraint(value, pltpu.VMEM)


def swap_cores(value):
    return lax.ppermute(value, "core", [(0, 1), (1, 0)])


def exchange(value, axes):
    return lax.all_to_all(value, axes, split_axis=0, concat_axis=0, tiled=True)


def shards(
    tokens,
    gain_in,
    w_heads,
    w_scalar,
    strength_bias,
    decay_rate,
    decay_bias,
    state_init,
    gain_head,
    w_output,
    gain_expert,
    expert_ids,
    gate_weights,
    w_gate_up,
    w_down,
):
    tok_dev, width = tokens.shape
    dim = state_init.shape[-1]
    x_count, y_count, core_count = (lax.axis_size(axis) for axis in ("x", "y", "core"))
    ctx_count = lax.axis_size("ctx")
    chips = x_count * y_count
    expert_total = chips * core_count
    core = lax.axis_index("core").astype(jnp.int32)
    place = lax.axis_index("ctx").astype(jnp.int32)

    copies = norm_copies(tokens, gain_in, chips)
    mine = exchange(copies, ("x", "y"))
    w_pair = (w_output, swap_cores(w_output))
    scalars = jnp.concatenate([strength_bias, decay_rate, decay_bias])
    w_logit = jnp.pad(w_scalar, ((0, 0), (0, LANES - w_scalar.shape[1])))
    spots = jnp.stack([core, lax.axis_index("y").astype(jnp.int32), place])
    numbers = jnp.arange(expert_total, dtype=jnp.int32)
    named = expert_ids[:, :, None] == numbers[None, None, :]
    routes = jnp.sum(jnp.where(named, gate_weights[:, :, None], 0.0), axis=1)
    routes = routes.reshape(tok_dev, chips, core_count).transpose(1, 0, 2)
    routes = jnp.where(core == 0, routes, routes[:, :, ::-1])
    routes = jnp.stack(pieces(routes), axis=-1).reshape(chips, tok_dev, -1)
    payload = jnp.pad(routes, ((0, 0), (0, 0), (width, LANES - routes.shape[-1])))

    mine, w_pair, scalars, w_logit, spots, payload = lax.optimization_barrier(
        (mine, w_pair, scalars, w_logit, spots, payload)
    )
    theirs = swap_cores(mine)
    beside = tuple(send_y(rows) for rows in w_pair)

    *parts, maps = block_maps(spots, scalars, mine, theirs, w_heads, w_logit, dim, ctx_count, 4)
    first, maps = lax.optimization_barrier((beside[0], maps))
    across = send_y(first)
    all_maps = exchange(maps, "ctx")
    slope, base, gate = block_reads(spots, mine, theirs, w_heads, gain_head, parts, dim, PER_STEP)
    across, second, slope = lax.optimization_barrier((across, beside[1], slope))
    beside = (first, second)
    w_rows = [*w_pair, *beside, across, *[swap_cores(rows) for rows in (*beside, across)]]
    gated = emit(
        spots, all_maps, state_init[0], slope, base, gate, x_count, y_count * core_count
    )
    heads = y_count * core_count
    gated = exchange(gated, ("y", "core")).reshape(heads, x_count * tok_dev, dim)
    partial = project(spots, gated, w_rows, x_count, 1024)

    summed, copies = join(exchange(partial, "x"), tokens, gain_expert, payload)
    far_gate_up, far_down, summed = lax.optimization_barrier((w_gate_up, w_down, summed))
    swapped = (swap_cores(far_gate_up), swap_cores(far_down))
    received = exchange(copies, ("x", "y"))
    outputs = experts_of(received, (w_gate_up, w_down), swapped, 2)
    expert_out = total_of([exchange(outputs, ("x", "y"))])
    return (summed, expert_out)


PER_STEP = 4


def solution(mesh):
    fine = Mesh(mesh.devices.reshape(mesh.shape["ctx"], 4, 4, 2), ("ctx", "x", "y", "core"))
    exp = ("x", "y", "core")
    rows = ("ctx", "x", "y", "core")
    return jax.shard_map(
        shards,
        mesh=fine,
        in_specs=(
            P(rows, None),
            P(),
            P(None, exp),
            P(None, exp),
            P(exp),
            P(exp),
            P(exp),
            P(exp, None, None),
            P(),
            P(exp, None),
            P(),
            P(rows, None),
            P(rows, None),
            P(exp, None, None),
            P(exp, None, None),
        ),
        out_specs=(P(rows, None), P(rows, None)),
        check_vma=False,
    )
```
